32 devices in a mesh: prompt: 4 (over z), tensor: 8 (over y, x, core).
Axes of the slice: x: 2, y: 2, z: 4, core: 2. Of those that a mesh axis runs over, the one named last changes fastest.
Arguments:
- embeds: bfloat16 [4, 64, 8192], P('prompt', None, 'tensor'), may hold values from -400 to 400
- norm_gain: bfloat16 [8192], replicated, may hold values from 0.5 to 1.5
- query_weight: bfloat16 [8192, 8192], P('prompt', 'tensor'), may hold values from -1 to 1
- key_weight: bfloat16 [8192, 1024], P('prompt', 'tensor'), may hold values from -6 to 6
- value_weight: bfloat16 [8192, 1024], P('prompt', 'tensor'), may hold values from -0.0625 to 0.0625
- out_weight: bfloat16 [8192, 8192], P('tensor', 'prompt'), may hold values from -0.0625 to 0.0625
- out_grad: bfloat16 [4, 64, 8192], P('prompt', None, 'tensor'), may hold values from -6 to 6
- suffix_pos: int32 [4, 20], P('prompt'), may hold values from 0 to 63
- vocab_table: bfloat16 [65536, 8192], P(('prompt', 'tensor')), may hold values from -0.0625 to 0.0625
- banned: int32 [65536], P(('prompt', 'tensor')), may hold values 0 or 1
Outputs:
- token_scores: float32 [4, 20, 65536], P(None, None, ('prompt', 'tensor'))
The draws below stay inside these ranges and needn't reach their ends.
All inputs are finite; a program needn't handle non-finite values. No bound on the sum of `banned` on one device may be relied on, other than what follows from the above.
Results may differ from the reference program's by a relative error of at most 0.01.
The reference program's roundings to bfloat16 on the way (of `normed`, `probs_low`, `context_grad`, `logit_grad`, `query_grad`, `key_grad`, `value_grad` and `suffix_grad`) count: a program that leaves them out, or rounds other values in their place, can miss the bound.
Values may be sent and summed in bfloat16 or wider, within the bound.
A program may use at most 192 MiB of HBM per device.

```python
import math
import jax
import jax.numpy as jnp
from jax import lax

D = 8192
H = 64
KVH = 8
HD = 128
V = 65536
SEQ = 64
NSUF = 20
PROMPTS = 4


def shared_query(key):
    subkey = jax.random.fold_in(key, 11)
    return jnp.clip(jax.random.normal(subkey, (D, H * HD), jnp.float32), -4.0, 4.0) / math.sqrt(D)


def draw_query_weight(key, part):
    return shared_query(key).astype(jnp.bfloat16)


def draw_key_weight(key, part):
    subkey = jax.random.fold_in(key, 13)
    return (jnp.clip(jax.random.normal(subkey, (D, KVH * HD), jnp.float32), -4.0, 4.0) / math.sqrt(D)).astype(jnp.bfloat16)


def draw_embeds(key, part):
    shape = (PROMPTS, SEQ, D)
    row_key = jax.random.fold_in(key, 21)
    column_key = jax.random.fold_in(key, 22)
    noise_key = jax.random.fold_in(key, 23)
    row_scale = jnp.exp(jax.random.uniform(row_key, (PROMPTS, SEQ, 1), jnp.float32, 0.0, math.log(10.0)))
    column_scale = jnp.exp(jax.random.uniform(column_key, (1, 1, D), jnp.float32, 0.0, math.log(10.0)))
    noise = jnp.clip(jax.random.normal(noise_key, shape, jnp.float32), -4.0, 4.0)
    return (noise * row_scale * column_scale).astype(jnp.bfloat16)


def touch_ends(values, rng, smallest, high):
    dims = values.shape
    index_at = [jax.random.randint(jax.random.fold_in(rng, axis), (), 0, dims[axis]) for axis in range(len(dims))]
    values = values.at[tuple(index_at)].set(smallest)
    longest = dims.index(max(dims))
    index_at[longest] = (index_at[longest] + 1) % dims[longest]
    return values.at[tuple(index_at)].set(high)


def block_scale(stream_key, dims, cuts, smallest, high):
    level = 1.0
    for dim, blocks in cuts:
        draws = jax.random.uniform(jax.random.fold_in(jax.random.fold_in(stream_key, 6), dim), (blocks,), jnp.float32, smallest / len(cuts), high / len(cuts))
        level = level * jnp.repeat(jnp.exp(draws), dims[dim] // blocks).reshape((-1,) + (1,) * (len(dims) - 1 - dim))
    return level


def bell_draw(rng, shape, width, limit, shards=(), dtype=jnp.bfloat16):
    factor_of = block_scale(rng, shape, shards, -0.22, 0.18) if shards else 1.0
    entries = jax.random.normal(rng, shape, jnp.float32) * width * factor_of
    return jnp.minimum(jnp.maximum(entries, -limit), limit).astype(dtype)


def setup_inputs(seed: int = 0) -> dict:
    keys = jax.random.split(jax.random.key(seed), 11)
    embeds = draw_embeds(jax.random.fold_in(keys[10], 71), 0)
    norm_gain = jnp.clip(1.0 + 0.1 * jax.random.normal(keys[1], (D,), jnp.float32), 0.5, 1.5).astype(jnp.bfloat16)
    query_weight = draw_query_weight(jax.random.fold_in(keys[10], 71), 0)
    key_weight = draw_key_weight(jax.random.fold_in(keys[10], 71), 0)
    value_weight = bell_draw(keys[4], (D, KVH * HD), D ** -0.5, 0.0625, ((0, 4), (1, 8)))
    out_weight = bell_draw(keys[5], (H * HD, D), (H * HD) ** -0.5, 0.0625, ((0, 8), (1, 4)))
    out_grad = bell_draw(keys[6], (PROMPTS, SEQ, D), 1.0, 6.0, ((0, 4), (2, 8)))
    suffix_pos = touch_ends(jax.random.randint(keys[7], (PROMPTS, NSUF), 0, SEQ), jax.random.fold_in(keys[7], 1), 0, SEQ - 1).astype(jnp.int32)
    vocab_table = bell_draw(keys[8], (V, D), D ** -0.5, 0.0625, ((0, 32),))
    banned = touch_ends((jax.random.randint(keys[9], (V,), 0, 8) < 1).astype(jnp.int32), jax.random.fold_in(keys[9], 1), 0, 1)
    return {"embeds": embeds, "norm_gain": norm_gain, "query_weight": query_weight, "key_weight": key_weight, "value_weight": value_weight, "out_weight": out_weight, "out_grad": out_grad, "suffix_pos": suffix_pos, "vocab_table": vocab_table, "banned": banned}


EPSILON = 1e-05

def take_one(rows_block, positions):
    return jnp.take(rows_block, positions, axis=0)

def reference(embeds, norm_gain, query_weight, key_weight, value_weight, out_weight, out_grad, suffix_pos, vocab_table, banned):
    prompts = embeds.shape[0]
    picker = jax.vmap(take_one)
    embeds_float = embeds.astype(jnp.float32)
    inverse_norm = lax.rsqrt(lax.optimization_barrier(jnp.mean(embeds_float * embeds_float, axis=-1, keepdims=True)) + EPSILON)
    gain_float = norm_gain.astype(jnp.float32)
    normed = (embeds_float * inverse_norm * gain_float).astype(jnp.bfloat16)
    flat_normed = normed.reshape(prompts * SEQ, D)
    queries = jnp.dot(flat_normed, query_weight, preferred_element_type=jnp.float32).astype(jnp.bfloat16)
    keys_all = jnp.dot(flat_normed, key_weight, preferred_element_type=jnp.float32).astype(jnp.bfloat16)
    values_all = jnp.dot(flat_normed, value_weight, preferred_element_type=jnp.float32).astype(jnp.bfloat16)
    group_size = H // KVH
    query_heads = queries.reshape(prompts, SEQ, H, HD).astype(jnp.float32)
    key_heads = jnp.tile(keys_all.reshape(prompts, SEQ, KVH, HD), (1, 1, group_size, 1)).astype(jnp.float32)
    value_heads = jnp.tile(values_all.reshape(prompts, SEQ, KVH, HD), (1, 1, group_size, 1)).astype(jnp.float32)
    logit_scale = 1.0 / math.sqrt(HD)
    logits = jnp.einsum('pqhd,pkhd->phqk', query_heads, key_heads) * logit_scale
    row_index = lax.broadcasted_iota(jnp.int32, (SEQ, SEQ), 0)
    col_index = lax.broadcasted_iota(jnp.int32, (SEQ, SEQ), 1)
    causal = col_index <= row_index
    largest = lax.optimization_barrier(jnp.max(jnp.where(causal, logits, -1e+30), axis=-1, keepdims=True))
    raised = jnp.where(causal, jnp.exp(logits - largest), 0.0)
    probs_float = raised / lax.optimization_barrier(jnp.sum(raised, axis=-1, keepdims=True))
    probs_low = probs_float.astype(jnp.bfloat16)
    context_grad = jnp.dot(out_grad.reshape(prompts * SEQ, D), out_weight.T, preferred_element_type=jnp.float32).astype(jnp.bfloat16)
    context_heads = context_grad.reshape(prompts, SEQ, H, HD).astype(jnp.float32)
    prob_grad = jnp.einsum('pqhd,pkhd->phqk', context_heads, value_heads)
    logit_grad = (probs_float * (prob_grad - lax.optimization_barrier(jnp.sum(prob_grad * probs_float, axis=-1, keepdims=True))) * logit_scale).astype(jnp.bfloat16)
    logit_float = logit_grad.astype(jnp.float32)
    query_grad = jnp.einsum('phqk,pkhd->pqhd', logit_float, key_heads).astype(jnp.bfloat16).reshape(prompts, SEQ, H * HD)
    key_each = jnp.einsum('phqk,pqhd->pkhd', logit_float, query_heads)
    key_grad = lax.optimization_barrier(jnp.sum(key_each.reshape(prompts, SEQ, group_size, KVH, HD), axis=2)).astype(jnp.bfloat16).reshape(prompts, SEQ, KVH * HD)
    value_each = jnp.einsum('phqk,pqhd->pkhd', probs_low.astype(jnp.float32), context_heads)
    value_grad = lax.optimization_barrier(jnp.sum(value_each.reshape(prompts, SEQ, group_size, KVH, HD), axis=2)).astype(jnp.bfloat16).reshape(prompts, SEQ, KVH * HD)
    query_rows = picker(query_grad, suffix_pos).reshape(prompts * NSUF, H * HD)
    key_rows = picker(key_grad, suffix_pos).reshape(prompts * NSUF, KVH * HD)
    value_rows = picker(value_grad, suffix_pos).reshape(prompts * NSUF, KVH * HD)
    branch = jnp.dot(query_rows, query_weight.T, preferred_element_type=jnp.float32)
    branch = branch + jnp.dot(key_rows, key_weight.T, preferred_element_type=jnp.float32)
    branch = branch + jnp.dot(value_rows, value_weight.T, preferred_element_type=jnp.float32)
    branch = branch.reshape(prompts, NSUF, D)
    embed_rows = picker(embeds_float, suffix_pos)
    norm_rows = picker(inverse_norm, suffix_pos)
    scaled = embed_rows * norm_rows
    weighted = branch * gain_float
    suffix_grad = (norm_rows * (weighted - scaled * lax.optimization_barrier(jnp.mean(weighted * scaled, axis=-1, keepdims=True)))).astype(jnp.bfloat16)
    scores = -jnp.dot(suffix_grad.reshape(prompts * NSUF, D), vocab_table.T, preferred_element_type=jnp.float32)
    scores = scores.reshape(prompts, NSUF, V)
    return jnp.where(banned[None, None, :] == 1, 0.0, scores)
```

```python
import functools
import math

import jax
import jax.numpy as jnp
from jax import lax
from jax.experimental import pallas as pl
from jax.experimental.pallas import tpu as pltpu
from jax.sharding import PartitionSpec as P

KVH = 8
HD = 128


EPSILON = 1e-05


def exchange_kernel(axis, count, spread, *refs):
    arrays = len(spread)
    sources, targets = refs[:arrays], refs[arrays : 2 * arrays]
    send_sem, recv_sem, own_sem = refs[2 * arrays :]
    here = lax.axis_index(axis)

    def block(i, to):
        return sources[i].at[to] if spread[i] else sources[i]

    kept = []
    for i in range(arrays):
        copy = pltpu.make_async_copy(block(i, here), targets[i].at[here], own_sem.at[i])
        copy.start()
        kept.append(copy)
    barrier = pltpu.get_barrier_semaphore()
    for step in range(1, count):
        peer = lax.rem(here + step, count)
        pl.semaphore_signal(
            barrier, inc=1, device_id={axis: peer}, device_id_type=pl.DeviceIdType.MESH
        )
    pl.semaphore_wait(barrier, count - 1)
    copies = []
    for step in range(1, count):
        peer = lax.rem(here + step, count)
        for i in range(arrays):
            copy = pltpu.make_async_remote_copy(
                src_ref=block(i, peer),
                dst_ref=targets[i].at[here],
                send_sem=send_sem.at[i, step - 1],
                recv_sem=recv_sem.at[i, step - 1],
                device_id={axis: peer},
                device_id_type=pl.DeviceIdType.MESH,
            )
            copy.start()
            copies.append(copy)
    for copy in kept + copies:
        copy.wait()


def exchange(axis, number, *operands):
    count = lax.axis_size(axis)
    arrays = [array for array, _ in operands]
    spread = tuple(each for _, each in operands)
    shapes = [
        jax.ShapeDtypeStruct(((count,) + (a.shape[1:] if each else a.shape)), a.dtype)
        for a, each in operands
    ]
    space = pl.BlockSpec(memory_space=pltpu.VMEM)
    sems = pltpu.SemaphoreType.DMA((len(arrays), count - 1))
    return pl.pallas_call(
        functools.partial(exchange_kernel, axis, count, spread),
        out_shape=shapes,
        in_specs=[space] * len(arrays),
        out_specs=[space] * len(arrays),
        scratch_shapes=[sems, sems, pltpu.SemaphoreType.DMA((len(arrays),))],
        compiler_params=pltpu.CompilerParams(
            collective_id=number, has_side_effects=True, vmem_limit_bytes=40 << 20
        ),
    )(*arrays)


def dot_f32(spec, a, b):
    return jnp.einsum(spec, a, b, preferred_element_type=jnp.float32)


MESH = pl.DeviceIdType.MESH


def greet(axis, peers):
    barrier = pltpu.get_barrier_semaphore()
    for peer in peers:
        pl.semaphore_signal(barrier, inc=1, device_id={axis: peer}, device_id_type=MESH)
    pl.semaphore_wait(barrier, len(peers))


def gather_kernel(axis, count, arrays, *refs):
    sources, targets = refs[:arrays], refs[arrays : 2 * arrays]
    send_sem, recv_sem, own_sem = refs[2 * arrays :]
    here = lax.axis_index(axis)
    chips = count // 2
    chip, core = here // 2, lax.rem(here, 2)
    pair = 2 * chip + (1 - core)
    kept = []
    for i in range(arrays):
        copy = pltpu.make_async_copy(sources[i], targets[i].at[here], own_sem.at[i])
        copy.start()
        kept.append(copy)

    def push(i, source, slot, number, peer):
        return pltpu.make_async_remote_copy(
            src_ref=source,
            dst_ref=targets[i].at[slot],
            send_sem=send_sem.at[i, number],
            recv_sem=recv_sem.at[i, number],
            device_id={axis: peer},
            device_id_type=MESH,
        )

    others = [2 * lax.rem(chip + step, chips) + core for step in range(1, chips)]
    greet(axis, others + [pair])
    first = []
    for step in range(1, chips):
        for i in range(arrays):
            copy = push(i, sources[i], here, step, others[step - 1])
            copy.start()
            first.append(copy)
    rest = []
    for i in range(arrays):
        copy = push(i, sources[i], here, 0, pair)
        copy.start()
        rest.append(copy)
    for step in range(1, chips):
        slot = 2 * lax.rem(chip + chips - step, chips) + core
        for i in range(arrays):
            first[(step - 1) * arrays + i].wait_recv()
            copy = push(i, targets[i].at[slot], slot, chips - 1 + step, pair)
            copy.start()
            rest.append(copy)
    for copy in first:
        copy.wait_send()
    for copy in kept + rest:
        copy.wait()


def gather(axis, number, *arrays):
    count = lax.axis_size(axis)
    shapes = [jax.ShapeDtypeStruct((count,) + a.shape, a.dtype) for a in arrays]
    space = pl.BlockSpec(memory_space=pltpu.VMEM)
    sems = pltpu.SemaphoreType.DMA((len(arrays), count - 1))
    return pl.pallas_call(
        functools.partial(gather_kernel, axis, count, len(arrays)),
        out_shape=shapes,
        in_specs=[space] * len(arrays),
        out_specs=[space] * len(arrays),
        scratch_shapes=[sems, sems, pltpu.SemaphoreType.DMA((len(arrays),))],
        compiler_params=pltpu.CompilerParams(
            collective_id=number, has_side_effects=True, vmem_limit_bytes=40 << 20
        ),
    )(*arrays)


def line_kernel(axis, source, target, relay, send_sem, recv_sem, own_sem):
    here = lax.axis_index(axis)
    own = pltpu.make_async_copy(source.at[here], target.at[here], own_sem.at[0])
    own.start()
    greet(axis, [lax.rem(here + step, 4) for step in range(1, 4)])

    def push(block, slot, number, peer, into=None):
        return pltpu.make_async_remote_copy(
            src_ref=block,
            dst_ref=target.at[slot] if into is None else into,
            send_sem=send_sem.at[number],
            recv_sem=recv_sem.at[slot if into is None else 4],
            device_id={axis: peer},
            device_id_type=MESH,
        )

    for role in range(4):
        far = 3 if role < 2 else 0
        middle = 1 if role < 2 else 2
        across = 3 - middle

        @pl.when(here == role)
        def _():
            if role == middle:
                sent = [
                    push(source.at[across], role, 0, across),
                    push(source.at[3 - far], role, 1, 3 - far),
                ]
                for copy in sent:
                    copy.start()
                total = push(relay, role, 2, far)
                push(source.at[far], role, 3, far, relay).wait_recv()
                relay[...] = relay[...] + source[far]
                total.start()
                sent.append(total)
                arriving = [0, across, 3]
            else:
                handed = push(source.at[far], role, 0, middle, relay)
                handed.start()
                target[far] = jnp.zeros_like(target[far])
                handed.wait_send()
                sent = [
                    push(source.at[across], role, 1, across),
                    push(source.at[middle], role, 2, middle),
                ]
                for copy in sent:
                    copy.start()
                arriving = [1, 2]
            for slot in arriving:
                push(source.at[slot], slot, 3, slot).wait_recv()
            for copy in sent:
                copy.wait_send()

    own.wait()


def line_exchange(axis, number, blocks):
    if lax.axis_size(axis) != 4:
        return exchange(axis, number, (blocks, True))[0]
    space = pl.BlockSpec(memory_space=pltpu.VMEM)
    return pl.pallas_call(
        functools.partial(line_kernel, axis),
        out_shape=jax.ShapeDtypeStruct(blocks.shape, blocks.dtype),
        in_specs=[space],
        out_specs=space,
        scratch_shapes=[
            pltpu.VMEM(blocks.shape[1:], blocks.dtype),
            pltpu.SemaphoreType.DMA((4,)),
            pltpu.SemaphoreType.DMA((5,)),
            pltpu.SemaphoreType.DMA((1,)),
        ],
        compiler_params=pltpu.CompilerParams(
            collective_id=number, has_side_effects=True, vmem_limit_bytes=40 << 20
        ),
    )(blocks)


CHUNK = 512


def score_kernel(
    axis, count, part, vocab, scores, got, flat, table, send_sem, recv_sem, own_sem, load_sem
):
    def load(c):
        span = pl.ds(pl.multiple_of(c * CHUNK, CHUNK), CHUNK)
        return pltpu.make_async_copy(vocab.at[span], table.at[span], load_sem.at[c])

    chunks = vocab.shape[0] // CHUNK
    for c in range(chunks):
        load(c).start()
    gather_kernel(axis, count, 1, part, got, send_sem, recv_sem, own_sem)
    wide = part.shape[2]
    for p in range(part.shape[0]):
        for t in range(count):
            start = (p * count + t) * wide
            flat[:, start : start + wide] = got[t, p]

    @pl.loop(0, chunks)
    def _(c):
        load(c).wait()
        span = pl.ds(pl.multiple_of(c * CHUNK, CHUNK), CHUNK)
        scores[:, span] = -lax.dot_general(
            flat[...],
            table[span, :],
            (((1,), (1,)), ((), ())),
            preferred_element_type=jnp.float32,
        )


def gather_score(axis, number, part, vocab):
    count = lax.axis_size(axis)
    n_prompt, rows, wide = part.shape
    vocab_here, width = vocab.shape
    if wide % 128 or vocab_here % CHUNK or rows % 16:
        (part,) = gather(axis, number, part)
        return -dot_f32("rd,vd->rv", part.transpose(2, 1, 0, 3).reshape(rows, width), vocab)
    sems = pltpu.SemaphoreType.DMA((1, count - 1))
    return pl.pallas_call(
        functools.partial(score_kernel, axis, count),
        out_shape=jax.ShapeDtypeStruct((rows, vocab_here), jnp.float32),
        in_specs=[pl.BlockSpec(memory_space=pltpu.VMEM), pl.BlockSpec(memory_space=pl.ANY)],
        out_specs=pl.BlockSpec(memory_space=pltpu.VMEM),
        scratch_shapes=[
            pltpu.VMEM((count,) + part.shape, part.dtype),
            pltpu.VMEM((rows, width), part.dtype),
            pltpu.VMEM(vocab.shape, vocab.dtype),
            sems,
            sems,
            pltpu.SemaphoreType.DMA((1,)),
            pltpu.SemaphoreType.DMA((vocab_here // CHUNK,)),
        ],
        compiler_params=pltpu.CompilerParams(
            collective_id=number, has_side_effects=True, vmem_limit_bytes=52 << 20
        ),
    )(part, vocab)


def on_device(
    embeds,
    norm_gain,
    query_weight,
    key_weight,
    value_weight,
    out_weight,
    out_grad,
    suffix_pos,
    vocab_table,
    banned,
):
    n_prompt = lax.axis_size("prompt")
    n_tensor = lax.axis_size("tensor")
    here_prompt = lax.axis_index("prompt")
    here_tensor = lax.axis_index("tensor")
    seq_len = embeds.shape[1]
    suffix_count = suffix_pos.shape[1]
    width = embeds.shape[2] * n_tensor
    rows_here, head_cols = query_weight.shape
    key_cols = key_weight.shape[1]
    heads_here = head_cols // HD
    slice_width = rows_here // n_tensor
    logit_scale = 1.0 / math.sqrt(HD)

    split_rows = seq_len // n_tensor
    ratio = n_tensor // n_prompt
    feature_cols = embeds.shape[2]
    both = jnp.concatenate(
        [
            embeds.reshape(n_tensor, split_rows, feature_cols),
            out_grad.reshape(n_tensor, split_rows, feature_cols),
        ],
        axis=1,
    )
    (both,) = exchange("tensor", 0, (both, True))
    own = both[:, :split_rows].astype(jnp.float32)
    inverse_norm = lax.rsqrt(jnp.sum(own * own, axis=(0, 2))[:, None] / width + EPSILON)
    inverse_norm = jnp.broadcast_to(inverse_norm, (split_rows, 128))
    both = both.reshape(n_prompt, ratio, 2 * split_rows, feature_cols)
    both, inverse_norm, suffix_all = exchange(
        "prompt", 1, (both, True), (inverse_norm, False), (suffix_pos, False)
    )
    both, inverse_norm = gather("tensor", 2, both, inverse_norm)
    suffix_all = suffix_all.reshape(n_prompt, suffix_count)
    both = both.reshape(n_tensor, n_prompt, ratio, 2, split_rows, feature_cols)
    both = both.transpose(3, 1, 0, 4, 2, 5).reshape(2, n_prompt, seq_len, rows_here)
    embeds, out_grad = both[0], both[1]
    inverse_norm = inverse_norm[..., :1].transpose(1, 0, 2, 3).reshape(n_prompt, seq_len, 1)
    embeds_float = embeds.astype(jnp.float32)
    gain_rows = lax.dynamic_slice_in_dim(norm_gain, here_prompt * rows_here, rows_here, 0)
    gain_rows = gain_rows.astype(jnp.float32)
    normed = (embeds_float * inverse_norm * gain_rows).astype(jnp.bfloat16)

    parts = jnp.concatenate(
        [
            dot_f32("psd,dc->psc", normed, query_weight),
            dot_f32("psd,dc->psc", normed, key_weight),
            dot_f32("psd,dc->psc", normed, value_weight),
            dot_f32("psd,cd->psc", out_grad, out_weight),
        ],
        axis=2,
    )
    parts = line_exchange("prompt", 3, parts)
    whole = jnp.sum(parts, axis=0).astype(jnp.bfloat16)
    contexts = whole[:, head_cols + 2 * key_cols :]
    contexts = contexts.reshape(seq_len, heads_here, HD)
    queries = whole[:, :head_cols].reshape(seq_len, heads_here, HD)
    (key_values,) = gather("tensor", 4, whole[:, head_cols : head_cols + 2 * key_cols])
    key_values = key_values.reshape(n_tensor, seq_len, 2, key_cols).transpose(2, 1, 0, 3)
    key_values = key_values.reshape(2, seq_len, KVH * HD)
    fold = min(heads_here, KVH)
    first = ((here_tensor * heads_here) % KVH) * HD
    if fold < KVH:
        key_values = lax.dynamic_slice_in_dim(key_values, first, fold * HD, 2)
    key_values = key_values.reshape(2, seq_len, fold, HD)
    if heads_here > fold:
        key_values = jnp.tile(key_values, (1, 1, heads_here // fold, 1))
    keys, values = key_values[0], key_values[1]

    logits = dot_f32("qhd,khd->hqk", queries, keys) * logit_scale
    row_index = lax.broadcasted_iota(jnp.int32, (seq_len, seq_len), 0)
    col_index = lax.broadcasted_iota(jnp.int32, (seq_len, seq_len), 1)
    causal = col_index <= row_index
    largest = jnp.max(jnp.where(causal, logits, -1e30), axis=-1, keepdims=True)
    raised = jnp.where(causal, jnp.exp(logits - largest), 0.0)
    probs = raised / jnp.sum(raised, axis=-1, keepdims=True)
    probs_low = probs.astype(jnp.bfloat16)
    prob_grad = dot_f32("qhd,khd->hqk", contexts, values)
    logit_grad = (
        probs * (prob_grad - jnp.sum(prob_grad * probs, axis=-1, keepdims=True)) * logit_scale
    ).astype(jnp.bfloat16)
    steps_iota = lax.broadcasted_iota(jnp.int32, (suffix_count, seq_len), 1)
    chooser = (steps_iota == suffix_pos[0][:, None]).astype(jnp.bfloat16)
    logit_rows = dot_f32("ns,hsk->hnk", chooser, logit_grad).astype(jnp.bfloat16)
    query_grad = dot_f32("hnk,khd->nhd", logit_rows, keys).astype(jnp.bfloat16)
    query_grad = query_grad.reshape(suffix_count, head_cols)
    logit_cols = dot_f32("hqk,nk->hnq", logit_grad, chooser).astype(jnp.bfloat16)
    prob_cols = dot_f32("hqk,nk->hnq", probs_low, chooser).astype(jnp.bfloat16)
    key_each = dot_f32("hnq,qhd->nhd", logit_cols, queries)
    value_each = dot_f32("hnq,qhd->nhd", prob_cols, contexts)
    slots = jnp.stack([key_each, value_each])
    slots = slots.reshape(2, suffix_count, heads_here // fold, fold * HD).sum(axis=2)
    if fold < KVH:
        slots = lax.dynamic_update_slice_in_dim(
            jnp.zeros((2, suffix_count, KVH * HD), jnp.float32), slots, first, 2
        )
    slots = slots.reshape(2 * suffix_count, n_tensor, key_cols).transpose(1, 0, 2)
    (grads,) = exchange("tensor", 5, (slots, True))
    grads = jnp.sum(grads, axis=0).astype(jnp.bfloat16).reshape(2, suffix_count, key_cols)
    grads = jnp.concatenate([query_grad, grads[0], grads[1]], axis=1)
    (grads,) = exchange("prompt", 6, (grads, False))
    rows = n_prompt * suffix_count
    grads = grads.reshape(rows, head_cols + 2 * key_cols)
    steps_iota = lax.broadcasted_iota(jnp.int32, (n_prompt, suffix_count, seq_len), 2)
    chooser_all = steps_iota == suffix_all[:, :, None]
    embed_rows = dot_f32("pns,psd->pnd", chooser_all.astype(jnp.bfloat16), embeds)
    norm_rows = jnp.sum(
        jnp.where(chooser_all, inverse_norm[:, None, :, 0], 0.0), axis=-1, keepdims=True
    )
    scaled = (embed_rows * norm_rows).reshape(rows, rows_here)
    norm_rows = norm_rows.reshape(rows, 1)
    branch = dot_f32("nc,dc->nd", grads[:, :head_cols], query_weight)
    branch = branch + dot_f32("nc,dc->nd", grads[:, head_cols : head_cols + key_cols], key_weight)
    branch = branch + dot_f32("nc,dc->nd", grads[:, head_cols + key_cols :], value_weight)
    branch = branch * gain_rows
    inner = jnp.sum(branch * scaled, axis=-1)
    branch = branch.reshape(rows, n_tensor, slice_width).transpose(1, 0, 2)
    share, inner = exchange("tensor", 7, (branch, True), (inner[None, :], False))
    weighted = jnp.sum(share, axis=0)
    (inner,) = exchange("prompt", 8, (jnp.sum(inner, axis=0), False))
    inner = jnp.sum(inner, axis=0).reshape(rows, 1) / width
    scaled = lax.dynamic_slice_in_dim(scaled, here_tensor * slice_width, slice_width, 1)
    suffix_grad = (norm_rows * (weighted - scaled * inner)).astype(jnp.bfloat16)
    (suffix_grad,) = exchange("prompt", 9, (suffix_grad, False))
    scores = gather_score("tensor", 10, suffix_grad, vocab_table)
    scores = scores.reshape(n_prompt, suffix_count, vocab_table.shape[0])
    return jnp.where(banned[None, None, :] == 1, 0.0, scores)


PAD = 32
TINY = 1e-30
FULL = 32767.0
SEMS = 208


def pick_column(row, rows):
    wide = row.shape[1]
    down = lax.broadcasted_iota(jnp.int32, (rows, wide), 0)
    along = lax.broadcasted_iota(jnp.int32, (rows, wide), 1)
    return jnp.sum(jnp.where(down == along, row, 0.0), axis=1, keepdims=True)


def lay_row(column, wide):
    rows = column.shape[0]
    down = lax.broadcasted_iota(jnp.int32, (rows, wide), 0)
    along = lax.broadcasted_iota(jnp.int32, (rows, wide), 1)
    return jnp.sum(jnp.where(down == along, column, 0.0), axis=0, keepdims=True)


def lane_sums(values):
    total = values[:, :128]
    for j in range(128, values.shape[1], 128):
        total = total + values[:, j : j + 128]
    return jnp.sum(total, axis=1, keepdims=True)


def code_block(read, write, heads, rows):
    lanes = lax.broadcasted_iota(jnp.int32, (rows, HD), 1)
    powers = jnp.zeros((rows, HD), jnp.float32)
    for h in range(heads):
        block = read(h)
        peak = jnp.max(jnp.abs(block), axis=1, keepdims=True)
        power = jnp.floor(jnp.log2(jnp.maximum(peak, TINY))) + 1.0
        fixed = jnp.floor(block * (jnp.exp2(-power) * FULL) + 0.5)
        fixed = jnp.clip(fixed, -FULL, FULL)
        write(h, fixed.astype(jnp.int32).astype(jnp.int16))
        powers = jnp.where(lanes == h, power, powers)
    write(heads, powers.astype(jnp.int32).astype(jnp.int16))


def scale_of(tile):
    return jnp.exp2(tile.astype(jnp.int32).astype(jnp.float32)) * (1.0 / FULL)


def fused_kernel(
    embeds,
    out_grad,
    gain,
    query_weight,
    key_weight,
    value_weight,
    out_weight,
    suffix,
    vocab,
    banned,
    out,
    wq,
    wkv,
    wo,
    table,
    mine,
    stage,
    x,
    sums,
    norms,
    spots,
    nb,
    pkv,
    rkv,
    relay_kv,
    pp,
    coded,
    arrived,
    relay,
    total,
    kvg,
    whole,
    slots,
    slots_in,
    grads,
    scaled,
    weighted,
    pair_in,
    shares,
    inner_in,
    inner_z,
    suffix_grads,
    send_sem,
    recv_sem,
    load_sem,
    own_sem,
):
    z = lax.axis_index("prompt")
    t = lax.axis_index("tensor")
    chip, core = t // 2, lax.rem(t, 2)
    pair = 2 * chip + (1 - core)
    chip_y, chip_x = chip // 2, lax.rem(chip, 2)
    near = [
        chip,
        2 * chip_y + (1 - chip_x),
        2 * (1 - chip_y) + chip_x,
        2 * (1 - chip_y) + (1 - chip_x),
    ]
    seq, cols = embeds.shape[1], embeds.shape[2]
    width = gain.shape[1]
    rows_here, head_cols = query_weight.shape
    heads = head_cols // HD
    count = suffix.shape[1]
    rows = 4 * count
    quarter = seq // 4
    slice_width = rows_here // 8
    scale = 1.0 / math.sqrt(HD)
    dot = functools.partial(lax.dot_general, preferred_element_type=jnp.float32)
    plain = (((1,), (0,)), ((), ()))
    crossed = (((1,), (1,)), ((), ()))

    chunks = vocab.shape[0] // CHUNK

    def load_table(c):
        span = pl.ds(pl.multiple_of(c * CHUNK, CHUNK), CHUNK)
        return pltpu.make_async_copy(vocab.at[span], table.at[span], load_sem.at[8 + c])

    loads = {
        "e": pltpu.make_async_copy(embeds.at[0], mine, load_sem.at[0]),
        "k": pltpu.make_async_copy(key_weight, wkv.at[:, :HD], load_sem.at[1]),
        "v": pltpu.make_async_copy(value_weight, wkv.at[:, HD:], load_sem.at[2]),
        "q": pltpu.make_async_copy(query_weight, wq, load_sem.at[3]),
        "o": pltpu.make_async_copy(out_weight, wo, load_sem.at[4]),
    }
    for each in loads.values():
        each.start()
    for c in range(chunks):
        load_table(c).start()

    barrier = pltpu.get_barrier_semaphore()
    for step in range(1, 8):
        pl.semaphore_signal(
            barrier, inc=1, device_id={"tensor": lax.rem(t + step, 8)}, device_id_type=MESH
        )
    for step in range(1, 4):
        pl.semaphore_signal(
            barrier, inc=1, device_id={"prompt": lax.rem(z + step, 4)}, device_id_type=MESH
        )
    pl.semaphore_wait(barrier, 10)

    used = [0]
    sent = []

    def take(number=1):
        used[0] += number
        assert used[0] <= SEMS
        return used[0] - number

    def move(source, target, s, r, device):
        return pltpu.make_async_remote_copy(
            src_ref=source,
            dst_ref=target,
            send_sem=send_sem.at[s],
            recv_sem=recv_sem.at[r],
            device_id=device,
            device_id_type=MESH,
        )

    def push(source, target, s, r, device):
        copy = move(source, target, s, r, device)
        copy.start()
        sent.append(copy)

    def plane(s, other=False):
        return {"tensor": 2 * near[s] + ((1 - core) if other else core)}

    def along(step):
        return {"prompt": lax.rem(z + step, 4)}

    def rows_of(chip_index):
        return pl.ds(pl.multiple_of(quarter * chip_index, quarter), quarter)

    sources = (embeds.at[0], out_grad.at[0])
    own_cols = pl.ds(pl.multiple_of(core * cols, 128), cols)
    pair_cols = pl.ds(pl.multiple_of((1 - core) * cols, 128), cols)

    hop = [take(4) for _ in range(2)]
    for a in range(2):
        for s in (3, 1, 2):
            push(
                sources[a].at[rows_of(near[s])], stage.at[a, s - 1], hop[a] + s, hop[a] + s, plane(s)
            )
    at_spots = take(4)
    for step in range(1, 4):
        push(suffix, spots.at[z], at_spots + step, at_spots + step, along(step))
    spots[z] = suffix[...]

    loads["e"].wait()
    square = jnp.zeros((seq, 128), jnp.float32)
    for j in range(0, cols, 128):
        block = mine[:, j : j + 128].astype(jnp.float32)
        square = square + block * block
    square = jnp.sum(square, axis=1, keepdims=True)
    sums[t] = jnp.broadcast_to(lay_row(square, 128), (8, 128))
    at_sums = take(8)
    for step in range(1, 8):
        push(
            sums.at[t], sums.at[t], at_sums + step, at_sums + step, {"tensor": lax.rem(t + step, 8)}
        )

    across = [take(4) for _ in range(2)]
    across_in = [take(4) for _ in range(2)]

    def second_hop(a):
        for s in range(4):
            if s == 0:
                block = sources[a].at[rows_of(chip)]
            else:
                move(stage.at[a, s - 1], stage.at[a, s - 1], 0, hop[a] + s, plane(s)).wait_recv()
                block = stage.at[a, s - 1]
            target = x.at[a, z, rows_of(chip), own_cols]

            @pl.when(near[s] == z)
            def _():
                copy = pltpu.make_async_copy(block, target, own_sem.at[a])
                copy.start()
                copy.wait()

            @pl.when(near[s] != z)
            def _():
                move(block, target, across[a] + s, across_in[a] + z, {"prompt": near[s]}).start()

    second_hop(0)
    for step in range(1, 8):
        move(sums.at[t], sums.at[t], 0, at_sums + step, plane(1)).wait_recv()
    square = sums[0]
    for j in range(1, 8):
        square = square + sums[j]
    norms[z] = lax.rsqrt(square / width + EPSILON)
    at_norms = take(4)
    for step in range(1, 4):
        push(norms.at[z], norms.at[z], at_norms + step, at_norms + step, along(step))
    second_hop(1)

    order = (0, 1, 3, 2)
    third = [[take(4) for _ in range(4)] for _ in range(2)]
    fourth = [[take(4) for _ in range(4)] for _ in range(2)]

    def third_hop(a):
        for step in order:
            p = lax.rem(z + step, 4)
            block = x.at[a, p, rows_of(chip), own_cols]
            if step:
                move(block, block, 0, across_in[a] + p, plane(1)).wait_recv()
            for s in (3, 1, 2):
                push(block, block, third[a][step] + s, third[a][step] + s, plane(s))
            push(block, block, third[a][step], third[a][step], {"tensor": pair})

    def fourth_hop(a):
        for step in order:
            p = lax.rem(z + step, 4)
            for s in (1, 2, 3):
                block = x.at[a, p, rows_of(near[s]), own_cols]
                move(block, block, 0, third[a][step] + s, plane(s)).wait_recv()
                push(block, block, fourth[a][step] + s, fourth[a][step] + s, {"tensor": pair})

    def last_hop(a):
        for step in order:
            p = lax.rem(z + step, 4)
            for s in range(4):
                block = x.at[a, p, rows_of(near[s]), pair_cols]
                number = fourth[a][step] + s if s else third[a][step]
                move(block, block, 0, number, {"tensor": pair}).wait_recv()

    third_hop(0)
    third_hop(1)
    fourth_hop(0)
    last_hop(0)

    for step in range(1, 4):
        move(norms.at[z], norms.at[z], 0, at_norms + step, plane(1)).wait_recv()
        move(suffix, spots.at[z], 0, at_spots + step, plane(1)).wait_recv()

    gain_here = pl.ds(pl.multiple_of(z * rows_here, 128), rows_here)

    @pl.loop(0, 4)
    def _(p):
        inverse = pick_column(norms[p][:1], seq)
        gains = gain[:, gain_here].astype(jnp.float32)
        for j in range(0, rows_here, 512):
            block = x[0, p, :, j : j + 512].astype(jnp.float32)
            block = block * inverse * gains[:, j : j + 512]
            nb[p, :, j : j + 512] = block.astype(jnp.bfloat16)

    loads["k"].wait()
    loads["v"].wait()
    normed = nb[...].reshape(4 * seq, rows_here)
    pkv[...] = dot(normed, wkv[...], plain).reshape(4, seq, 2 * HD)

    is_end = (z == 0) | (z == 3)
    is_mid = (z == 1) | (z == 2)
    end_far, end_mid = 3 - z, 1 + z // 3
    mid_far, mid_near = 6 - 3 * z, 3 * z - 3

    def line_sends(block, into, relay_into, base):
        hand = move(block(end_far), relay_into, base, base + 4, {"prompt": end_mid})
        one = move(block(3 - end_mid), into.at[z], base + 1, base + z, {"prompt": 3 - end_mid})
        two = move(block(end_mid), into.at[z], base + 2, base + z, {"prompt": end_mid})
        over = move(block(3 - z), into.at[z], base, base + z, {"prompt": 3 - z})
        back = move(block(mid_near), into.at[z], base + 1, base + z, {"prompt": mid_near})
        return (hand, one, two), (over, back)

    def line_start(block, into, relay_into, base):
        ends, mids = line_sends(block, into, relay_into, base)

        @pl.when(is_end)
        def _():
            for copy in ends:
                copy.start()

        @pl.when(is_mid)
        def _():
            for copy in mids:
                copy.start()

    def line_relay(block, into, relay_into, base, add, out_block):
        @pl.when(is_mid)
        def _():
            move(relay_into, relay_into, 0, base + 4, {"prompt": mid_far}).wait_recv()
            add()
            move(out_block, into.at[z], base + 2, base + z, {"prompt": mid_far}).start()

    def line_arrive(into, base):
        @pl.when(is_end)
        def _():
            for source in (end_mid, 3 - end_mid):
                move(into.at[z], into.at[z], 0, base + source, plane(1)).wait_recv()

        @pl.when(is_mid)
        def _():
            for source in (0, 3, 3 - z):
                move(into.at[z], into.at[z], 0, base + source, plane(1)).wait_recv()

    def line_sent(block, into, relay_into, base, out_block):
        ends, mids = line_sends(block, into, relay_into, base)

        @pl.when(is_end)
        def _():
            for copy in ends:
                copy.wait_send()

        @pl.when(is_mid)
        def _():
            for copy in mids:
                copy.wait_send()
            move(out_block, into.at[z], base + 2, base + z, {"prompt": mid_far}).wait_send()

    @pl.when(is_end)
    def _():
        rkv[end_far] = jnp.zeros(rkv.shape[1:], rkv.dtype)
        for i in range(2):
            arrived[i, end_far] = jnp.zeros(arrived.shape[2:], arrived.dtype)

    line_kv = take(5)
    line = [take(5) for _ in range(2)]
    kv_args = (lambda d: pkv.at[d], rkv, relay_kv)
    line_start(*kv_args, line_kv)

    def code(i):
        for step in (3, 2, 1):
            d = lax.rem(z + step, 4)

            def write(h, tile):
                coded[i, d, :, h * HD : (h + 1) * HD] = tile

            code_block(lambda h: pp[i, d, :, h * HD : (h + 1) * HD], write, heads, seq)

    def line_of(i):
        return (lambda d: coded.at[i, d], arrived.at[i], relay.at[i])

    def add_coded(i):
        def add():
            factors = scale_of(relay[i, :, heads * HD :])

            def read(h):
                got = relay[i, :, h * HD : (h + 1) * HD].astype(jnp.int32).astype(jnp.float32)
                return got * factors[:, h : h + 1] + pp[i, mid_far, :, h * HD : (h + 1) * HD]

            def write(h, tile):
                total[i, :, h * HD : (h + 1) * HD] = tile

            code_block(read, write, heads, seq)

        return add

    loads["q"].wait()

    @pl.loop(0, head_cols // 256)
    def _(j):
        span = pl.ds(pl.multiple_of(j * 256, 256), 256)
        part = dot(nb[...].reshape(4 * seq, rows_here), wq[:, span], plain)
        pp[0, :, :, span] = part.reshape(4, seq, 256)

    code(0)
    line_start(*line_of(0), line[0])

    def add_kv():
        relay_kv[...] = relay_kv[...] + pkv[mid_far]

    line_relay(*kv_args, line_kv, add_kv, relay_kv)

    fourth_hop(1)
    last_hop(1)
    loads["o"].wait()

    @pl.loop(0, head_cols // 256)
    def _(j):
        span = pl.ds(pl.multiple_of(j * 256, 256), 256)
        part = dot(x[1].reshape(4 * seq, rows_here), wo[span, :], crossed)
        pp[1, :, :, span] = part.reshape(4, seq, 256)

    code(1)
    line_start(*line_of(1), line[1])

    line_arrive(rkv, line_kv)
    own = pkv[z]
    for step in range(1, 4):
        own = own + rkv[lax.rem(z + step, 4)]
    kvg[t] = own.astype(jnp.bfloat16)
    at_kv = take(8)
    for step in range(1, 8):
        push(kvg.at[t], kvg.at[t], at_kv + step, at_kv + step, {"tensor": lax.rem(t + step, 8)})
    line_relay(*line_of(0), line[0], add_coded(0), total.at[0])
    line_relay(*line_of(1), line[1], add_coded(1), total.at[1])

    down = lax.broadcasted_iota(jnp.int32, (rows, count), 0)
    over = lax.broadcasted_iota(jnp.int32, (rows, count), 1)
    place = jnp.zeros((rows, 1), jnp.float32)
    prompt_of = jnp.zeros((rows, 1), jnp.int32)
    row_at = lax.broadcasted_iota(jnp.int32, (rows, 1), 0)
    for p in range(4):
        found = jnp.where(down - p * count == over, spots[p].astype(jnp.float32), 0.0)
        place = place + jnp.sum(found, axis=1, keepdims=True)
        if p:
            prompt_of = prompt_of + (row_at >= p * count).astype(jnp.int32)
    place = place + seq * prompt_of.astype(jnp.float32)
    marks = lax.broadcasted_iota(jnp.int32, (rows, 4 * seq), 1).astype(jnp.float32)
    chosen = (marks == place).astype(jnp.bfloat16)
    norm_rows = jnp.zeros((rows, 1), jnp.float32)
    inside = lax.broadcasted_iota(jnp.int32, (rows, 128), 1).astype(jnp.float32)
    for p in range(4):
        hit = (inside + p * seq == place) & (inside < seq)
        norm_rows = norm_rows + jnp.sum(jnp.where(hit, norms[p][:1], 0.0), axis=1, keepdims=True)
    for j in range(0, rows_here, 512):
        block = x[0, :, :, j : j + 512].reshape(4 * seq, 512)
        scaled[:, j : j + 512] = dot(chosen, block, plain) * norm_rows

    def finish(i):
        line_arrive(arrived.at[i], line[i])
        factors = [scale_of(arrived[i, lax.rem(z + s, 4), :, heads * HD :]) for s in (1, 2, 3)]
        for h in range(heads):
            span = slice(h * HD, (h + 1) * HD)
            value = pp[i, z, :, span]
            for s in (1, 2, 3):
                got = arrived[i, lax.rem(z + s, 4), :, span].astype(jnp.int32)
                value = value + got.astype(jnp.float32) * factors[s - 1][:, h : h + 1]
            whole[i, :, span] = value.astype(jnp.bfloat16)

    finish(0)
    for step in range(1, 8):
        move(kvg.at[t], kvg.at[t], 0, at_kv + step, plane(1)).wait_recv()
    finish(1)

    own_spots = jnp.where(
        lax.broadcasted_iota(jnp.int32, (PAD, count), 0)
        == lax.broadcasted_iota(jnp.int32, (PAD, count), 1),
        suffix[...].astype(jnp.float32),
        0.0,
    )
    own_spots = jnp.sum(own_spots, axis=1, keepdims=True)
    real = lax.broadcasted_iota(jnp.int32, (PAD, 1), 0) < count
    own_spots = jnp.where(real, own_spots, -1.0)
    steps_iota = lax.broadcasted_iota(jnp.int32, (PAD, seq), 1).astype(jnp.float32)
    chooser = (steps_iota == own_spots).astype(jnp.bfloat16)
    causal = lax.broadcasted_iota(jnp.int32, (seq, seq), 1) <= lax.broadcasted_iota(
        jnp.int32, (seq, seq), 0
    )
    for h in range(heads):
        span = slice(h * HD, (h + 1) * HD)
        queries, contexts = whole[0, :, span], whole[1, :, span]
        keys, values = kvg[h, :, :HD], kvg[h, :, HD:]
        logits = dot(queries, keys, crossed) * scale
        largest = jnp.max(jnp.where(causal, logits, -1e30), axis=-1, keepdims=True)
        raised = jnp.where(causal, jnp.exp(logits - largest), 0.0)
        probs = raised / jnp.sum(raised, axis=-1, keepdims=True)
        probs_low = probs.astype(jnp.bfloat16)
        prob_grad = dot(contexts, values, crossed)
        less = jnp.sum(prob_grad * probs, axis=-1, keepdims=True)
        logit_grad = (probs * (prob_grad - less) * scale).astype(jnp.bfloat16)
        logit_rows = dot(chooser, logit_grad, plain).astype(jnp.bfloat16)
        grads[z, :, span] = dot(logit_rows, keys, plain).astype(jnp.bfloat16)
        logit_cols = dot(chooser, logit_grad, crossed).astype(jnp.bfloat16)
        prob_cols = dot(chooser, probs_low, crossed).astype(jnp.bfloat16)
        slots[h, :24] = dot(logit_cols, queries, plain)[:24]
        slots[h, 24:] = dot(prob_cols, contexts, plain)[:24]

    at_slots = take(8)
    for step in range(1, 8):
        to = lax.rem(t + step, 8)
        push(slots.at[to], slots_in.at[t], at_slots + step, at_slots + step, {"tensor": to})
    at_grads = take(8)
    head_part = grads.at[z, :, :head_cols]
    for step in (2, 1, 3):
        push(head_part, head_part, at_grads + step, at_grads + step, along(step))
    slots_in[t] = slots[t]
    for step in range(1, 8):
        move(slots_in.at[t], slots_in.at[t], 0, at_slots + step, plane(1)).wait_recv()
    summed = slots_in[0]
    for j in range(1, 8):
        summed = summed + slots_in[j]
    filler = jnp.zeros((PAD - 24, HD), jnp.float32)
    key_rows = jnp.concatenate([summed[:24], filler], axis=0)
    value_rows = jnp.concatenate([summed[24:], filler], axis=0)
    grads[z, :, head_cols : head_cols + HD] = key_rows.astype(jnp.bfloat16)
    grads[z, :, head_cols + HD :] = value_rows.astype(jnp.bfloat16)
    tail_part = grads.at[z, :, head_cols:]
    for step in (2, 1, 3):
        push(tail_part, tail_part, at_grads + 4 + step, at_grads + 4 + step, along(step))
    for step in range(1, 4):
        move(head_part, head_part, 0, at_grads + step, plane(1)).wait_recv()
        move(tail_part, tail_part, 0, at_grads + 4 + step, plane(1)).wait_recv()

    packed_at = lax.broadcasted_iota(jnp.int32, (rows, 4 * PAD), 1)
    packer = (packed_at - (PAD - count) * prompt_of == row_at).astype(jnp.bfloat16)
    packed = dot(packer, grads[...].reshape(4 * PAD, head_cols + 2 * HD), plain)
    packed = packed.astype(jnp.bfloat16)
    inner = jnp.zeros((rows, 128), jnp.float32)
    at_pair = take(4)
    for half in range(2):
        for s in range(4):
            owner = 2 * near[s] + ((1 - core) if half == 0 else core)
            span = pl.ds(pl.multiple_of(owner * slice_width, slice_width), slice_width)
            part = dot(packed[:, :head_cols], wq[span, :], crossed)
            part = part + dot(packed[:, head_cols:], wkv[span, :], crossed)
            where = pl.ds(pl.multiple_of(z * rows_here + owner * slice_width, 128), slice_width)
            part = part * gain[:, where].astype(jnp.float32)
            product = part * scaled[:, span]
            for j in range(0, slice_width, 128):
                inner = inner + product[:, j : j + 128]
            weighted[half, s] = part
            if half == 0:
                push(weighted.at[0, s], pair_in.at[s], at_pair + s, at_pair + s, {"tensor": pair})
    inner = jnp.sum(inner, axis=1, keepdims=True)
    inner_in[t] = jnp.broadcast_to(lay_row(inner, 128), (8, 128))
    at_inner = take(8)
    for step in range(1, 8):
        push(
            inner_in.at[t],
            inner_in.at[t],
            at_inner + step,
            at_inner + step,
            {"tensor": lax.rem(t + step, 8)},
        )
    at_shares = take(4)
    for s in (3, 1, 2, 0):
        move(pair_in.at[s], pair_in.at[s], 0, at_pair + s, {"tensor": pair}).wait_recv()
        weighted[1, s] = weighted[1, s] + pair_in[s]
        if s:
            push(weighted.at[1, s], shares.at[s - 1], at_shares + s, at_shares + s, plane(s))
    for step in range(1, 8):
        move(inner_in.at[t], inner_in.at[t], 0, at_inner + step, plane(1)).wait_recv()
    inner = inner_in[0]
    for j in range(1, 8):
        inner = inner + inner_in[j]
    inner_z[z] = inner
    at_inner_z = take(4)
    for step in range(1, 4):
        push(inner_z.at[z], inner_z.at[z], at_inner_z + step, at_inner_z + step, along(step))
    for s in (1, 2, 3):
        move(shares.at[s - 1], shares.at[s - 1], 0, at_shares + s, plane(1)).wait_recv()
    own = weighted[1, 0] + shares[0] + shares[1] + shares[2]
    for step in range(1, 4):
        move(inner_z.at[z], inner_z.at[z], 0, at_inner_z + step, plane(1)).wait_recv()
    inner = (inner_z[0] + inner_z[1] + inner_z[2] + inner_z[3])[:1]
    inner = pick_column(inner, rows) / width

    here = pl.ds(pl.multiple_of(t * slice_width, slice_width), slice_width)
    suffix_grads[z, :, here] = (norm_rows * (own - scaled[:, here] * inner)).astype(jnp.bfloat16)

    def grad_of(p, chip_index, core_index):
        first = (2 * chip_index + core_index) * slice_width
        return suffix_grads.at[p, :, pl.ds(pl.multiple_of(first, slice_width), slice_width)]

    at_z = take(4)
    spread = [take(4) for _ in range(4)]
    doubled = [take(4) for _ in range(4)]
    mine_now = grad_of(z, chip, core)
    for step in (2, 1, 3):
        push(mine_now, mine_now, at_z + step, at_z + step, along(step))
    for step in order:
        block = grad_of(lax.rem(z - step + 4, 4), chip, core)
        if step:
            move(block, block, 0, at_z + step, plane(1)).wait_recv()
        for s in (3, 1, 2):
            push(block, block, spread[step] + s, spread[step] + s, plane(s))
        push(block, block, spread[step], spread[step], {"tensor": pair})

    for i, step in enumerate(order):
        p = lax.rem(z - step + 4, 4)
        for s in (1, 2, 3):
            block = grad_of(p, near[s], core)
            move(block, block, 0, spread[step] + s, plane(s)).wait_recv()
            push(block, block, doubled[step] + s, doubled[step] + s, {"tensor": pair})
        for s in range(4):
            block = grad_of(p, near[s], 1 - core)
            number = doubled[step] + s if s else spread[step]
            move(block, block, 0, number, {"tensor": pair}).wait_recv()
        features = pl.ds(pl.multiple_of(p * rows_here, rows_here), rows_here)

        @pl.loop(0, chunks)
        def _(c):
            if i == 0:
                load_table(c).wait()
            span = pl.ds(pl.multiple_of(c * CHUNK, CHUNK), CHUNK)
            part = dot(suffix_grads[p], table[span, features], crossed)
            if i:
                part = part + out[:, span]
            if i == 3:
                part = jnp.where(banned[:, span] == 1, 0.0, -part)
            out[:, span] = part

    for copy in sent:
        copy.wait_send()
    for a in range(2):
        for s in range(4):

            @pl.when(near[s] != z)
            def _():
                block = x.at[a, z, rows_of(chip), own_cols]
                move(block, block, across[a] + s, 0, {"prompt": near[s]}).wait_send()

    line_sent(*kv_args, line_kv, relay_kv)
    for i in range(2):
        line_sent(*line_of(i), line[i], total.at[i])


def fused(
    embeds,
    norm_gain,
    query_weight,
    key_weight,
    value_weight,
    out_weight,
    out_grad,
    suffix_pos,
    vocab_table,
    banned,
):
    seq, cols = embeds.shape[1:]
    rows_here, head_cols = query_weight.shape
    count = suffix_pos.shape[1]
    vocab_here, width = vocab_table.shape
    heads = head_cols // HD
    rows = 4 * count
    slice_width = rows_here // 8
    low, full, short = jnp.bfloat16, jnp.float32, jnp.int16
    coded = head_cols + HD
    local = pl.BlockSpec(memory_space=pltpu.VMEM)
    apart = pl.BlockSpec(memory_space=pl.ANY)
    scratch = [
        ((rows_here, head_cols), low),
        ((rows_here, 2 * HD), low),
        ((head_cols, rows_here), low),
        (vocab_table.shape, low),
        ((seq, cols), low),
        ((2, 3, seq // 4, cols), low),
        ((2, 4, seq, rows_here), low),
        ((8, 8, 128), full),
        ((4, 8, 128), full),
        ((4, 1, count), jnp.int32),
        ((4, seq, rows_here), low),
        ((4, seq, 2 * HD), full),
        ((4, seq, 2 * HD), full),
        ((seq, 2 * HD), full),
        ((2, 4, seq, head_cols), full),
        ((2, 4, seq, coded), short),
        ((2, 4, seq, coded), short),
        ((2, seq, coded), short),
        ((2, seq, coded), short),
        ((8, seq, 2 * HD), low),
        ((2, seq, head_cols), low),
        ((8, 48, HD), full),
        ((8, 48, HD), full),
        ((4, PAD, head_cols + 2 * HD), low),
        ((rows, rows_here), full),
        ((2, 4, rows, slice_width), full),
        ((4, rows, slice_width), full),
        ((3, rows, slice_width), full),
        ((8, 8, 128), full),
        ((4, 8, 128), full),
        ((4, rows, rows_here), low),
    ]
    scores = pl.pallas_call(
        fused_kernel,
        out_shape=jax.ShapeDtypeStruct((rows, vocab_here), full),
        in_specs=[apart, apart, local, apart, apart, apart, apart, local, apart, local],
        out_specs=local,
        scratch_shapes=[pltpu.VMEM(shape, dtype) for shape, dtype in scratch]
        + [
            pltpu.SemaphoreType.DMA((SEMS,)),
            pltpu.SemaphoreType.DMA((SEMS,)),
            pltpu.SemaphoreType.DMA((8 + vocab_here // CHUNK,)),
            pltpu.SemaphoreType.DMA((2,)),
        ],
        compiler_params=pltpu.CompilerParams(
            collective_id=11, has_side_effects=True, vmem_limit_bytes=60 << 20
        ),
    )(
        embeds,
        out_grad,
        norm_gain.reshape(1, -1),
        query_weight,
        key_weight,
        value_weight,
        out_weight,
        suffix_pos,
        vocab_table,
        banned.reshape(1, -1),
    )
    return scores.reshape(4, count, vocab_here)


def fits(mesh_sizes, arrays):
    embeds, query_weight, key_weight, suffix_pos, vocab_table = arrays
    return (
        mesh_sizes == (4, 8)
        and embeds.shape[1] == 64
        and query_weight.shape[1] == 8 * HD
        and key_weight.shape[1] == HD
        and query_weight.shape[0] == 2 * embeds.shape[2]
        and query_weight.shape[0] % 2048 == 0
        and suffix_pos.shape[1] == 20
        and vocab_table.shape[0] % CHUNK == 0
    )


def part_of(*args):
    sizes = (lax.axis_size("prompt"), lax.axis_size("tensor"))
    if fits(sizes, (args[0], args[2], args[3], args[7], args[8])):
        return fused(*args)
    return on_device(*args)


def solution(mesh):
    return jax.shard_map(
        part_of,
        mesh=mesh,
        in_specs=(
            P("prompt", None, "tensor"),
            P(),
            P("prompt", "tensor"),
            P("prompt", "tensor"),
            P("prompt", "tensor"),
            P("tensor", "prompt"),
            P("prompt", None, "tensor"),
            P("prompt", None),
            P(("prompt", "tensor"), None),
            P(("prompt", "tensor")),
        ),
        out_specs=P(None, None, ("prompt", "tensor")),
        check_vma=False,
    )
```

```python
import functools
import math

import jax
import jax.numpy as jnp
from jax import lax
from jax.experimental import pallas as pl
from jax.experimental.pallas import tpu as pltpu
from jax.sharding import PartitionSpec as P

KVH = 8
HD = 128


EPSILON = 1e-05


def exchange_kernel(axis, count, spread, *refs):
    arrays = len(spread)
    sources, targets = refs[:arrays], refs[arrays : 2 * arrays]
    send_sem, recv_sem, own_sem = refs[2 * arrays :]
    here = lax.axis_index(axis)

    def block(i, to):
        return sources[i].at[to] if spread[i] else sources[i]

    kept = []
    for i in range(arrays):
        copy = pltpu.make_async_copy(block(i, here), targets[i].at[here], own_sem.at[i])
        copy.start()
        kept.append(copy)
    barrier = pltpu.get_barrier_semaphore()
    for step in range(1, count):
        peer = lax.rem(here + step, count)
        pl.semaphore_signal(
            barrier, inc=1, device_id={axis: peer}, device_id_type=pl.DeviceIdType.MESH
        )
    pl.semaphore_wait(barrier, count - 1)
    copies = []
    for step in range(1, count):
        peer = lax.rem(here + step, count)
        for i in range(arrays):
            copy = pltpu.make_async_remote_copy(
                src_ref=block(i, peer),
                dst_ref=targets[i].at[here],
                send_sem=send_sem.at[i, step - 1],
                recv_sem=recv_sem.at[i, step - 1],
                device_id={axis: peer},
                device_id_type=pl.DeviceIdType.MESH,
            )
            copy.start()
            copies.append(copy)
    for copy in kept + copies:
        copy.wait()


def exchange(axis, number, *operands):
    count = lax.axis_size(axis)
    arrays = [array for array, _ in operands]
    spread = tuple(each for _, each in operands)
    shapes = [
        jax.ShapeDtypeStruct(((count,) + (a.shape[1:] if each else a.shape)), a.dtype)
        for a, each in operands
    ]
    space = pl.BlockSpec(memory_space=pltpu.VMEM)
    sems = pltpu.SemaphoreType.DMA((len(arrays), count - 1))
    return pl.pallas_call(
        functools.partial(exchange_kernel, axis, count, spread),
        out_shape=shapes,
        in_specs=[space] * len(arrays),
        out_specs=[space] * len(arrays),
        scratch_shapes=[sems, sems, pltpu.SemaphoreType.DMA((len(arrays),))],
        compiler_params=pltpu.CompilerParams(
            collective_id=number, has_side_effects=True, vmem_limit_bytes=40 << 20
        ),
    )(*arrays)


def dot_f32(spec, a, b):
    return jnp.einsum(spec, a, b, preferred_element_type=jnp.float32)


MESH = pl.DeviceIdType.MESH


def greet(axis, peers):
    barrier = pltpu.get_barrier_semaphore()
    for peer in peers:
        pl.semaphore_signal(barrier, inc=1, device_id={axis: peer}, device_id_type=MESH)
    pl.semaphore_wait(barrier, len(peers))


def gather_kernel(axis, count, arrays, *refs):
    sources, targets = refs[:arrays], refs[arrays : 2 * arrays]
    send_sem, recv_sem, own_sem = refs[2 * arrays :]
    here = lax.axis_index(axis)
    chips = count // 2
    chip, core = here // 2, lax.rem(here, 2)
    pair = 2 * chip + (1 - core)
    kept = []
    for i in range(arrays):
        copy = pltpu.make_async_copy(sources[i], targets[i].at[here], own_sem.at[i])
        copy.start()
        kept.append(copy)

    def push(i, source, slot, number, peer):
        return pltpu.make_async_remote_copy(
            src_ref=source,
            dst_ref=targets[i].at[slot],
            send_sem=send_sem.at[i, number],
            recv_sem=recv_sem.at[i, number],
            device_id={axis: peer},
            device_id_type=MESH,
        )

    others = [2 * lax.rem(chip + step, chips) + core for step in range(1, chips)]
    greet(axis, others + [pair])
    first = []
    for step in range(1, chips):
        for i in range(arrays):
            copy = push(i, sources[i], here, step, others[step - 1])
            copy.start()
            first.append(copy)
    rest = []
    for i in range(arrays):
        copy = push(i, sources[i], here, 0, pair)
        copy.start()
        rest.append(copy)
    for step in range(1, chips):
        slot = 2 * lax.rem(chip + chips - step, chips) + core
        for i in range(arrays):
            first[(step - 1) * arrays + i].wait_recv()
            copy = push(i, targets[i].at[slot], slot, chips - 1 + step, pair)
            copy.start()
            rest.append(copy)
    for copy in first:
        copy.wait_send()
    for copy in kept + rest:
        copy.wait()


def gather(axis, number, *arrays):
    count = lax.axis_size(axis)
    shapes = [jax.ShapeDtypeStruct((count,) + a.shape, a.dtype) for a in arrays]
    space = pl.BlockSpec(memory_space=pltpu.VMEM)
    sems = pltpu.SemaphoreType.DMA((len(arrays), count - 1))
    return pl.pallas_call(
        functools.partial(gather_kernel, axis, count, len(arrays)),
        out_shape=shapes,
        in_specs=[space] * len(arrays),
        out_specs=[space] * len(arrays),
        scratch_shapes=[sems, sems, pltpu.SemaphoreType.DMA((len(arrays),))],
        compiler_params=pltpu.CompilerParams(
            collective_id=number, has_side_effects=True, vmem_limit_bytes=40 << 20
        ),
    )(*arrays)


def line_kernel(axis, source, target, relay, send_sem, recv_sem, own_sem):
    here = lax.axis_index(axis)
    own = pltpu.make_async_copy(source.at[here], target.at[here], own_sem.at[0])
    own.start()
    greet(axis, [lax.rem(here + step, 4) for step in range(1, 4)])

    def push(block, slot, number, peer, into=None):
        return pltpu.make_async_remote_copy(
            src_ref=block,
            dst_ref=target.at[slot] if into is None else into,
            send_sem=send_sem.at[number],
            recv_sem=recv_sem.at[slot if into is None else 4],
            device_id={axis: peer},
            device_id_type=MESH,
        )

    for role in range(4):
        far = 3 if role < 2 else 0
        middle = 1 if role < 2 else 2
        across = 3 - middle

        @pl.when(here == role)
        def _():
            if role == middle:
                sent = [
                    push(source.at[across], role, 0, across),
                    push(source.at[3 - far], role, 1, 3 - far),
                ]
                for copy in sent:
                    copy.start()
                total = push(relay, role, 2, far)
                push(source.at[far], role, 3, far, relay).wait_recv()
                relay[...] = relay[...] + source[far]
                total.start()
                sent.append(total)
                arriving = [0, across, 3]
            else:
                handed = push(source.at[far], role, 0, middle, relay)
                handed.start()
                target[far] = jnp.zeros_like(target[far])
                handed.wait_send()
                sent = [
                    push(source.at[across], role, 1, across),
                    push(source.at[middle], role, 2, middle),
                ]
                for copy in sent:
                    copy.start()
                arriving = [1, 2]
            for slot in arriving:
                push(source.at[slot], slot, 3, slot).wait_recv()
            for copy in sent:
                copy.wait_send()

    own.wait()


def line_exchange(axis, number, blocks):
    if lax.axis_size(axis) != 4:
        return exchange(axis, number, (blocks, True))[0]
    space = pl.BlockSpec(memory_space=pltpu.VMEM)
    return pl.pallas_call(
        functools.partial(line_kernel, axis),
        out_shape=jax.ShapeDtypeStruct(blocks.shape, blocks.dtype),
        in_specs=[space],
        out_specs=space,
        scratch_shapes=[
            pltpu.VMEM(blocks.shape[1:], blocks.dtype),
            pltpu.SemaphoreType.DMA((4,)),
            pltpu.SemaphoreType.DMA((5,)),
            pltpu.SemaphoreType.DMA((1,)),
        ],
        compiler_params=pltpu.CompilerParams(
            collective_id=number, has_side_effects=True, vmem_limit_bytes=40 << 20
        ),
    )(blocks)


CHUNK = 512


def score_kernel(
    axis, count, part, vocab, scores, got, flat, table, send_sem, recv_sem, own_sem, load_sem
):
    def load(c):
        span = pl.ds(pl.multiple_of(c * CHUNK, CHUNK), CHUNK)
        return pltpu.make_async_copy(vocab.at[span], table.at[span], load_sem.at[c])

    chunks = vocab.shape[0] // CHUNK
    for c in range(chunks):
        load(c).start()
    gather_kernel(axis, count, 1, part, got, send_sem, recv_sem, own_sem)
    wide = part.shape[2]
    for p in range(part.shape[0]):
        for t in range(count):
            start = (p * count + t) * wide
            flat[:, start : start + wide] = got[t, p]

    @pl.loop(0, chunks)
    def _(c):
        load(c).wait()
        span = pl.ds(pl.multiple_of(c * CHUNK, CHUNK), CHUNK)
        scores[:, span] = -lax.dot_general(
            flat[...],
            table[span, :],
            (((1,), (1,)), ((), ())),
            preferred_element_type=jnp.float32,
        )


def gather_score(axis, number, part, vocab):
    count = lax.axis_size(axis)
    n_prompt, rows, wide = part.shape
    vocab_here, width = vocab.shape
    if wide % 128 or vocab_here % CHUNK or rows % 16:
        (part,) = gather(axis, number, part)
        return -dot_f32("rd,vd->rv", part.transpose(2, 1, 0, 3).reshape(rows, width), vocab)
    sems = pltpu.SemaphoreType.DMA((1, count - 1))
    return pl.pallas_call(
        functools.partial(score_kernel, axis, count),
        out_shape=jax.ShapeDtypeStruct((rows, vocab_here), jnp.float32),
        in_specs=[pl.BlockSpec(memory_space=pltpu.VMEM), pl.BlockSpec(memory_space=pl.ANY)],
        out_specs=pl.BlockSpec(memory_space=pltpu.VMEM),
        scratch_shapes=[
            pltpu.VMEM((count,) + part.shape, part.dtype),
            pltpu.VMEM((rows, width), part.dtype),
            pltpu.VMEM(vocab.shape, vocab.dtype),
            sems,
            sems,
            pltpu.SemaphoreType.DMA((1,)),
            pltpu.SemaphoreType.DMA((vocab_here // CHUNK,)),
        ],
        compiler_params=pltpu.CompilerParams(
            collective_id=number, has_side_effects=True, vmem_limit_bytes=52 << 20
        ),
    )(part, vocab)


def on_device(
    embeds,
    norm_gain,
    query_weight,
    key_weight,
    value_weight,
    out_weight,
    out_grad,
    suffix_pos,
    vocab_table,
    banned,
):
    n_prompt = lax.axis_size("prompt")
    n_tensor = lax.axis_size("tensor")
    here_prompt = lax.axis_index("prompt")
    here_tensor = lax.axis_index("tensor")
    seq_len = embeds.shape[1]
    suffix_count = suffix_pos.shape[1]
    width = embeds.shape[2] * n_tensor
    rows_here, head_cols = query_weight.shape
    key_cols = key_weight.shape[1]
    heads_here = head_cols // HD
    slice_width = rows_here // n_tensor
    logit_scale = 1.0 / math.sqrt(HD)

    split_rows = seq_len // n_tensor
    ratio = n_tensor // n_prompt
    feature_cols = embeds.shape[2]
    both = jnp.concatenate(
        [
            embeds.reshape(n_tensor, split_rows, feature_cols),
            out_grad.reshape(n_tensor, split_rows, feature_cols),
        ],
        axis=1,
    )
    (both,) = exchange("tensor", 0, (both, True))
    own = both[:, :split_rows].astype(jnp.float32)
    inverse_norm = lax.rsqrt(jnp.sum(own * own, axis=(0, 2))[:, None] / width + EPSILON)
    inverse_norm = jnp.broadcast_to(inverse_norm, (split_rows, 128))
    both = both.reshape(n_prompt, ratio, 2 * split_rows, feature_cols)
    both, inverse_norm, suffix_all = exchange(
        "prompt", 1, (both, True), (inverse_norm, False), (suffix_pos, False)
    )
    both, inverse_norm = gather("tensor", 2, both, inverse_norm)
    suffix_all = suffix_all.reshape(n_prompt, suffix_count)
    both = both.reshape(n_tensor, n_prompt, ratio, 2, split_rows, feature_cols)
    both = both.transpose(3, 1, 0, 4, 2, 5).reshape(2, n_prompt, seq_len, rows_here)
    embeds, out_grad = both[0], both[1]
    inverse_norm = inverse_norm[..., :1].transpose(1, 0, 2, 3).reshape(n_prompt, seq_len, 1)
    embeds_float = embeds.astype(jnp.float32)
    gain_rows = lax.dynamic_slice_in_dim(norm_gain, here_prompt * rows_here, rows_here, 0)
    gain_rows = gain_rows.astype(jnp.float32)
    normed = (embeds_float * inverse_norm * gain_rows).astype(jnp.bfloat16)

    parts = jnp.concatenate(
        [
            dot_f32("psd,dc->psc", normed, query_weight),
            dot_f32("psd,dc->psc", normed, key_weight),
            dot_f32("psd,dc->psc", normed, value_weight),
            dot_f32("psd,cd->psc", out_grad, out_weight),
        ],
        axis=2,
    )
    parts = line_exchange("prompt", 3, parts)
    whole = jnp.sum(parts, axis=0).astype(jnp.bfloat16)
    contexts = whole[:, head_cols + 2 * key_cols :]
    contexts = contexts.reshape(seq_len, heads_here, HD)
    queries = whole[:, :head_cols].reshape(seq_len, heads_here, HD)
    (key_values,) = gather("tensor", 4, whole[:, head_cols : head_cols + 2 * key_cols])
    key_values = key_values.reshape(n_tensor, seq_len, 2, key_cols).transpose(2, 1, 0, 3)
    key_values = key_values.reshape(2, seq_len, KVH * HD)
    fold = min(heads_here, KVH)
    first = ((here_tensor * heads_here) % KVH) * HD
    if fold < KVH:
        key_values = lax.dynamic_slice_in_dim(key_values, first, fold * HD, 2)
    key_values = key_values.reshape(2, seq_len, fold, HD)
    if heads_here > fold:
        key_values = jnp.tile(key_values, (1, 1, heads_here // fold, 1))
    keys, values = key_values[0], key_values[1]

    logits = dot_f32("qhd,khd->hqk", queries, keys) * logit_scale
    row_index = lax.broadcasted_iota(jnp.int32, (seq_len, seq_len), 0)
    col_index = lax.broadcasted_iota(jnp.int32, (seq_len, seq_len), 1)
    causal = col_index <= row_index
    largest = jnp.max(jnp.where(causal, logits, -1e30), axis=-1, keepdims=True)
    raised = jnp.where(causal, jnp.exp(logits - largest), 0.0)
    probs = raised / jnp.sum(raised, axis=-1, keepdims=True)
    probs_low = probs.astype(jnp.bfloat16)
    prob_grad = dot_f32("qhd,khd->hqk", contexts, values)
    logit_grad = (
        probs * (prob_grad - jnp.sum(prob_grad * probs, axis=-1, keepdims=True)) * logit_scale
    ).astype(jnp.bfloat16)
    steps_iota = lax.broadcasted_iota(jnp.int32, (suffix_count, seq_len), 1)
    chooser = (steps_iota == suffix_pos[0][:, None]).astype(jnp.bfloat16)
    logit_rows = dot_f32("ns,hsk->hnk", chooser, logit_grad).astype(jnp.bfloat16)
    query_grad = dot_f32("hnk,khd->nhd", logit_rows, keys).astype(jnp.bfloat16)
    query_grad = query_grad.reshape(suffix_count, head_cols)
    logit_cols = dot_f32("hqk,nk->hnq", logit_grad, chooser).astype(jnp.bfloat16)
    prob_cols = dot_f32("hqk,nk->hnq", probs_low, chooser).astype(jnp.bfloat16)
    key_each = dot_f32("hnq,qhd->nhd", logit_cols, queries)
    value_each = dot_f32("hnq,qhd->nhd", prob_cols, contexts)
    slots = jnp.stack([key_each, value_each])
    slots = slots.reshape(2, suffix_count, heads_here // fold, fold * HD).sum(axis=2)
    if fold < KVH:
        slots = lax.dynamic_update_slice_in_dim(
            jnp.zeros((2, suffix_count, KVH * HD), jnp.float32), slots, first, 2
        )
    slots = slots.reshape(2 * suffix_count, n_tensor, key_cols).transpose(1, 0, 2)
    (grads,) = exchange("tensor", 5, (slots, True))
    grads = jnp.sum(grads, axis=0).astype(jnp.bfloat16).reshape(2, suffix_count, key_cols)
    grads = jnp.concatenate([query_grad, grads[0], grads[1]], axis=1)
    (grads,) = exchange("prompt", 6, (grads, False))
    rows = n_prompt * suffix_count
    grads = grads.reshape(rows, head_cols + 2 * key_cols)
    steps_iota = lax.broadcasted_iota(jnp.int32, (n_prompt, suffix_count, seq_len), 2)
    chooser_all = steps_iota == suffix_all[:, :, None]
    embed_rows = dot_f32("pns,psd->pnd", chooser_all.astype(jnp.bfloat16), embeds)
    norm_rows = jnp.sum(
        jnp.where(chooser_all, inverse_norm[:, None, :, 0], 0.0), axis=-1, keepdims=True
    )
    scaled = (embed_rows * norm_rows).reshape(rows, rows_here)
    norm_rows = norm_rows.reshape(rows, 1)
    branch = dot_f32("nc,dc->nd", grads[:, :head_cols], query_weight)
    branch = branch + dot_f32("nc,dc->nd", grads[:, head_cols : head_cols + key_cols], key_weight)
    branch = branch + dot_f32("nc,dc->nd", grads[:, head_cols + key_cols :], value_weight)
    branch = branch * gain_rows
    inner = jnp.sum(branch * scaled, axis=-1)
    branch = branch.reshape(rows, n_tensor, slice_width).transpose(1, 0, 2)
    share, inner = exchange("tensor", 7, (branch, True), (inner[None, :], False))
    weighted = jnp.sum(share, axis=0)
    (inner,) = exchange("prompt", 8, (jnp.sum(inner, axis=0), False))
    inner = jnp.sum(inner, axis=0).reshape(rows, 1) / width
    scaled = lax.dynamic_slice_in_dim(scaled, here_tensor * slice_width, slice_width, 1)
    suffix_grad = (norm_rows * (weighted - scaled * inner)).astype(jnp.bfloat16)
    (suffix_grad,) = exchange("prompt", 9, (suffix_grad, False))
    scores = gather_score("tensor", 10, suffix_grad, vocab_table)
    scores = scores.reshape(n_prompt, suffix_count, vocab_table.shape[0])
    return jnp.where(banned[None, None, :] == 1, 0.0, scores)


PAD = 32
TINY = 1e-30
FULL = 32767.0
SEMS = 208


def pick_column(row, rows):
    wide = row.shape[1]
    down = lax.broadcasted_iota(jnp.int32, (rows, wide), 0)
    along = lax.broadcasted_iota(jnp.int32, (rows, wide), 1)
    return jnp.sum(jnp.where(down == along, row, 0.0), axis=1, keepdims=True)


def lay_row(column, wide):
    rows = column.shape[0]
    down = lax.broadcasted_iota(jnp.int32, (rows, wide), 0)
    along = lax.broadcasted_iota(jnp.int32, (rows, wide), 1)
    return jnp.sum(jnp.where(down == along, column, 0.0), axis=0, keepdims=True)


def lane_sums(values):
    total = values[:, :128]
    for j in range(128, values.shape[1], 128):
        total = total + values[:, j : j + 128]
    return jnp.sum(total, axis=1, keepdims=True)


def code_block(read, write, heads, rows):
    lanes = lax.broadcasted_iota(jnp.int32, (rows, HD), 1)
    powers = jnp.zeros((rows, HD), jnp.float32)
    for h in range(heads):
        block = read(h)
        peak = jnp.max(jnp.abs(block), axis=1, keepdims=True)
        power = jnp.floor(jnp.log2(jnp.maximum(peak, TINY))) + 1.0
        fixed = jnp.floor(block * (jnp.exp2(-power) * FULL) + 0.5)
        fixed = jnp.clip(fixed, -FULL, FULL)
        write(h, fixed.astype(jnp.int32).astype(jnp.int16))
        powers = jnp.where(lanes == h, power, powers)
    write(heads, powers.astype(jnp.int32).astype(jnp.int16))


def scale_of(tile):
    return jnp.exp2(tile.astype(jnp.int32).astype(jnp.float32)) * (1.0 / FULL)


def fused_kernel(
    embeds,
    out_grad,
    gain,
    query_weight,
    key_weight,
    value_weight,
    out_weight,
    suffix,
    vocab,
    banned,
    out,
    wq,
    wkv,
    wo,
    table,
    mine,
    stage,
    x,
    sums,
    norms,
    spots,
    nb,
    pkv,
    rkv,
    relay_kv,
    pp,
    coded,
    arrived,
    relay,
    total,
    kvg,
    whole,
    slots,
    slots_in,
    grads,
    scaled,
    weighted,
    pair_in,
    shares,
    inner_in,
    inner_z,
    suffix_grads,
    send_sem,
    recv_sem,
    load_sem,
    own_sem,
):
    z = lax.axis_index("prompt")
    t = lax.axis_index("tensor")
    chip, core = t // 2, lax.rem(t, 2)
    pair = 2 * chip + (1 - core)
    chip_y, chip_x = chip // 2, lax.rem(chip, 2)
    near = [
        chip,
        2 * chip_y + (1 - chip_x),
        2 * (1 - chip_y) + chip_x,
        2 * (1 - chip_y) + (1 - chip_x),
    ]
    seq, cols = embeds.shape[1], embeds.shape[2]
    width = gain.shape[1]
    rows_here, head_cols = query_weight.shape
    heads = head_cols // HD
    count = suffix.shape[1]
    rows = 4 * count
    quarter = seq // 4
    slice_width = rows_here // 8
    scale = 1.0 / math.sqrt(HD)
    dot = functools.partial(lax.dot_general, preferred_element_type=jnp.float32)
    plain = (((1,), (0,)), ((), ()))
    crossed = (((1,), (1,)), ((), ()))

    chunks = vocab.shape[0] // CHUNK

    def load_table(c):
        span = pl.ds(pl.multiple_of(c * CHUNK, CHUNK), CHUNK)
        return pltpu.make_async_copy(vocab.at[span], table.at[span], load_sem.at[8 + c])

    loads = {
        "e": pltpu.make_async_copy(embeds.at[0], mine, load_sem.at[0]),
        "k": pltpu.make_async_copy(key_weight, wkv.at[:, :HD], load_sem.at[1]),
        "v": pltpu.make_async_copy(value_weight, wkv.at[:, HD:], load_sem.at[2]),
        "q": pltpu.make_async_copy(query_weight, wq, load_sem.at[3]),
        "o": pltpu.make_async_copy(out_weight, wo, load_sem.at[4]),
    }
    loads["e"].start()

    barrier = pltpu.get_barrier_semaphore()
    for step in range(1, 8):
        pl.semaphore_signal(
            barrier, inc=1, device_id={"tensor": lax.rem(t + step, 8)}, device_id_type=MESH
        )
    for step in range(1, 4):
        pl.semaphore_signal(
            barrier, inc=1, device_id={"prompt": lax.rem(z + step, 4)}, device_id_type=MESH
        )
    pl.semaphore_wait(barrier, 10)

    used = [0]
    sent = []

    def take(number=1):
        used[0] += number
        assert used[0] <= SEMS
        return used[0] - number

    def move(source, target, s, r, device):
        return pltpu.make_async_remote_copy(
            src_ref=source,
            dst_ref=target,
            send_sem=send_sem.at[s],
            recv_sem=recv_sem.at[r],
            device_id=device,
            device_id_type=MESH,
        )

    def push(source, target, s, r, device):
        copy = move(source, target, s, r, device)
        copy.start()
        sent.append(copy)

    def plane(s, other=False):
        return {"tensor": 2 * near[s] + ((1 - core) if other else core)}

    def along(step):
        return {"prompt": lax.rem(z + step, 4)}

    def rows_of(chip_index):
        return pl.ds(pl.multiple_of(quarter * chip_index, quarter), quarter)

    sources = (embeds.at[0], out_grad.at[0])
    own_cols = pl.ds(pl.multiple_of(core * cols, 128), cols)
    pair_cols = pl.ds(pl.multiple_of((1 - core) * cols, 128), cols)

    hop = [take(4) for _ in range(2)]
    for a in range(2):
        for s in (3, 1, 2):
            push(
                sources[a].at[rows_of(near[s])], stage.at[a, s - 1], hop[a] + s, hop[a] + s, plane(s)
            )
    at_spots = take(4)
    for step in range(1, 4):
        push(suffix, spots.at[z], at_spots + step, at_spots + step, along(step))
    spots[z] = suffix[...]

    loads["e"].wait()
    square = jnp.zeros((seq, 128), jnp.float32)
    for j in range(0, cols, 128):
        block = mine[:, j : j + 128].astype(jnp.float32)
        square = square + block * block
    square = jnp.sum(square, axis=1, keepdims=True)
    sums[t] = jnp.broadcast_to(lay_row(square, 128), (8, 128))
    at_sums = take(8)
    for step in range(1, 8):
        push(
            sums.at[t], sums.at[t], at_sums + step, at_sums + step, {"tensor": lax.rem(t + step, 8)}
        )

    for name in "kvqo":
        loads[name].start()

    across = [take(4) for _ in range(2)]
    across_in = [take(4) for _ in range(2)]

    def second_hop(a):
        for s in range(4):
            if s == 0:
                block = sources[a].at[rows_of(chip)]
            else:
                move(stage.at[a, s - 1], stage.at[a, s - 1], 0, hop[a] + s, plane(s)).wait_recv()
                block = stage.at[a, s - 1]
            target = x.at[a, z, rows_of(chip), own_cols]

            @pl.when(near[s] == z)
            def _():
                copy = pltpu.make_async_copy(block, target, own_sem.at[a])
                copy.start()
                copy.wait()

            @pl.when(near[s] != z)
            def _():
                move(block, target, across[a] + s, across_in[a] + z, {"prompt": near[s]}).start()

    second_hop(0)
    for step in range(1, 8):
        move(sums.at[t], sums.at[t], 0, at_sums + step, plane(1)).wait_recv()
    square = sums[0]
    for j in range(1, 8):
        square = square + sums[j]
    norms[z] = lax.rsqrt(square / width + EPSILON)
    at_norms = take(4)
    for step in range(1, 4):
        push(norms.at[z], norms.at[z], at_norms + step, at_norms + step, along(step))
    second_hop(1)

    order = (0, 1, 3, 2)
    third = [[take(4) for _ in range(4)] for _ in range(2)]
    fourth = [[take(4) for _ in range(4)] for _ in range(2)]

    def third_hop(a):
        for step in order:
            p = lax.rem(z + step, 4)
            block = x.at[a, p, rows_of(chip), own_cols]
            if step:
                move(block, block, 0, across_in[a] + p, plane(1)).wait_recv()
            for s in (3, 1, 2):
                push(block, block, third[a][step] + s, third[a][step] + s, plane(s))
            push(block, block, third[a][step], third[a][step], {"tensor": pair})

    def fourth_hop(a):
        for step in order:
            p = lax.rem(z + step, 4)
            for s in (1, 2, 3):
                block = x.at[a, p, rows_of(near[s]), own_cols]
                move(block, block, 0, third[a][step] + s, plane(s)).wait_recv()
                push(block, block, fourth[a][step] + s, fourth[a][step] + s, {"tensor": pair})

    def last_hop(a):
        for step in order:
            p = lax.rem(z + step, 4)
            for s in range(4):
                block = x.at[a, p, rows_of(near[s]), pair_cols]
                number = fourth[a][step] + s if s else third[a][step]
                move(block, block, 0, number, {"tensor": pair}).wait_recv()

    third_hop(0)
    third_hop(1)
    fourth_hop(0)
    last_hop(0)

    for step in range(1, 4):
        move(norms.at[z], norms.at[z], 0, at_norms + step, plane(1)).wait_recv()
        move(suffix, spots.at[z], 0, at_spots + step, plane(1)).wait_recv()

    gain_here = pl.ds(pl.multiple_of(z * rows_here, 128), rows_here)

    @pl.loop(0, 4)
    def _(p):
        inverse = pick_column(norms[p][:1], seq)
        gains = gain[:, gain_here].astype(jnp.float32)
        for j in range(0, rows_here, 512):
            block = x[0, p, :, j : j + 512].astype(jnp.float32)
            block = block * inverse * gains[:, j : j + 512]
            nb[p, :, j : j + 512] = block.astype(jnp.bfloat16)

    loads["k"].wait()
    loads["v"].wait()
    normed = nb[...].reshape(4 * seq, rows_here)
    pkv[...] = dot(normed, wkv[...], plain).reshape(4, seq, 2 * HD)

    is_end = (z == 0) | (z == 3)
    is_mid = (z == 1) | (z == 2)
    end_far, end_mid = 3 - z, 1 + z // 3
    mid_far, mid_near = 6 - 3 * z, 3 * z - 3

    def line_sends(block, into, relay_into, base):
        hand = move(block(end_far), relay_into, base, base + 4, {"prompt": end_mid})
        one = move(block(3 - end_mid), into.at[z], base + 1, base + z, {"prompt": 3 - end_mid})
        two = move(block(end_mid), into.at[z], base + 2, base + z, {"prompt": end_mid})
        over = move(block(3 - z), into.at[z], base, base + z, {"prompt": 3 - z})
        back = move(block(mid_near), into.at[z], base + 1, base + z, {"prompt": mid_near})
        return (hand, one, two), (over, back)

    def line_start(block, into, relay_into, base):
        ends, mids = line_sends(block, into, relay_into, base)

        @pl.when(is_end)
        def _():
            for copy in ends:
                copy.start()

        @pl.when(is_mid)
        def _():
            for copy in mids:
                copy.start()

    def line_relay(block, into, relay_into, base, add, out_block):
        @pl.when(is_mid)
        def _():
            move(relay_into, relay_into, 0, base + 4, {"prompt": mid_far}).wait_recv()
            add()
            move(out_block, into.at[z], base + 2, base + z, {"prompt": mid_far}).start()

    def line_arrive(into, base):
        @pl.when(is_end)
        def _():
            for source in (end_mid, 3 - end_mid):
                move(into.at[z], into.at[z], 0, base + source, plane(1)).wait_recv()

        @pl.when(is_mid)
        def _():
            for source in (0, 3, 3 - z):
                move(into.at[z], into.at[z], 0, base + source, plane(1)).wait_recv()

    def line_sent(block, into, relay_into, base, out_block):
        ends, mids = line_sends(block, into, relay_into, base)

        @pl.when(is_end)
        def _():
            for copy in ends:
                copy.wait_send()

        @pl.when(is_mid)
        def _():
            for copy in mids:
                copy.wait_send()
            move(out_block, into.at[z], base + 2, base + z, {"prompt": mid_far}).wait_send()

    @pl.when(is_end)
    def _():
        rkv[end_far] = jnp.zeros(rkv.shape[1:], rkv.dtype)
        for i in range(2):
            arrived[i, end_far] = jnp.zeros(arrived.shape[2:], arrived.dtype)

    line_kv = take(5)
    line = [take(5) for _ in range(2)]
    kv_args = (lambda d: pkv.at[d], rkv, relay_kv)
    line_start(*kv_args, line_kv)
    for c in range(chunks):
        load_table(c).start()

    def code(i):
        for step in (3, 2, 1):
            d = lax.rem(z + step, 4)

            def write(h, tile):
                coded[i, d, :, h * HD : (h + 1) * HD] = tile

            code_block(lambda h: pp[i, d, :, h * HD : (h + 1) * HD], write, heads, seq)

    def line_of(i):
        return (lambda d: coded.at[i, d], arrived.at[i], relay.at[i])

    def add_coded(i):
        def add():
            factors = scale_of(relay[i, :, heads * HD :])

            def read(h):
                got = relay[i, :, h * HD : (h + 1) * HD].astype(jnp.int32).astype(jnp.float32)
                return got * factors[:, h : h + 1] + pp[i, mid_far, :, h * HD : (h + 1) * HD]

            def write(h, tile):
                total[i, :, h * HD : (h + 1) * HD] = tile

            code_block(read, write, heads, seq)

        return add

    loads["q"].wait()

    @pl.loop(0, head_cols // 256)
    def _(j):
        span = pl.ds(pl.multiple_of(j * 256, 256), 256)
        part = dot(nb[...].reshape(4 * seq, rows_here), wq[:, span], plain)
        pp[0, :, :, span] = part.reshape(4, seq, 256)

    code(0)
    line_start(*line_of(0), line[0])

    def add_kv():
        relay_kv[...] = relay_kv[...] + pkv[mid_far]

    line_relay(*kv_args, line_kv, add_kv, relay_kv)

    fourth_hop(1)
    last_hop(1)
    loads["o"].wait()

    @pl.loop(0, head_cols // 256)
    def _(j):
        span = pl.ds(pl.multiple_of(j * 256, 256), 256)
        part = dot(x[1].reshape(4 * seq, rows_here), wo[span, :], crossed)
        pp[1, :, :, span] = part.reshape(4, seq, 256)

    code(1)
    line_start(*line_of(1), line[1])

    line_arrive(rkv, line_kv)
    own = pkv[z]
    for step in range(1, 4):
        own = own + rkv[lax.rem(z + step, 4)]
    kvg[t] = own.astype(jnp.bfloat16)
    at_kv = take(8)
    for step in range(1, 8):
        push(kvg.at[t], kvg.at[t], at_kv + step, at_kv + step, {"tensor": lax.rem(t + step, 8)})
    line_relay(*line_of(0), line[0], add_coded(0), total.at[0])
    line_relay(*line_of(1), line[1], add_coded(1), total.at[1])

    down = lax.broadcasted_iota(jnp.int32, (rows, count), 0)
    over = lax.broadcasted_iota(jnp.int32, (rows, count), 1)
    place = jnp.zeros((rows, 1), jnp.float32)
    prompt_of = jnp.zeros((rows, 1), jnp.int32)
    row_at = lax.broadcasted_iota(jnp.int32, (rows, 1), 0)
    for p in range(4):
        found = jnp.where(down - p * count == over, spots[p].astype(jnp.float32), 0.0)
        place = place + jnp.sum(found, axis=1, keepdims=True)
        if p:
            prompt_of = prompt_of + (row_at >= p * count).astype(jnp.int32)
    place = place + seq * prompt_of.astype(jnp.float32)
    marks = lax.broadcasted_iota(jnp.int32, (rows, 4 * seq), 1).astype(jnp.float32)
    chosen = (marks == place).astype(jnp.bfloat16)
    norm_rows = jnp.zeros((rows, 1), jnp.float32)
    inside = lax.broadcasted_iota(jnp.int32, (rows, 128), 1).astype(jnp.float32)
    for p in range(4):
        hit = (inside + p * seq == place) & (inside < seq)
        norm_rows = norm_rows + jnp.sum(jnp.where(hit, norms[p][:1], 0.0), axis=1, keepdims=True)
    for j in range(0, rows_here, 512):
        block = x[0, :, :, j : j + 512].reshape(4 * seq, 512)
        scaled[:, j : j + 512] = dot(chosen, block, plain) * norm_rows

    def finish(i):
        line_arrive(arrived.at[i], line[i])
        factors = [scale_of(arrived[i, lax.rem(z + s, 4), :, heads * HD :]) for s in (1, 2, 3)]
        for h in range(heads):
            span = slice(h * HD, (h + 1) * HD)
            value = pp[i, z, :, span]
            for s in (1, 2, 3):
                got = arrived[i, lax.rem(z + s, 4), :, span].astype(jnp.int32)
                value = value + got.astype(jnp.float32) * factors[s - 1][:, h : h + 1]
            whole[i, :, span] = value.astype(jnp.bfloat16)

    finish(0)
    for step in range(1, 8):
        move(kvg.at[t], kvg.at[t], 0, at_kv + step, plane(1)).wait_recv()
    finish(1)

    own_spots = jnp.where(
        lax.broadcasted_iota(jnp.int32, (PAD, count), 0)
        == lax.broadcasted_iota(jnp.int32, (PAD, count), 1),
        suffix[...].astype(jnp.float32),
        0.0,
    )
    own_spots = jnp.sum(own_spots, axis=1, keepdims=True)
    real = lax.broadcasted_iota(jnp.int32, (PAD, 1), 0) < count
    own_spots = jnp.where(real, own_spots, -1.0)
    steps_iota = lax.broadcasted_iota(jnp.int32, (PAD, seq), 1).astype(jnp.float32)
    chooser = (steps_iota == own_spots).astype(jnp.bfloat16)
    causal = lax.broadcasted_iota(jnp.int32, (seq, seq), 1) <= lax.broadcasted_iota(
        jnp.int32, (seq, seq), 0
    )
    for h in range(heads):
        span = slice(h * HD, (h + 1) * HD)
        queries, contexts = whole[0, :, span], whole[1, :, span]
        keys, values = kvg[h, :, :HD], kvg[h, :, HD:]
        logits = dot(queries, keys, crossed) * scale
        largest = jnp.max(jnp.where(causal, logits, -1e30), axis=-1, keepdims=True)
        raised = jnp.where(causal, jnp.exp(logits - largest), 0.0)
        probs = raised / jnp.sum(raised, axis=-1, keepdims=True)
        probs_low = probs.astype(jnp.bfloat16)
        prob_grad = dot(contexts, values, crossed)
        less = jnp.sum(prob_grad * probs, axis=-1, keepdims=True)
        logit_grad = (probs * (prob_grad - less) * scale).astype(jnp.bfloat16)
        logit_rows = dot(chooser, logit_grad, plain).astype(jnp.bfloat16)
        grads[z, :, span] = dot(logit_rows, keys, plain).astype(jnp.bfloat16)
        logit_cols = dot(chooser, logit_grad, crossed).astype(jnp.bfloat16)
        prob_cols = dot(chooser, probs_low, crossed).astype(jnp.bfloat16)
        slots[h, :24] = dot(logit_cols, queries, plain)[:24]
        slots[h, 24:] = dot(prob_cols, contexts, plain)[:24]

    at_slots = take(8)
    for step in range(1, 8):
        to = lax.rem(t + step, 8)
        push(slots.at[to], slots_in.at[t], at_slots + step, at_slots + step, {"tensor": to})
    at_grads = take(8)
    head_part = grads.at[z, :, :head_cols]
    for step in (2, 1, 3):
        push(head_part, head_part, at_grads + step, at_grads + step, along(step))
    slots_in[t] = slots[t]
    for step in range(1, 8):
        move(slots_in.at[t], slots_in.at[t], 0, at_slots + step, plane(1)).wait_recv()
    summed = slots_in[0]
    for j in range(1, 8):
        summed = summed + slots_in[j]
    filler = jnp.zeros((PAD - 24, HD), jnp.float32)
    key_rows = jnp.concatenate([summed[:24], filler], axis=0)
    value_rows = jnp.concatenate([summed[24:], filler], axis=0)
    grads[z, :, head_cols : head_cols + HD] = key_rows.astype(jnp.bfloat16)
    grads[z, :, head_cols + HD :] = value_rows.astype(jnp.bfloat16)
    tail_part = grads.at[z, :, head_cols:]
    for step in (2, 1, 3):
        push(tail_part, tail_part, at_grads + 4 + step, at_grads + 4 + step, along(step))
    for step in range(1, 4):
        move(head_part, head_part, 0, at_grads + step, plane(1)).wait_recv()
        move(tail_part, tail_part, 0, at_grads + 4 + step, plane(1)).wait_recv()

    packed_at = lax.broadcasted_iota(jnp.int32, (rows, 4 * PAD), 1)
    packer = (packed_at - (PAD - count) * prompt_of == row_at).astype(jnp.bfloat16)
    packed = dot(packer, grads[...].reshape(4 * PAD, head_cols + 2 * HD), plain)
    packed = packed.astype(jnp.bfloat16)
    inner = jnp.zeros((rows, 128), jnp.float32)
    at_pair = take(4)
    for half in range(2):
        for s in range(4):
            owner = 2 * near[s] + ((1 - core) if half == 0 else core)
            span = pl.ds(pl.multiple_of(owner * slice_width, slice_width), slice_width)
            part = dot(packed[:, :head_cols], wq[span, :], crossed)
            part = part + dot(packed[:, head_cols:], wkv[span, :], crossed)
            where = pl.ds(pl.multiple_of(z * rows_here + owner * slice_width, 128), slice_width)
            part = part * gain[:, where].astype(jnp.float32)
            product = part * scaled[:, span]
            for j in range(0, slice_width, 128):
                inner = inner + product[:, j : j + 128]
            weighted[half, s] = part
            if half == 0:
                push(weighted.at[0, s], pair_in.at[s], at_pair + s, at_pair + s, {"tensor": pair})
    inner = jnp.sum(inner, axis=1, keepdims=True)
    inner_in[t] = jnp.broadcast_to(lay_row(inner, 128), (8, 128))
    at_inner = take(8)
    for step in range(1, 8):
        push(
            inner_in.at[t],
            inner_in.at[t],
            at_inner + step,
            at_inner + step,
            {"tensor": lax.rem(t + step, 8)},
        )
    at_shares = take(4)
    for s in (3, 1, 2, 0):
        move(pair_in.at[s], pair_in.at[s], 0, at_pair + s, {"tensor": pair}).wait_recv()
        weighted[1, s] = weighted[1, s] + pair_in[s]
        if s:
            push(weighted.at[1, s], shares.at[s - 1], at_shares + s, at_shares + s, plane(s))
    for step in range(1, 8):
        move(inner_in.at[t], inner_in.at[t], 0, at_inner + step, plane(1)).wait_recv()
    inner = inner_in[0]
    for j in range(1, 8):
        inner = inner + inner_in[j]
    inner_z[z] = inner
    at_inner_z = take(4)
    for step in range(1, 4):
        push(inner_z.at[z], inner_z.at[z], at_inner_z + step, at_inner_z + step, along(step))
    for s in (1, 2, 3):
        move(shares.at[s - 1], shares.at[s - 1], 0, at_shares + s, plane(1)).wait_recv()
    own = weighted[1, 0] + shares[0] + shares[1] + shares[2]
    for step in range(1, 4):
        move(inner_z.at[z], inner_z.at[z], 0, at_inner_z + step, plane(1)).wait_recv()
    inner = (inner_z[0] + inner_z[1] + inner_z[2] + inner_z[3])[:1]
    inner = pick_column(inner, rows) / width

    here = pl.ds(pl.multiple_of(t * slice_width, slice_width), slice_width)
    suffix_grads[z, :, here] = (norm_rows * (own - scaled[:, here] * inner)).astype(jnp.bfloat16)

    def grad_of(p, chip_index, core_index):
        first = (2 * chip_index + core_index) * slice_width
        return suffix_grads.at[p, :, pl.ds(pl.multiple_of(first, slice_width), slice_width)]

    at_z = take(4)
    spread = [take(4) for _ in range(4)]
    doubled = [take(4) for _ in range(4)]
    mine_now = grad_of(z, chip, core)
    for step in (2, 1, 3):
        push(mine_now, mine_now, at_z + step, at_z + step, along(step))
    for step in order:
        block = grad_of(lax.rem(z - step + 4, 4), chip, core)
        if step:
            move(block, block, 0, at_z + step, plane(1)).wait_recv()
        for s in (3, 1, 2):
            push(block, block, spread[step] + s, spread[step] + s, plane(s))
        push(block, block, spread[step], spread[step], {"tensor": pair})

    for i, step in enumerate(order):
        p = lax.rem(z - step + 4, 4)
        for s in (1, 2, 3):
            block = grad_of(p, near[s], core)
            move(block, block, 0, spread[step] + s, plane(s)).wait_recv()
            push(block, block, doubled[step] + s, doubled[step] + s, {"tensor": pair})
        for s in range(4):
            block = grad_of(p, near[s], 1 - core)
            number = doubled[step] + s if s else spread[step]
            move(block, block, 0, number, {"tensor": pair}).wait_recv()
        features = pl.ds(pl.multiple_of(p * rows_here, rows_here), rows_here)

        @pl.loop(0, chunks)
        def _(c):
            if i == 0:
                load_table(c).wait()
            span = pl.ds(pl.multiple_of(c * CHUNK, CHUNK), CHUNK)
            part = dot(suffix_grads[p], table[span, features], crossed)
            if i:
                part = part + out[:, span]
            if i == 3:
                part = jnp.where(banned[:, span] == 1, 0.0, -part)
            out[:, span] = part

    for copy in sent:
        copy.wait_send()
    for a in range(2):
        for s in range(4):

            @pl.when(near[s] != z)
            def _():
                block = x.at[a, z, rows_of(chip), own_cols]
                move(block, block, across[a] + s, 0, {"prompt": near[s]}).wait_send()

    line_sent(*kv_args, line_kv, relay_kv)
    for i in range(2):
        line_sent(*line_of(i), line[i], total.at[i])


def fused(
    embeds,
    norm_gain,
    query_weight,
    key_weight,
    value_weight,
    out_weight,
    out_grad,
    suffix_pos,
    vocab_table,
    banned,
):
    seq, cols = embeds.shape[1:]
    rows_here, head_cols = query_weight.shape
    count = suffix_pos.shape[1]
    vocab_here, width = vocab_table.shape
    heads = head_cols // HD
    rows = 4 * count
    slice_width = rows_here // 8
    low, full, short = jnp.bfloat16, jnp.float32, jnp.int16
    coded = head_cols + HD
    local = pl.BlockSpec(memory_space=pltpu.VMEM)
    apart = pl.BlockSpec(memory_space=pl.ANY)
    scratch = [
        ((rows_here, head_cols), low),
        ((rows_here, 2 * HD), low),
        ((head_cols, rows_here), low),
        (vocab_table.shape, low),
        ((seq, cols), low),
        ((2, 3, seq // 4, cols), low),
        ((2, 4, seq, rows_here), low),
        ((8, 8, 128), full),
        ((4, 8, 128), full),
        ((4, 1, count), jnp.int32),
        ((4, seq, rows_here), low),
        ((4, seq, 2 * HD), full),
        ((4, seq, 2 * HD), full),
        ((seq, 2 * HD), full),
        ((2, 4, seq, head_cols), full),
        ((2, 4, seq, coded), short),
        ((2, 4, seq, coded), short),
        ((2, seq, coded), short),
        ((2, seq, coded), short),
        ((8, seq, 2 * HD), low),
        ((2, seq, head_cols), low),
        ((8, 48, HD), full),
        ((8, 48, HD), full),
        ((4, PAD, head_cols + 2 * HD), low),
        ((rows, rows_here), full),
        ((2, 4, rows, slice_width), full),
        ((4, rows, slice_width), full),
        ((3, rows, slice_width), full),
        ((8, 8, 128), full),
        ((4, 8, 128), full),
        ((4, rows, rows_here), low),
    ]
    scores = pl.pallas_call(
        fused_kernel,
        out_shape=jax.ShapeDtypeStruct((rows, vocab_here), full),
        in_specs=[apart, apart, local, apart, apart, apart, apart, local, apart, local],
        out_specs=local,
        scratch_shapes=[pltpu.VMEM(shape, dtype) for shape, dtype in scratch]
        + [
            pltpu.SemaphoreType.DMA((SEMS,)),
            pltpu.SemaphoreType.DMA((SEMS,)),
            pltpu.SemaphoreType.DMA((8 + vocab_here // CHUNK,)),
            pltpu.SemaphoreType.DMA((2,)),
        ],
        compiler_params=pltpu.CompilerParams(
            collective_id=11, has_side_effects=True, vmem_limit_bytes=60 << 20
        ),
    )(
        embeds,
        out_grad,
        norm_gain.reshape(1, -1),
        query_weight,
        key_weight,
        value_weight,
        out_weight,
        suffix_pos,
        vocab_table,
        banned.reshape(1, -1),
    )
    return scores.reshape(4, count, vocab_here)


def fits(mesh_sizes, arrays):
    embeds, query_weight, key_weight, suffix_pos, vocab_table = arrays
    return (
        mesh_sizes == (4, 8)
        and embeds.shape[1] == 64
        and query_weight.shape[1] == 8 * HD
        and key_weight.shape[1] == HD
        and query_weight.shape[0] == 2 * embeds.shape[2]
        and query_weight.shape[0] % 2048 == 0
        and suffix_pos.shape[1] == 20
        and vocab_table.shape[0] % CHUNK == 0
    )


def part_of(*args):
    sizes = (lax.axis_size("prompt"), lax.axis_size("tensor"))
    if fits(sizes, (args[0], args[2], args[3], args[7], args[8])):
        return fused(*args)
    return on_device(*args)


def solution(mesh):
    return jax.shard_map(
        part_of,
        mesh=mesh,
        in_specs=(
            P("prompt", None, "tensor"),
            P(),
            P("prompt", "tensor"),
            P("prompt", "tensor"),
            P("prompt", "tensor"),
            P("tensor", "prompt"),
            P("prompt", None, "tensor"),
            P("prompt", None),
            P(("prompt", "tensor"), None),
            P(("prompt", "tensor")),
        ),
        out_specs=P(None, None, ("prompt", "tensor")),
        check_vma=False,
    )
```

```python
import functools
import math

import jax
import jax.numpy as jnp
from jax import lax
from jax.experimental import pallas as pl
from jax.experimental.pallas import tpu as pltpu
from jax.sharding import PartitionSpec as P

KVH = 8
HD = 128


EPSILON = 1e-05


def exchange_kernel(axis, count, spread, *refs):
    arrays = len(spread)
    sources, targets = refs[:arrays], refs[arrays : 2 * arrays]
    send_sem, recv_sem, own_sem = refs[2 * arrays :]
    here = lax.axis_index(axis)

    def block(i, to):
        return sources[i].at[to] if spread[i] else sources[i]

    kept = []
    for i in range(arrays):
        copy = pltpu.make_async_copy(block(i, here), targets[i].at[here], own_sem.at[i])
        copy.start()
        kept.append(copy)
    barrier = pltpu.get_barrier_semaphore()
    for step in range(1, count):
        peer = lax.rem(here + step, count)
        pl.semaphore_signal(
            barrier, inc=1, device_id={axis: peer}, device_id_type=pl.DeviceIdType.MESH
        )
    pl.semaphore_wait(barrier, count - 1)
    copies = []
    for step in range(1, count):
        peer = lax.rem(here + step, count)
        for i in range(arrays):
            copy = pltpu.make_async_remote_copy(
                src_ref=block(i, peer),
                dst_ref=targets[i].at[here],
                send_sem=send_sem.at[i, step - 1],
                recv_sem=recv_sem.at[i, step - 1],
                device_id={axis: peer},
                device_id_type=pl.DeviceIdType.MESH,
            )
            copy.start()
            copies.append(copy)
    for copy in kept + copies:
        copy.wait()


def exchange(axis, number, *operands):
    count = lax.axis_size(axis)
    arrays = [array for array, _ in operands]
    spread = tuple(each for _, each in operands)
    shapes = [
        jax.ShapeDtypeStruct(((count,) + (a.shape[1:] if each else a.shape)), a.dtype)
        for a, each in operands
    ]
    space = pl.BlockSpec(memory_space=pltpu.VMEM)
    sems = pltpu.SemaphoreType.DMA((len(arrays), count - 1))
    return pl.pallas_call(
        functools.partial(exchange_kernel, axis, count, spread),
        out_shape=shapes,
        in_specs=[space] * len(arrays),
        out_specs=[space] * len(arrays),
        scratch_shapes=[sems, sems, pltpu.SemaphoreType.DMA((len(arrays),))],
        compiler_params=pltpu.CompilerParams(
            collective_id=number, has_side_effects=True, vmem_limit_bytes=40 << 20
        ),
    )(*arrays)


def dot_f32(spec, a, b):
    return jnp.einsum(spec, a, b, preferred_element_type=jnp.float32)


MESH = pl.DeviceIdType.MESH


def greet(axis, peers):
    barrier = pltpu.get_barrier_semaphore()
    for peer in peers:
        pl.semaphore_signal(barrier, inc=1, device_id={axis: peer}, device_id_type=MESH)
    pl.semaphore_wait(barrier, len(peers))


def gather_kernel(axis, count, arrays, *refs):
    sources, targets = refs[:arrays], refs[arrays : 2 * arrays]
    send_sem, recv_sem, own_sem = refs[2 * arrays :]
    here = lax.axis_index(axis)
    chips = count // 2
    chip, core = here // 2, lax.rem(here, 2)
    pair = 2 * chip + (1 - core)
    kept = []
    for i in range(arrays):
        copy = pltpu.make_async_copy(sources[i], targets[i].at[here], own_sem.at[i])
        copy.start()
        kept.append(copy)

    def push(i, source, slot, number, peer):
        return pltpu.make_async_remote_copy(
            src_ref=source,
            dst_ref=targets[i].at[slot],
            send_sem=send_sem.at[i, number],
            recv_sem=recv_sem.at[i, number],
            device_id={axis: peer},
            device_id_type=MESH,
        )

    others = [2 * lax.rem(chip + step, chips) + core for step in range(1, chips)]
    greet(axis, others + [pair])
    first = []
    for step in range(1, chips):
        for i in range(arrays):
            copy = push(i, sources[i], here, step, others[step - 1])
            copy.start()
            first.append(copy)
    rest = []
    for i in range(arrays):
        copy = push(i, sources[i], here, 0, pair)
        copy.start()
        rest.append(copy)
    for step in range(1, chips):
        slot = 2 * lax.rem(chip + chips - step, chips) + core
        for i in range(arrays):
            first[(step - 1) * arrays + i].wait_recv()
            copy = push(i, targets[i].at[slot], slot, chips - 1 + step, pair)
            copy.start()
            rest.append(copy)
    for copy in first:
        copy.wait_send()
    for copy in kept + rest:
        copy.wait()


def gather(axis, number, *arrays):
    count = lax.axis_size(axis)
    shapes = [jax.ShapeDtypeStruct((count,) + a.shape, a.dtype) for a in arrays]
    space = pl.BlockSpec(memory_space=pltpu.VMEM)
    sems = pltpu.SemaphoreType.DMA((len(arrays), count - 1))
    return pl.pallas_call(
        functools.partial(gather_kernel, axis, count, len(arrays)),
        out_shape=shapes,
        in_specs=[space] * len(arrays),
        out_specs=[space] * len(arrays),
        scratch_shapes=[sems, sems, pltpu.SemaphoreType.DMA((len(arrays),))],
        compiler_params=pltpu.CompilerParams(
            collective_id=number, has_side_effects=True, vmem_limit_bytes=40 << 20
        ),
    )(*arrays)


def line_kernel(axis, source, target, relay, send_sem, recv_sem, own_sem):
    here = lax.axis_index(axis)
    own = pltpu.make_async_copy(source.at[here], target.at[here], own_sem.at[0])
    own.start()
    greet(axis, [lax.rem(here + step, 4) for step in range(1, 4)])

    def push(block, slot, number, peer, into=None):
        return pltpu.make_async_remote_copy(
            src_ref=block,
            dst_ref=target.at[slot] if into is None else into,
            send_sem=send_sem.at[number],
            recv_sem=recv_sem.at[slot if into is None else 4],
            device_id={axis: peer},
            device_id_type=MESH,
        )

    for role in range(4):
        far = 3 if role < 2 else 0
        middle = 1 if role < 2 else 2
        across = 3 - middle

        @pl.when(here == role)
        def _():
            if role == middle:
                sent = [
                    push(source.at[across], role, 0, across),
                    push(source.at[3 - far], role, 1, 3 - far),
                ]
                for copy in sent:
                    copy.start()
                total = push(relay, role, 2, far)
                push(source.at[far], role, 3, far, relay).wait_recv()
                relay[...] = relay[...] + source[far]
                total.start()
                sent.append(total)
                arriving = [0, across, 3]
            else:
                handed = push(source.at[far], role, 0, middle, relay)
                handed.start()
                target[far] = jnp.zeros_like(target[far])
                handed.wait_send()
                sent = [
                    push(source.at[across], role, 1, across),
                    push(source.at[middle], role, 2, middle),
                ]
                for copy in sent:
                    copy.start()
                arriving = [1, 2]
            for slot in arriving:
                push(source.at[slot], slot, 3, slot).wait_recv()
            for copy in sent:
                copy.wait_send()

    own.wait()


def line_exchange(axis, number, blocks):
    if lax.axis_size(axis) != 4:
        return exchange(axis, number, (blocks, True))[0]
    space = pl.BlockSpec(memory_space=pltpu.VMEM)
    return pl.pallas_call(
        functools.partial(line_kernel, axis),
        out_shape=jax.ShapeDtypeStruct(blocks.shape, blocks.dtype),
        in_specs=[space],
        out_specs=space,
        scratch_shapes=[
            pltpu.VMEM(blocks.shape[1:], blocks.dtype),
            pltpu.SemaphoreType.DMA((4,)),
            pltpu.SemaphoreType.DMA((5,)),
            pltpu.SemaphoreType.DMA((1,)),
        ],
        compiler_params=pltpu.CompilerParams(
            collective_id=number, has_side_effects=True, vmem_limit_bytes=40 << 20
        ),
    )(blocks)


CHUNK = 512


def score_kernel(
    axis, count, part, vocab, scores, got, flat, table, send_sem, recv_sem, own_sem, load_sem
):
    def load(c):
        span = pl.ds(pl.multiple_of(c * CHUNK, CHUNK), CHUNK)
        return pltpu.make_async_copy(vocab.at[span], table.at[span], load_sem.at[c])

    chunks = vocab.shape[0] // CHUNK
    for c in range(chunks):
        load(c).start()
    gather_kernel(axis, count, 1, part, got, send_sem, recv_sem, own_sem)
    wide = part.shape[2]
    for p in range(part.shape[0]):
        for t in range(count):
            start = (p * count + t) * wide
            flat[:, start : start + wide] = got[t, p]

    @pl.loop(0, chunks)
    def _(c):
        load(c).wait()
        span = pl.ds(pl.multiple_of(c * CHUNK, CHUNK), CHUNK)
        scores[:, span] = -lax.dot_general(
            flat[...],
            table[span, :],
            (((1,), (1,)), ((), ())),
            preferred_element_type=jnp.float32,
        )


def gather_score(axis, number, part, vocab):
    count = lax.axis_size(axis)
    n_prompt, rows, wide = part.shape
    vocab_here, width = vocab.shape
    if wide % 128 or vocab_here % CHUNK or rows % 16:
        (part,) = gather(axis, number, part)
        return -dot_f32("rd,vd->rv", part.transpose(2, 1, 0, 3).reshape(rows, width), vocab)
    sems = pltpu.SemaphoreType.DMA((1, count - 1))
    return pl.pallas_call(
        functools.partial(score_kernel, axis, count),
        out_shape=jax.ShapeDtypeStruct((rows, vocab_here), jnp.float32),
        in_specs=[pl.BlockSpec(memory_space=pltpu.VMEM), pl.BlockSpec(memory_space=pl.ANY)],
        out_specs=pl.BlockSpec(memory_space=pltpu.VMEM),
        scratch_shapes=[
            pltpu.VMEM((count,) + part.shape, part.dtype),
            pltpu.VMEM((rows, width), part.dtype),
            pltpu.VMEM(vocab.shape, vocab.dtype),
            sems,
            sems,
            pltpu.SemaphoreType.DMA((1,)),
            pltpu.SemaphoreType.DMA((vocab_here // CHUNK,)),
        ],
        compiler_params=pltpu.CompilerParams(
            collective_id=number, has_side_effects=True, vmem_limit_bytes=52 << 20
        ),
    )(part, vocab)


def on_device(
    embeds,
    norm_gain,
    query_weight,
    key_weight,
    value_weight,
    out_weight,
    out_grad,
    suffix_pos,
    vocab_table,
    banned,
):
    n_prompt = lax.axis_size("prompt")
    n_tensor = lax.axis_size("tensor")
    here_prompt = lax.axis_index("prompt")
    here_tensor = lax.axis_index("tensor")
    seq_len = embeds.shape[1]
    suffix_count = suffix_pos.shape[1]
    width = embeds.shape[2] * n_tensor
    rows_here, head_cols = query_weight.shape
    key_cols = key_weight.shape[1]
    heads_here = head_cols // HD
    slice_width = rows_here // n_tensor
    logit_scale = 1.0 / math.sqrt(HD)

    split_rows = seq_len // n_tensor
    ratio = n_tensor // n_prompt
    feature_cols = embeds.shape[2]
    both = jnp.concatenate(
        [
            embeds.reshape(n_tensor, split_rows, feature_cols),
            out_grad.reshape(n_tensor, split_rows, feature_cols),
        ],
        axis=1,
    )
    (both,) = exchange("tensor", 0, (both, True))
    own = both[:, :split_rows].astype(jnp.float32)
    inverse_norm = lax.rsqrt(jnp.sum(own * own, axis=(0, 2))[:, None] / width + EPSILON)
    inverse_norm = jnp.broadcast_to(inverse_norm, (split_rows, 128))
    both = both.reshape(n_prompt, ratio, 2 * split_rows, feature_cols)
    both, inverse_norm, suffix_all = exchange(
        "prompt", 1, (both, True), (inverse_norm, False), (suffix_pos, False)
    )
    both, inverse_norm = gather("tensor", 2, both, inverse_norm)
    suffix_all = suffix_all.reshape(n_prompt, suffix_count)
    both = both.reshape(n_tensor, n_prompt, ratio, 2, split_rows, feature_cols)
    both = both.transpose(3, 1, 0, 4, 2, 5).reshape(2, n_prompt, seq_len, rows_here)
    embeds, out_grad = both[0], both[1]
    inverse_norm = inverse_norm[..., :1].transpose(1, 0, 2, 3).reshape(n_prompt, seq_len, 1)
    embeds_float = embeds.astype(jnp.float32)
    gain_rows = lax.dynamic_slice_in_dim(norm_gain, here_prompt * rows_here, rows_here, 0)
    gain_rows = gain_rows.astype(jnp.float32)
    normed = (embeds_float * inverse_norm * gain_rows).astype(jnp.bfloat16)

    parts = jnp.concatenate(
        [
            dot_f32("psd,dc->psc", normed, query_weight),
            dot_f32("psd,dc->psc", normed, key_weight),
            dot_f32("psd,dc->psc", normed, value_weight),
            dot_f32("psd,cd->psc", out_grad, out_weight),
        ],
        axis=2,
    )
    parts = line_exchange("prompt", 3, parts)
    whole = jnp.sum(parts, axis=0).astype(jnp.bfloat16)
    contexts = whole[:, head_cols + 2 * key_cols :]
    contexts = contexts.reshape(seq_len, heads_here, HD)
    queries = whole[:, :head_cols].reshape(seq_len, heads_here, HD)
    (key_values,) = gather("tensor", 4, whole[:, head_cols : head_cols + 2 * key_cols])
    key_values = key_values.reshape(n_tensor, seq_len, 2, key_cols).transpose(2, 1, 0, 3)
    key_values = key_values.reshape(2, seq_len, KVH * HD)
    fold = min(heads_here, KVH)
    first = ((here_tensor * heads_here) % KVH) * HD
    if fold < KVH:
        key_values = lax.dynamic_slice_in_dim(key_values, first, fold * HD, 2)
    key_values = key_values.reshape(2, seq_len, fold, HD)
    if heads_here > fold:
        key_values = jnp.tile(key_values, (1, 1, heads_here // fold, 1))
    keys, values = key_values[0], key_values[1]

    logits = dot_f32("qhd,khd->hqk", queries, keys) * logit_scale
    row_index = lax.broadcasted_iota(jnp.int32, (seq_len, seq_len), 0)
    col_index = lax.broadcasted_iota(jnp.int32, (seq_len, seq_len), 1)
    causal = col_index <= row_index
    largest = jnp.max(jnp.where(causal, logits, -1e30), axis=-1, keepdims=True)
    raised = jnp.where(causal, jnp.exp(logits - largest), 0.0)
    probs = raised / jnp.sum(raised, axis=-1, keepdims=True)
    probs_low = probs.astype(jnp.bfloat16)
    prob_grad = dot_f32("qhd,khd->hqk", contexts, values)
    logit_grad = (
        probs * (prob_grad - jnp.sum(prob_grad * probs, axis=-1, keepdims=True)) * logit_scale
    ).astype(jnp.bfloat16)
    steps_iota = lax.broadcasted_iota(jnp.int32, (suffix_count, seq_len), 1)
    chooser = (steps_iota == suffix_pos[0][:, None]).astype(jnp.bfloat16)
    logit_rows = dot_f32("ns,hsk->hnk", chooser, logit_grad).astype(jnp.bfloat16)
    query_grad = dot_f32("hnk,khd->nhd", logit_rows, keys).astype(jnp.bfloat16)
    query_grad = query_grad.reshape(suffix_count, head_cols)
    logit_cols = dot_f32("hqk,nk->hnq", logit_grad, chooser).astype(jnp.bfloat16)
    prob_cols = dot_f32("hqk,nk->hnq", probs_low, chooser).astype(jnp.bfloat16)
    key_each = dot_f32("hnq,qhd->nhd", logit_cols, queries)
    value_each = dot_f32("hnq,qhd->nhd", prob_cols, contexts)
    slots = jnp.stack([key_each, value_each])
    slots = slots.reshape(2, suffix_count, heads_here // fold, fold * HD).sum(axis=2)
    if fold < KVH:
        slots = lax.dynamic_update_slice_in_dim(
            jnp.zeros((2, suffix_count, KVH * HD), jnp.float32), slots, first, 2
        )
    slots = slots.reshape(2 * suffix_count, n_tensor, key_cols).transpose(1, 0, 2)
    (grads,) = exchange("tensor", 5, (slots, True))
    grads = jnp.sum(grads, axis=0).astype(jnp.bfloat16).reshape(2, suffix_count, key_cols)
    grads = jnp.concatenate([query_grad, grads[0], grads[1]], axis=1)
    (grads,) = exchange("prompt", 6, (grads, False))
    rows = n_prompt * suffix_count
    grads = grads.reshape(rows, head_cols + 2 * key_cols)
    steps_iota = lax.broadcasted_iota(jnp.int32, (n_prompt, suffix_count, seq_len), 2)
    chooser_all = steps_iota == suffix_all[:, :, None]
    embed_rows = dot_f32("pns,psd->pnd", chooser_all.astype(jnp.bfloat16), embeds)
    norm_rows = jnp.sum(
        jnp.where(chooser_all, inverse_norm[:, None, :, 0], 0.0), axis=-1, keepdims=True
    )
    scaled = (embed_rows * norm_rows).reshape(rows, rows_here)
    norm_rows = norm_rows.reshape(rows, 1)
    branch = dot_f32("nc,dc->nd", grads[:, :head_cols], query_weight)
    branch = branch + dot_f32("nc,dc->nd", grads[:, head_cols : head_cols + key_cols], key_weight)
    branch = branch + dot_f32("nc,dc->nd", grads[:, head_cols + key_cols :], value_weight)
    branch = branch * gain_rows
    inner = jnp.sum(branch * scaled, axis=-1)
    branch = branch.reshape(rows, n_tensor, slice_width).transpose(1, 0, 2)
    share, inner = exchange("tensor", 7, (branch, True), (inner[None, :], False))
    weighted = jnp.sum(share, axis=0)
    (inner,) = exchange("prompt", 8, (jnp.sum(inner, axis=0), False))
    inner = jnp.sum(inner, axis=0).reshape(rows, 1) / width
    scaled = lax.dynamic_slice_in_dim(scaled, here_tensor * slice_width, slice_width, 1)
    suffix_grad = (norm_rows * (weighted - scaled * inner)).astype(jnp.bfloat16)
    (suffix_grad,) = exchange("prompt", 9, (suffix_grad, False))
    scores = gather_score("tensor", 10, suffix_grad, vocab_table)
    scores = scores.reshape(n_prompt, suffix_count, vocab_table.shape[0])
    return jnp.where(banned[None, None, :] == 1, 0.0, scores)


PAD = 32
TINY = 1e-30
FULL = 32767.0
SEMS = 224


def pick_column(row, rows):
    wide = row.shape[1]
    down = lax.broadcasted_iota(jnp.int32, (rows, wide), 0)
    along = lax.broadcasted_iota(jnp.int32, (rows, wide), 1)
    return jnp.sum(jnp.where(down == along, row, 0.0), axis=1, keepdims=True)


def lay_row(column, wide):
    rows = column.shape[0]
    down = lax.broadcasted_iota(jnp.int32, (rows, wide), 0)
    along = lax.broadcasted_iota(jnp.int32, (rows, wide), 1)
    return jnp.sum(jnp.where(down == along, column, 0.0), axis=0, keepdims=True)


def lane_sums(values):
    total = values[:, :128]
    for j in range(128, values.shape[1], 128):
        total = total + values[:, j : j + 128]
    return jnp.sum(total, axis=1, keepdims=True)


def code_block(read, write, heads, rows):
    lanes = lax.broadcasted_iota(jnp.int32, (rows, HD), 1)
    powers = jnp.zeros((rows, HD), jnp.float32)
    for h in range(heads):
        block = read(h)
        peak = jnp.max(jnp.abs(block), axis=1, keepdims=True)
        power = jnp.floor(jnp.log2(jnp.maximum(peak, TINY))) + 1.0
        fixed = jnp.floor(block * (jnp.exp2(-power) * FULL) + 0.5)
        fixed = jnp.clip(fixed, -FULL, FULL)
        write(h, fixed.astype(jnp.int32).astype(jnp.int16))
        powers = jnp.where(lanes == h, power, powers)
    write(heads, powers.astype(jnp.int32).astype(jnp.int16))


def scale_of(tile):
    return jnp.exp2(tile.astype(jnp.int32).astype(jnp.float32)) * (1.0 / FULL)


def fused_kernel(
    embeds,
    out_grad,
    gain,
    query_weight,
    key_weight,
    value_weight,
    out_weight,
    suffix,
    vocab,
    banned,
    out,
    wq,
    wkv,
    wo,
    table,
    mine,
    stage,
    x,
    sums,
    norms,
    spots,
    nb,
    pkv,
    rkv,
    relay_kv,
    pp,
    coded,
    arrived,
    relay,
    total,
    kvg,
    whole,
    slots,
    slots_in,
    grads,
    scaled,
    weighted,
    pair_in,
    shares,
    inner_in,
    inner_z,
    suffix_grads,
    partial,
    gain_row,
    send_sem,
    recv_sem,
    load_sem,
    own_sem,
):
    z = lax.axis_index("prompt")
    t = lax.axis_index("tensor")
    chip, core = t // 2, lax.rem(t, 2)
    pair = 2 * chip + (1 - core)
    chip_y, chip_x = chip // 2, lax.rem(chip, 2)
    near = [
        chip,
        2 * chip_y + (1 - chip_x),
        2 * (1 - chip_y) + chip_x,
        2 * (1 - chip_y) + (1 - chip_x),
    ]
    seq, cols = embeds.shape[1], embeds.shape[2]
    width = gain.shape[0]
    rows_here, head_cols = query_weight.shape
    heads = head_cols // HD
    count = suffix.shape[1]
    rows = 4 * count
    quarter = seq // 4
    slice_width = rows_here // 8
    scale = 1.0 / math.sqrt(HD)
    dot = functools.partial(lax.dot_general, preferred_element_type=jnp.float32)
    plain = (((1,), (0,)), ((), ()))
    crossed = (((1,), (1,)), ((), ()))

    chunks = vocab.shape[0] // CHUNK

    def load_table(c):
        span = pl.ds(pl.multiple_of(c * CHUNK, CHUNK), CHUNK)
        return pltpu.make_async_copy(vocab.at[span], table.at[span], load_sem.at[8 + c])

    loads = {
        "e": pltpu.make_async_copy(embeds.at[0], mine, load_sem.at[0]),
        "k": pltpu.make_async_copy(key_weight, wkv.at[:, :HD], load_sem.at[1]),
        "v": pltpu.make_async_copy(value_weight, wkv.at[:, HD:], load_sem.at[2]),
        "q": pltpu.make_async_copy(query_weight, wq, load_sem.at[3]),
        "o": pltpu.make_async_copy(out_weight, wo, load_sem.at[4]),
    }
    loads["e"].start()

    barrier = pltpu.get_barrier_semaphore()
    for step in range(1, 8):
        pl.semaphore_signal(
            barrier, inc=1, device_id={"tensor": lax.rem(t + step, 8)}, device_id_type=MESH
        )
    for step in range(1, 4):
        pl.semaphore_signal(
            barrier, inc=1, device_id={"prompt": lax.rem(z + step, 4)}, device_id_type=MESH
        )
    pl.semaphore_wait(barrier, 10)

    used = [0]
    sent = []

    def take(number=1):
        used[0] += number
        assert used[0] <= SEMS
        return used[0] - number

    def move(source, target, s, r, device):
        return pltpu.make_async_remote_copy(
            src_ref=source,
            dst_ref=target,
            send_sem=send_sem.at[s],
            recv_sem=recv_sem.at[r],
            device_id=device,
            device_id_type=MESH,
        )

    def push(source, target, s, r, device):
        copy = move(source, target, s, r, device)
        copy.start()
        sent.append(copy)

    def plane(s, other=False):
        return {"tensor": 2 * near[s] + ((1 - core) if other else core)}

    def along(step):
        return {"prompt": lax.rem(z + step, 4)}

    def rows_of(chip_index):
        return pl.ds(pl.multiple_of(quarter * chip_index, quarter), quarter)

    sources = (embeds.at[0], out_grad.at[0])
    own_cols = pl.ds(pl.multiple_of(core * cols, 128), cols)
    pair_cols = pl.ds(pl.multiple_of((1 - core) * cols, 128), cols)

    hop = [take(4) for _ in range(2)]

    def first_hop(a):
        for s in (3, 1, 2):
            push(
                sources[a].at[rows_of(near[s])], stage.at[a, s - 1], hop[a] + s, hop[a] + s, plane(s)
            )

    first_hop(0)
    at_spots = take(4)
    for step in range(1, 4):
        push(suffix, spots.at[z], at_spots + step, at_spots + step, along(step))
    spots[z] = suffix[...]

    loads["e"].wait()
    square = jnp.zeros((seq, 128), jnp.float32)
    for j in range(0, cols, 128):
        block = mine[:, j : j + 128].astype(jnp.float32)
        square = square + block * block
    square = jnp.sum(square, axis=1, keepdims=True)
    sums[t] = jnp.broadcast_to(lay_row(square, 128), (8, 128))
    at_sums = take(8)
    for step in range(1, 8):
        push(
            sums.at[t], sums.at[t], at_sums + step, at_sums + step, {"tensor": lax.rem(t + step, 8)}
        )

    for name in "kvqo":
        loads[name].start()

    across = [take(4) for _ in range(2)]
    across_in = [take(4) for _ in range(2)]

    def second_hop(a):
        for s in range(4):
            if s == 0:
                block = sources[a].at[rows_of(chip)]
            else:
                move(stage.at[a, s - 1], stage.at[a, s - 1], 0, hop[a] + s, plane(s)).wait_recv()
                block = stage.at[a, s - 1]
            target = x.at[a, z, rows_of(chip), own_cols]

            @pl.when(near[s] == z)
            def _():
                copy = pltpu.make_async_copy(block, target, own_sem.at[a])
                copy.start()
                copy.wait()

            @pl.when(near[s] != z)
            def _():
                move(block, target, across[a] + s, across_in[a] + z, {"prompt": near[s]}).start()

    second_hop(0)
    first_hop(1)
    for step in range(1, 8):
        move(sums.at[t], sums.at[t], 0, at_sums + step, plane(1)).wait_recv()
    square = sums[0]
    for j in range(1, 8):
        square = square + sums[j]
    norms[z] = lax.rsqrt(square / width + EPSILON)
    at_norms = take(4)
    for step in range(1, 4):
        push(norms.at[z], norms.at[z], at_norms + step, at_norms + step, along(step))

    order = (0, 1, 3, 2)
    third = [[take(4) for _ in range(4)] for _ in range(2)]
    fourth = [[take(4) for _ in range(4)] for _ in range(2)]

    def third_hop(a):
        for step in order:
            p = lax.rem(z + step, 4)
            block = x.at[a, p, rows_of(chip), own_cols]
            if step:
                move(block, block, 0, across_in[a] + p, plane(1)).wait_recv()
            for s in (3, 1, 2):
                push(block, block, third[a][step] + s, third[a][step] + s, plane(s))
            push(block, block, third[a][step], third[a][step], {"tensor": pair})

    def fourth_hop(a):
        for step in order:
            p = lax.rem(z + step, 4)
            for s in (1, 2, 3):
                block = x.at[a, p, rows_of(near[s]), own_cols]
                move(block, block, 0, third[a][step] + s, plane(s)).wait_recv()
                push(block, block, fourth[a][step] + s, fourth[a][step] + s, {"tensor": pair})

    def last_hop(a):
        for step in order:
            p = lax.rem(z + step, 4)
            for s in range(4):
                block = x.at[a, p, rows_of(near[s]), pair_cols]
                number = fourth[a][step] + s if s else third[a][step]
                move(block, block, 0, number, {"tensor": pair}).wait_recv()

    third_hop(0)
    second_hop(1)
    fourth_hop(0)
    last_hop(0)
    third_hop(1)

    for step in range(1, 4):
        move(norms.at[z], norms.at[z], 0, at_norms + step, plane(1)).wait_recv()
        move(suffix, spots.at[z], 0, at_spots + step, plane(1)).wait_recv()

    gain_here = pl.ds(pl.multiple_of(z * rows_here, rows_here), rows_here)
    gain_row[...] = gain[gain_here].astype(jnp.float32).reshape(1, rows_here)

    @pl.loop(0, 4)
    def _(p):
        inverse = pick_column(norms[p][:1], seq)
        gains = gain_row[...]
        for j in range(0, rows_here, 512):
            block = x[0, p, :, j : j + 512].astype(jnp.float32)
            block = block * inverse * gains[:, j : j + 512]
            nb[p, :, j : j + 512] = block.astype(jnp.bfloat16)

    loads["k"].wait()
    loads["v"].wait()
    normed = nb[...].reshape(4 * seq, rows_here)
    pkv[...] = dot(normed, wkv[...], plain).reshape(4, seq, 2 * HD)

    is_end = (z == 0) | (z == 3)
    is_mid = (z == 1) | (z == 2)
    end_far, end_mid = 3 - z, 1 + z // 3
    mid_far, mid_near = 6 - 3 * z, 3 * z - 3

    def line_sends(block, into, relay_into, base):
        hand = move(block(end_far), relay_into, base, base + 4, {"prompt": end_mid})
        one = move(block(3 - end_mid), into.at[z], base + 1, base + z, {"prompt": 3 - end_mid})
        two = move(block(end_mid), into.at[z], base + 2, base + z, {"prompt": end_mid})
        over = move(block(3 - z), into.at[z], base, base + z, {"prompt": 3 - z})
        back = move(block(mid_near), into.at[z], base + 1, base + z, {"prompt": mid_near})
        return (hand, one, two), (over, back)

    def line_start(block, into, relay_into, base):
        ends, mids = line_sends(block, into, relay_into, base)

        @pl.when(is_end)
        def _():
            for copy in ends:
                copy.start()

        @pl.when(is_mid)
        def _():
            for copy in mids:
                copy.start()

    def line_relay(block, into, relay_into, base, add, out_block):
        @pl.when(is_mid)
        def _():
            move(relay_into, relay_into, 0, base + 4, {"prompt": mid_far}).wait_recv()
            add()
            move(out_block, into.at[z], base + 2, base + z, {"prompt": mid_far}).start()

    def line_arrive(into, base):
        @pl.when(is_end)
        def _():
            for source in (end_mid, 3 - end_mid):
                move(into.at[z], into.at[z], 0, base + source, plane(1)).wait_recv()

        @pl.when(is_mid)
        def _():
            for source in (0, 3, 3 - z):
                move(into.at[z], into.at[z], 0, base + source, plane(1)).wait_recv()

    def line_sent(block, into, relay_into, base, out_block):
        ends, mids = line_sends(block, into, relay_into, base)

        @pl.when(is_end)
        def _():
            for copy in ends:
                copy.wait_send()

        @pl.when(is_mid)
        def _():
            for copy in mids:
                copy.wait_send()
            move(out_block, into.at[z], base + 2, base + z, {"prompt": mid_far}).wait_send()

    @pl.when(is_end)
    def _():
        rkv[end_far] = jnp.zeros(rkv.shape[1:], rkv.dtype)
        for i in range(2):
            arrived[i, end_far] = jnp.zeros(arrived.shape[2:], arrived.dtype)

    line_kv = take(5)
    line = [take(5) for _ in range(2)]
    kv_args = (lambda d: pkv.at[d], rkv, relay_kv)
    line_start(*kv_args, line_kv)
    for c in range(chunks):
        load_table(c).start()

    def code(i):
        for step in (3, 2, 1):
            d = lax.rem(z + step, 4)

            def write(h, tile):
                coded[i, d, :, h * HD : (h + 1) * HD] = tile

            code_block(lambda h: pp[i, d, :, h * HD : (h + 1) * HD], write, heads, seq)

    def line_of(i):
        return (lambda d: coded.at[i, d], arrived.at[i], relay.at[i])

    def add_coded(i):
        def add():
            factors = scale_of(relay[i, :, heads * HD :])

            def read(h):
                got = relay[i, :, h * HD : (h + 1) * HD].astype(jnp.int32).astype(jnp.float32)
                return got * factors[:, h : h + 1] + pp[i, mid_far, :, h * HD : (h + 1) * HD]

            def write(h, tile):
                total[i, :, h * HD : (h + 1) * HD] = tile

            code_block(read, write, heads, seq)

        return add

    loads["q"].wait()

    @pl.loop(0, head_cols // 256)
    def _(j):
        span = pl.ds(pl.multiple_of(j * 256, 256), 256)
        part = dot(nb[...].reshape(4 * seq, rows_here), wq[:, span], plain)
        pp[0, :, :, span] = part.reshape(4, seq, 256)

    code(0)
    line_start(*line_of(0), line[0])

    def add_kv():
        relay_kv[...] = relay_kv[...] + pkv[mid_far]

    line_relay(*kv_args, line_kv, add_kv, relay_kv)

    fourth_hop(1)
    last_hop(1)
    loads["o"].wait()

    @pl.loop(0, head_cols // 256)
    def _(j):
        span = pl.ds(pl.multiple_of(j * 256, 256), 256)
        part = dot(x[1].reshape(4 * seq, rows_here), wo[span, :], crossed)
        pp[1, :, :, span] = part.reshape(4, seq, 256)

    code(1)
    line_start(*line_of(1), line[1])

    line_arrive(rkv, line_kv)
    own = pkv[z]
    for step in range(1, 4):
        own = own + rkv[lax.rem(z + step, 4)]
    kvg[t] = own.astype(jnp.bfloat16)
    at_kv = take(8)
    for step in range(1, 8):
        push(kvg.at[t], kvg.at[t], at_kv + step, at_kv + step, {"tensor": lax.rem(t + step, 8)})
    line_relay(*line_of(0), line[0], add_coded(0), total.at[0])
    line_relay(*line_of(1), line[1], add_coded(1), total.at[1])

    over = lax.broadcasted_iota(jnp.int32, (rows, count), 1)
    place = jnp.zeros((rows, 1), jnp.float32)
    row_at = lax.broadcasted_iota(jnp.int32, (rows, 1), 0)
    spot_of = row_at // 4
    prompt_of = row_at - 4 * spot_of
    for p in range(4):
        mark = (spot_of == over) & (prompt_of == p)
        found = jnp.where(mark, spots[p].astype(jnp.float32), 0.0)
        place = place + jnp.sum(found, axis=1, keepdims=True)
    place = place + seq * prompt_of.astype(jnp.float32)
    marks = lax.broadcasted_iota(jnp.int32, (rows, 4 * seq), 1).astype(jnp.float32)
    chosen = (marks == place).astype(jnp.bfloat16)
    norm_rows = jnp.zeros((rows, 1), jnp.float32)
    inside = lax.broadcasted_iota(jnp.int32, (rows, 128), 1).astype(jnp.float32)
    for p in range(4):
        hit = (inside + p * seq == place) & (inside < seq)
        norm_rows = norm_rows + jnp.sum(jnp.where(hit, norms[p][:1], 0.0), axis=1, keepdims=True)
    for j in range(0, rows_here, 512):
        block = x[0, :, :, j : j + 512].reshape(4 * seq, 512)
        scaled[:, j : j + 512] = dot(chosen, block, plain) * norm_rows

    def finish(i):
        line_arrive(arrived.at[i], line[i])
        factors = [scale_of(arrived[i, lax.rem(z + s, 4), :, heads * HD :]) for s in (1, 2, 3)]
        for h in range(heads):
            span = slice(h * HD, (h + 1) * HD)
            value = pp[i, z, :, span]
            for s in (1, 2, 3):
                got = arrived[i, lax.rem(z + s, 4), :, span].astype(jnp.int32)
                value = value + got.astype(jnp.float32) * factors[s - 1][:, h : h + 1]
            whole[i, :, span] = value.astype(jnp.bfloat16)

    finish(0)
    for step in range(1, 8):
        move(kvg.at[t], kvg.at[t], 0, at_kv + step, plane(1)).wait_recv()
    finish(1)

    own_spots = jnp.where(
        lax.broadcasted_iota(jnp.int32, (PAD, count), 0)
        == lax.broadcasted_iota(jnp.int32, (PAD, count), 1),
        suffix[...].astype(jnp.float32),
        0.0,
    )
    own_spots = jnp.sum(own_spots, axis=1, keepdims=True)
    real = lax.broadcasted_iota(jnp.int32, (PAD, 1), 0) < count
    own_spots = jnp.where(real, own_spots, -1.0)
    steps_iota = lax.broadcasted_iota(jnp.int32, (PAD, seq), 1).astype(jnp.float32)
    chooser = (steps_iota == own_spots).astype(jnp.bfloat16)
    causal = lax.broadcasted_iota(jnp.int32, (seq, seq), 1) <= lax.broadcasted_iota(
        jnp.int32, (seq, seq), 0
    )
    at_slots, slots_from = take(8), take(8)
    at_grads = take(12)

    def head_grads(h):
        span = slice(h * HD, (h + 1) * HD)
        queries, contexts = whole[0, :, span], whole[1, :, span]
        keys, values = kvg[h, :, :HD], kvg[h, :, HD:]
        logits = dot(queries, keys, crossed) * scale
        largest = jnp.max(jnp.where(causal, logits, -1e30), axis=-1, keepdims=True)
        raised = jnp.where(causal, jnp.exp(logits - largest), 0.0)
        probs = raised / jnp.sum(raised, axis=-1, keepdims=True)
        probs_low = probs.astype(jnp.bfloat16)
        prob_grad = dot(contexts, values, crossed)
        less = jnp.sum(prob_grad * probs, axis=-1, keepdims=True)
        logit_grad = (probs * (prob_grad - less) * scale).astype(jnp.bfloat16)
        logit_rows = dot(chooser, logit_grad, plain).astype(jnp.bfloat16)
        grads[z, :, span] = dot(logit_rows, keys, plain).astype(jnp.bfloat16)
        logit_cols = dot(chooser, logit_grad, crossed).astype(jnp.bfloat16)
        prob_cols = dot(chooser, probs_low, crossed).astype(jnp.bfloat16)
        slots[h, :24] = dot(logit_cols, queries, plain)[:24]
        slots[h, 24:] = dot(prob_cols, contexts, plain)[:24]


    def send_slots(h):
        return move(slots.at[h], slots_in.at[t], at_slots + h, slots_from + t, {"tensor": h})

    halves = 2
    head_parts = []
    for half in range(halves):
        group = range(half * heads // halves, (half + 1) * heads // halves)
        for h in group:
            head_grads(h)
        for h in group:

            @pl.when(t != h)
            def _():
                send_slots(h).start()

        part = grads.at[z, :, group.start * HD : group.stop * HD]
        head_parts.append(part)
        for step in (2, 1, 3):
            number = at_grads + 4 * half + step
            push(part, part, number, number, along(step))
    slots_in[t] = slots[t]
    for step in range(1, 8):
        source = lax.rem(t + step, 8)
        move(slots_in.at[t], slots_in.at[t], 0, slots_from + source, plane(1)).wait_recv()
    summed = slots_in[0]
    for j in range(1, 8):
        summed = summed + slots_in[j]
    filler = jnp.zeros((PAD - 24, HD), jnp.float32)
    key_rows = jnp.concatenate([summed[:24], filler], axis=0)
    value_rows = jnp.concatenate([summed[24:], filler], axis=0)
    grads[z, :, head_cols : head_cols + HD] = key_rows.astype(jnp.bfloat16)
    grads[z, :, head_cols + HD :] = value_rows.astype(jnp.bfloat16)
    tail_part = grads.at[z, :, head_cols:]
    for step in (2, 1, 3):
        push(tail_part, tail_part, at_grads + 8 + step, at_grads + 8 + step, along(step))
    for half in range(halves):
        for step in range(1, 4):
            part = head_parts[half]
            move(part, part, 0, at_grads + 4 * half + step, plane(1)).wait_recv()

    packed_at = lax.broadcasted_iota(jnp.int32, (rows, 4 * PAD), 1)
    packer = (packed_at == PAD * prompt_of + spot_of).astype(jnp.bfloat16)
    packed = dot(packer, grads[:, :, :head_cols].reshape(4 * PAD, head_cols), plain)
    packed = packed.astype(jnp.bfloat16)
    farthest = (3, 1, 2, 0)

    def owned(half, s):
        owner = 2 * near[s] + ((1 - core) if half == 0 else core)
        return pl.ds(pl.multiple_of(owner * slice_width, slice_width), slice_width)

    for half in range(2):
        for s in farthest:
            weighted[half, s] = dot(packed, wq[owned(half, s), :], crossed)
    for step in range(1, 4):
        move(tail_part, tail_part, 0, at_grads + 8 + step, plane(1)).wait_recv()
    packed = dot(packer, grads[:, :, head_cols:].reshape(4 * PAD, 2 * HD), plain)
    packed = packed.astype(jnp.bfloat16)
    inner = jnp.zeros((rows, 128), jnp.float32)
    at_pair, at_shares = take(4), take(4)
    for half in range(2):
        for s in farthest:
            span = owned(half, s)
            part = weighted[half, s] + dot(packed, wkv[span, :], crossed)
            part = part * gain_row[:, span]
            product = part * scaled[:, span]
            for j in range(0, slice_width, 128):
                inner = inner + product[:, j : j + 128]
            weighted[half, s] = part
            if half == 0:
                push(weighted.at[0, s], pair_in.at[s], at_pair + s, at_pair + s, {"tensor": pair})
    for s in farthest:
        move(pair_in.at[s], pair_in.at[s], 0, at_pair + s, {"tensor": pair}).wait_recv()
        weighted[1, s] = weighted[1, s] + pair_in[s]
        if s:
            push(weighted.at[1, s], shares.at[s - 1], at_shares + s, at_shares + s, plane(s))
    inner = jnp.sum(inner, axis=1, keepdims=True)
    inner_in[t] = jnp.broadcast_to(lay_row(inner, 128), (8, 128))
    at_inner = take(8)
    for step in range(1, 8):
        push(
            inner_in.at[t],
            inner_in.at[t],
            at_inner + step,
            at_inner + step,
            {"tensor": lax.rem(t + step, 8)},
        )
    for step in range(1, 8):
        move(inner_in.at[t], inner_in.at[t], 0, at_inner + step, plane(1)).wait_recv()
    inner = inner_in[0]
    for j in range(1, 8):
        inner = inner + inner_in[j]
    inner_z[z] = inner
    at_inner_z = take(4)
    for step in range(1, 4):
        push(inner_z.at[z], inner_z.at[z], at_inner_z + step, at_inner_z + step, along(step))
    for s in (1, 2, 3):
        move(shares.at[s - 1], shares.at[s - 1], 0, at_shares + s, plane(1)).wait_recv()
    own = weighted[1, 0] + shares[0] + shares[1] + shares[2]
    for step in range(1, 4):
        move(inner_z.at[z], inner_z.at[z], 0, at_inner_z + step, plane(1)).wait_recv()
    inner = (inner_z[0] + inner_z[1] + inner_z[2] + inner_z[3])[:1]
    inner = pick_column(inner, rows) / width

    here = pl.ds(pl.multiple_of(t * slice_width, slice_width), slice_width)
    suffix_grads[z, :, here] = (norm_rows * (own - scaled[:, here] * inner)).astype(jnp.bfloat16)

    def grad_of(p, chip_index, core_index):
        first = (2 * chip_index + core_index) * slice_width
        return suffix_grads.at[p, :, pl.ds(pl.multiple_of(first, slice_width), slice_width)]

    at_z = take(4)
    spread = [take(4) for _ in range(4)]
    doubled = [take(4) for _ in range(4)]
    mine_now = grad_of(z, chip, core)
    for step in (2, 1, 3):
        push(mine_now, mine_now, at_z + step, at_z + step, along(step))

    def to_plane(step):
        block = grad_of(lax.rem(z - step + 4, 4), chip, core)
        if step:
            move(block, block, 0, at_z + step, plane(1)).wait_recv()
        for s in (3, 1, 2):
            push(block, block, spread[step] + s, spread[step] + s, plane(s))
        push(block, block, spread[step], spread[step], {"tensor": pair})

    def to_pair(step):
        p = lax.rem(z - step + 4, 4)
        for s in (1, 2, 3):
            block = grad_of(p, near[s], core)
            move(block, block, 0, spread[step] + s, plane(s)).wait_recv()
            push(block, block, doubled[step] + s, doubled[step] + s, {"tensor": pair})

    def from_pair(step):
        p = lax.rem(z - step + 4, 4)
        for s in range(4):
            block = grad_of(p, near[s], 1 - core)
            number = doubled[step] + s if s else spread[step]
            move(block, block, 0, number, {"tensor": pair}).wait_recv()

    def multiply(step, half):
        p = lax.rem(z - step + 4, 4)
        features = pl.ds(pl.multiple_of(p * rows_here, rows_here), rows_here)
        wide = vocab.shape[0] // 2
        span = pl.ds(half * wide, wide)
        part = dot(suffix_grads[p], table[span, features], crossed)
        if step != order[0]:
            part = part + partial[:, span]
        if step != order[-1]:
            partial[:, span] = part
            return
        part = jnp.where(banned[:, span] == 1, 0.0, -part)
        for n in range(count):
            out[n, :, span] = part[4 * n : 4 * n + 4]

    to_plane(0)
    to_plane(1)
    to_pair(0)
    for c in range(chunks):
        load_table(c).wait()
    from_pair(0)
    multiply(0, 0)
    to_plane(3)
    to_plane(2)
    to_pair(1)
    multiply(0, 1)
    from_pair(1)
    multiply(1, 0)
    to_pair(3)
    multiply(1, 1)
    from_pair(3)
    multiply(3, 0)
    to_pair(2)
    multiply(3, 1)
    from_pair(2)
    multiply(2, 0)
    multiply(2, 1)

    for copy in sent:
        copy.wait_send()
    for h in range(heads):

        @pl.when(t != h)
        def _():
            send_slots(h).wait_send()

    for a in range(2):
        for s in range(4):

            @pl.when(near[s] != z)
            def _():
                block = x.at[a, z, rows_of(chip), own_cols]
                move(block, block, across[a] + s, 0, {"prompt": near[s]}).wait_send()

    line_sent(*kv_args, line_kv, relay_kv)
    for i in range(2):
        line_sent(*line_of(i), line[i], total.at[i])


def fused(
    embeds,
    norm_gain,
    query_weight,
    key_weight,
    value_weight,
    out_weight,
    out_grad,
    suffix_pos,
    vocab_table,
    banned,
):
    seq, cols = embeds.shape[1:]
    rows_here, head_cols = query_weight.shape
    count = suffix_pos.shape[1]
    vocab_here, width = vocab_table.shape
    heads = head_cols // HD
    rows = 4 * count
    slice_width = rows_here // 8
    low, full, short = jnp.bfloat16, jnp.float32, jnp.int16
    coded = head_cols + HD
    local = pl.BlockSpec(memory_space=pltpu.VMEM)
    apart = pl.BlockSpec(memory_space=pl.ANY)
    scratch = [
        ((rows_here, head_cols), low),
        ((rows_here, 2 * HD), low),
        ((head_cols, rows_here), low),
        (vocab_table.shape, low),
        ((seq, cols), low),
        ((2, 3, seq // 4, cols), low),
        ((2, 4, seq, rows_here), low),
        ((8, 8, 128), full),
        ((4, 8, 128), full),
        ((4, 1, count), jnp.int32),
        ((4, seq, rows_here), low),
        ((4, seq, 2 * HD), full),
        ((4, seq, 2 * HD), full),
        ((seq, 2 * HD), full),
        ((2, 4, seq, head_cols), full),
        ((2, 4, seq, coded), short),
        ((2, 4, seq, coded), short),
        ((2, seq, coded), short),
        ((2, seq, coded), short),
        ((8, seq, 2 * HD), low),
        ((2, seq, head_cols), low),
        ((8, 48, HD), full),
        ((8, 48, HD), full),
        ((4, PAD, head_cols + 2 * HD), low),
        ((rows, rows_here), full),
        ((2, 4, rows, slice_width), full),
        ((4, rows, slice_width), full),
        ((3, rows, slice_width), full),
        ((8, 8, 128), full),
        ((4, 8, 128), full),
        ((4, rows, rows_here), low),
        ((rows, vocab_here), full),
        ((1, rows_here), full),
    ]
    scores = pl.pallas_call(
        fused_kernel,
        out_shape=jax.ShapeDtypeStruct((count, 4, vocab_here), full),
        in_specs=[apart, apart, local, apart, apart, apart, apart, local, apart, local],
        out_specs=local,
        scratch_shapes=[pltpu.VMEM(shape, dtype) for shape, dtype in scratch]
        + [
            pltpu.SemaphoreType.DMA((SEMS,)),
            pltpu.SemaphoreType.DMA((SEMS,)),
            pltpu.SemaphoreType.DMA((8 + vocab_here // CHUNK,)),
            pltpu.SemaphoreType.DMA((2,)),
        ],
        compiler_params=pltpu.CompilerParams(
            collective_id=11, has_side_effects=True, vmem_limit_bytes=60 << 20
        ),
    )(
        embeds,
        out_grad,
        norm_gain,
        query_weight,
        key_weight,
        value_weight,
        out_weight,
        suffix_pos,
        vocab_table,
        banned.reshape(1, -1),
    )
    return scores.transpose(1, 0, 2)


def fits(mesh_sizes, arrays):
    embeds, query_weight, key_weight, suffix_pos, vocab_table = arrays
    return (
        mesh_sizes == (4, 8)
        and embeds.shape[1] == 64
        and query_weight.shape[1] == 8 * HD
        and key_weight.shape[1] == HD
        and query_weight.shape[0] == 2 * embeds.shape[2]
        and query_weight.shape[0] % 2048 == 0
        and suffix_pos.shape[1] == 20
        and vocab_table.shape[0] % CHUNK == 0
    )


def part_of(*args):
    sizes = (lax.axis_size("prompt"), lax.axis_size("tensor"))
    if fits(sizes, (args[0], args[2], args[3], args[7], args[8])):
        return fused(*args)
    return on_device(*args)


def solution(mesh):
    return jax.shard_map(
        part_of,
        mesh=mesh,
        in_specs=(
            P("prompt", None, "tensor"),
            P(),
            P("prompt", "tensor"),
            P("prompt", "tensor"),
            P("prompt", "tensor"),
            P("tensor", "prompt"),
            P("prompt", None, "tensor"),
            P("prompt", None),
            P(("prompt", "tensor"), None),
            P(("prompt", "tensor")),
        ),
        out_specs=P(None, None, ("prompt", "tensor")),
        check_vma=False,
    )
```

```python
import functools
import math

import jax
import jax.numpy as jnp
from jax import lax
from jax.experimental import pallas as pl
from jax.experimental.pallas import tpu as pltpu
from jax.sharding import PartitionSpec as P

KVH = 8
HD = 128


EPSILON = 1e-05


def exchange_kernel(axis, count, spread, *refs):
    arrays = len(spread)
    sources, targets = refs[:arrays], refs[arrays : 2 * arrays]
    send_sem, recv_sem, own_sem = refs[2 * arrays :]
    here = lax.axis_index(axis)

    def block(i, to):
        return sources[i].at[to] if spread[i] else sources[i]

    kept = []
    for i in range(arrays):
        copy = pltpu.make_async_copy(block(i, here), targets[i].at[here], own_sem.at[i])
        copy.start()
        kept.append(copy)
    barrier = pltpu.get_barrier_semaphore()
    for step in range(1, count):
        peer = lax.rem(here + step, count)
        pl.semaphore_signal(
            barrier, inc=1, device_id={axis: peer}, device_id_type=pl.DeviceIdType.MESH
        )
    pl.semaphore_wait(barrier, count - 1)
    copies = []
    for step in range(1, count):
        peer = lax.rem(here + step, count)
        for i in range(arrays):
            copy = pltpu.make_async_remote_copy(
                src_ref=block(i, peer),
                dst_ref=targets[i].at[here],
                send_sem=send_sem.at[i, step - 1],
                recv_sem=recv_sem.at[i, step - 1],
                device_id={axis: peer},
                device_id_type=pl.DeviceIdType.MESH,
            )
            copy.start()
            copies.append(copy)
    for copy in kept + copies:
        copy.wait()


def exchange(axis, number, *operands):
    count = lax.axis_size(axis)
    arrays = [array for array, _ in operands]
    spread = tuple(each for _, each in operands)
    shapes = [
        jax.ShapeDtypeStruct(((count,) + (a.shape[1:] if each else a.shape)), a.dtype)
        for a, each in operands
    ]
    space = pl.BlockSpec(memory_space=pltpu.VMEM)
    sems = pltpu.SemaphoreType.DMA((len(arrays), count - 1))
    return pl.pallas_call(
        functools.partial(exchange_kernel, axis, count, spread),
        out_shape=shapes,
        in_specs=[space] * len(arrays),
        out_specs=[space] * len(arrays),
        scratch_shapes=[sems, sems, pltpu.SemaphoreType.DMA((len(arrays),))],
        compiler_params=pltpu.CompilerParams(
            collective_id=number, has_side_effects=True, vmem_limit_bytes=40 << 20
        ),
    )(*arrays)


def dot_f32(spec, a, b):
    return jnp.einsum(spec, a, b, preferred_element_type=jnp.float32)


MESH = pl.DeviceIdType.MESH


def greet(axis, peers):
    barrier = pltpu.get_barrier_semaphore()
    for peer in peers:
        pl.semaphore_signal(barrier, inc=1, device_id={axis: peer}, device_id_type=MESH)
    pl.semaphore_wait(barrier, len(peers))


def gather_kernel(axis, count, arrays, *refs):
    sources, targets = refs[:arrays], refs[arrays : 2 * arrays]
    send_sem, recv_sem, own_sem = refs[2 * arrays :]
    here = lax.axis_index(axis)
    chips = count // 2
    chip, core = here // 2, lax.rem(here, 2)
    pair = 2 * chip + (1 - core)
    kept = []
    for i in range(arrays):
        copy = pltpu.make_async_copy(sources[i], targets[i].at[here], own_sem.at[i])
        copy.start()
        kept.append(copy)

    def push(i, source, slot, number, peer):
        return pltpu.make_async_remote_copy(
            src_ref=source,
            dst_ref=targets[i].at[slot],
            send_sem=send_sem.at[i, number],
            recv_sem=recv_sem.at[i, number],
            device_id={axis: peer},
            device_id_type=MESH,
        )

    others = [2 * lax.rem(chip + step, chips) + core for step in range(1, chips)]
    greet(axis, others + [pair])
    first = []
    for step in range(1, chips):
        for i in range(arrays):
            copy = push(i, sources[i], here, step, others[step - 1])
            copy.start()
            first.append(copy)
    rest = []
    for i in range(arrays):
        copy = push(i, sources[i], here, 0, pair)
        copy.start()
        rest.append(copy)
    for step in range(1, chips):
        slot = 2 * lax.rem(chip + chips - step, chips) + core
        for i in range(arrays):
            first[(step - 1) * arrays + i].wait_recv()
            copy = push(i, targets[i].at[slot], slot, chips - 1 + step, pair)
            copy.start()
            rest.append(copy)
    for copy in first:
        copy.wait_send()
    for copy in kept + rest:
        copy.wait()


def gather(axis, number, *arrays):
    count = lax.axis_size(axis)
    shapes = [jax.ShapeDtypeStruct((count,) + a.shape, a.dtype) for a in arrays]
    space = pl.BlockSpec(memory_space=pltpu.VMEM)
    sems = pltpu.SemaphoreType.DMA((len(arrays), count - 1))
    return pl.pallas_call(
        functools.partial(gather_kernel, axis, count, len(arrays)),
        out_shape=shapes,
        in_specs=[space] * len(arrays),
        out_specs=[space] * len(arrays),
        scratch_shapes=[sems, sems, pltpu.SemaphoreType.DMA((len(arrays),))],
        compiler_params=pltpu.CompilerParams(
            collective_id=number, has_side_effects=True, vmem_limit_bytes=40 << 20
        ),
    )(*arrays)


def line_kernel(axis, source, target, relay, send_sem, recv_sem, own_sem):
    here = lax.axis_index(axis)
    own = pltpu.make_async_copy(source.at[here], target.at[here], own_sem.at[0])
    own.start()
    greet(axis, [lax.rem(here + step, 4) for step in range(1, 4)])

    def push(block, slot, number, peer, into=None):
        return pltpu.make_async_remote_copy(
            src_ref=block,
            dst_ref=target.at[slot] if into is None else into,
            send_sem=send_sem.at[number],
            recv_sem=recv_sem.at[slot if into is None else 4],
            device_id={axis: peer},
            device_id_type=MESH,
        )

    for role in range(4):
        far = 3 if role < 2 else 0
        middle = 1 if role < 2 else 2
        across = 3 - middle

        @pl.when(here == role)
        def _():
            if role == middle:
                sent = [
                    push(source.at[across], role, 0, across),
                    push(source.at[3 - far], role, 1, 3 - far),
                ]
                for copy in sent:
                    copy.start()
                total = push(relay, role, 2, far)
                push(source.at[far], role, 3, far, relay).wait_recv()
                relay[...] = relay[...] + source[far]
                total.start()
                sent.append(total)
                arriving = [0, across, 3]
            else:
                handed = push(source.at[far], role, 0, middle, relay)
                handed.start()
                target[far] = jnp.zeros_like(target[far])
                handed.wait_send()
                sent = [
                    push(source.at[across], role, 1, across),
                    push(source.at[middle], role, 2, middle),
                ]
                for copy in sent:
                    copy.start()
                arriving = [1, 2]
            for slot in arriving:
                push(source.at[slot], slot, 3, slot).wait_recv()
            for copy in sent:
                copy.wait_send()

    own.wait()


def line_exchange(axis, number, blocks):
    if lax.axis_size(axis) != 4:
        return exchange(axis, number, (blocks, True))[0]
    space = pl.BlockSpec(memory_space=pltpu.VMEM)
    return pl.pallas_call(
        functools.partial(line_kernel, axis),
        out_shape=jax.ShapeDtypeStruct(blocks.shape, blocks.dtype),
        in_specs=[space],
        out_specs=space,
        scratch_shapes=[
            pltpu.VMEM(blocks.shape[1:], blocks.dtype),
            pltpu.SemaphoreType.DMA((4,)),
            pltpu.SemaphoreType.DMA((5,)),
            pltpu.SemaphoreType.DMA((1,)),
        ],
        compiler_params=pltpu.CompilerParams(
            collective_id=number, has_side_effects=True, vmem_limit_bytes=40 << 20
        ),
    )(blocks)


CHUNK = 512


def score_kernel(
    axis, count, part, vocab, scores, got, flat, table, send_sem, recv_sem, own_sem, load_sem
):
    def load(c):
        span = pl.ds(pl.multiple_of(c * CHUNK, CHUNK), CHUNK)
        return pltpu.make_async_copy(vocab.at[span], table.at[span], load_sem.at[c])

    chunks = vocab.shape[0] // CHUNK
    for c in range(chunks):
        load(c).start()
    gather_kernel(axis, count, 1, part, got, send_sem, recv_sem, own_sem)
    wide = part.shape[2]
    for p in range(part.shape[0]):
        for t in range(count):
            start = (p * count + t) * wide
            flat[:, start : start + wide] = got[t, p]

    @pl.loop(0, chunks)
    def _(c):
        load(c).wait()
        span = pl.ds(pl.multiple_of(c * CHUNK, CHUNK), CHUNK)
        scores[:, span] = -lax.dot_general(
            flat[...],
            table[span, :],
            (((1,), (1,)), ((), ())),
            preferred_element_type=jnp.float32,
        )


def gather_score(axis, number, part, vocab):
    count = lax.axis_size(axis)
    n_prompt, rows, wide = part.shape
    vocab_here, width = vocab.shape
    if wide % 128 or vocab_here % CHUNK or rows % 16:
        (part,) = gather(axis, number, part)
        return -dot_f32("rd,vd->rv", part.transpose(2, 1, 0, 3).reshape(rows, width), vocab)
    sems = pltpu.SemaphoreType.DMA((1, count - 1))
    return pl.pallas_call(
        functools.partial(score_kernel, axis, count),
        out_shape=jax.ShapeDtypeStruct((rows, vocab_here), jnp.float32),
        in_specs=[pl.BlockSpec(memory_space=pltpu.VMEM), pl.BlockSpec(memory_space=pl.ANY)],
        out_specs=pl.BlockSpec(memory_space=pltpu.VMEM),
        scratch_shapes=[
            pltpu.VMEM((count,) + part.shape, part.dtype),
            pltpu.VMEM((rows, width), part.dtype),
            pltpu.VMEM(vocab.shape, vocab.dtype),
            sems,
            sems,
            pltpu.SemaphoreType.DMA((1,)),
            pltpu.SemaphoreType.DMA((vocab_here // CHUNK,)),
        ],
        compiler_params=pltpu.CompilerParams(
            collective_id=number, has_side_effects=True, vmem_limit_bytes=52 << 20
        ),
    )(part, vocab)


def on_device(
    embeds,
    norm_gain,
    query_weight,
    key_weight,
    value_weight,
    out_weight,
    out_grad,
    suffix_pos,
    vocab_table,
    banned,
):
    n_prompt = lax.axis_size("prompt")
    n_tensor = lax.axis_size("tensor")
    here_prompt = lax.axis_index("prompt")
    here_tensor = lax.axis_index("tensor")
    seq_len = embeds.shape[1]
    suffix_count = suffix_pos.shape[1]
    width = embeds.shape[2] * n_tensor
    rows_here, head_cols = query_weight.shape
    key_cols = key_weight.shape[1]
    heads_here = head_cols // HD
    slice_width = rows_here // n_tensor
    logit_scale = 1.0 / math.sqrt(HD)

    split_rows = seq_len // n_tensor
    ratio = n_tensor // n_prompt
    feature_cols = embeds.shape[2]
    both = jnp.concatenate(
        [
            embeds.reshape(n_tensor, split_rows, feature_cols),
            out_grad.reshape(n_tensor, split_rows, feature_cols),
        ],
        axis=1,
    )
    (both,) = exchange("tensor", 0, (both, True))
    own = both[:, :split_rows].astype(jnp.float32)
    inverse_norm = lax.rsqrt(jnp.sum(own * own, axis=(0, 2))[:, None] / width + EPSILON)
    inverse_norm = jnp.broadcast_to(inverse_norm, (split_rows, 128))
    both = both.reshape(n_prompt, ratio, 2 * split_rows, feature_cols)
    both, inverse_norm, suffix_all = exchange(
        "prompt", 1, (both, True), (inverse_norm, False), (suffix_pos, False)
    )
    both, inverse_norm = gather("tensor", 2, both, inverse_norm)
    suffix_all = suffix_all.reshape(n_prompt, suffix_count)
    both = both.reshape(n_tensor, n_prompt, ratio, 2, split_rows, feature_cols)
    both = both.transpose(3, 1, 0, 4, 2, 5).reshape(2, n_prompt, seq_len, rows_here)
    embeds, out_grad = both[0], both[1]
    inverse_norm = inverse_norm[..., :1].transpose(1, 0, 2, 3).reshape(n_prompt, seq_len, 1)
    embeds_float = embeds.astype(jnp.float32)
    gain_rows = lax.dynamic_slice_in_dim(norm_gain, here_prompt * rows_here, rows_here, 0)
    gain_rows = gain_rows.astype(jnp.float32)
    normed = (embeds_float * inverse_norm * gain_rows).astype(jnp.bfloat16)

    parts = jnp.concatenate(
        [
            dot_f32("psd,dc->psc", normed, query_weight),
            dot_f32("psd,dc->psc", normed, key_weight),
            dot_f32("psd,dc->psc", normed, value_weight),
            dot_f32("psd,cd->psc", out_grad, out_weight),
        ],
        axis=2,
    )
    parts = line_exchange("prompt", 3, parts)
    whole = jnp.sum(parts, axis=0).astype(jnp.bfloat16)
    contexts = whole[:, head_cols + 2 * key_cols :]
    contexts = contexts.reshape(seq_len, heads_here, HD)
    queries = whole[:, :head_cols].reshape(seq_len, heads_here, HD)
    (key_values,) = gather("tensor", 4, whole[:, head_cols : head_cols + 2 * key_cols])
    key_values = key_values.reshape(n_tensor, seq_len, 2, key_cols).transpose(2, 1, 0, 3)
    key_values = key_values.reshape(2, seq_len, KVH * HD)
    fold = min(heads_here, KVH)
    first = ((here_tensor * heads_here) % KVH) * HD
    if fold < KVH:
        key_values = lax.dynamic_slice_in_dim(key_values, first, fold * HD, 2)
    key_values = key_values.reshape(2, seq_len, fold, HD)
    if heads_here > fold:
        key_values = jnp.tile(key_values, (1, 1, heads_here // fold, 1))
    keys, values = key_values[0], key_values[1]

    logits = dot_f32("qhd,khd->hqk", queries, keys) * logit_scale
    row_index = lax.broadcasted_iota(jnp.int32, (seq_len, seq_len), 0)
    col_index = lax.broadcasted_iota(jnp.int32, (seq_len, seq_len), 1)
    causal = col_index <= row_index
    largest = jnp.max(jnp.where(causal, logits, -1e30), axis=-1, keepdims=True)
    raised = jnp.where(causal, jnp.exp(logits - largest), 0.0)
    probs = raised / jnp.sum(raised, axis=-1, keepdims=True)
    probs_low = probs.astype(jnp.bfloat16)
    prob_grad = dot_f32("qhd,khd->hqk", contexts, values)
    logit_grad = (
        probs * (prob_grad - jnp.sum(prob_grad * probs, axis=-1, keepdims=True)) * logit_scale
    ).astype(jnp.bfloat16)
    steps_iota = lax.broadcasted_iota(jnp.int32, (suffix_count, seq_len), 1)
    chooser = (steps_iota == suffix_pos[0][:, None]).astype(jnp.bfloat16)
    logit_rows = dot_f32("ns,hsk->hnk", chooser, logit_grad).astype(jnp.bfloat16)
    query_grad = dot_f32("hnk,khd->nhd", logit_rows, keys).astype(jnp.bfloat16)
    query_grad = query_grad.reshape(suffix_count, head_cols)
    logit_cols = dot_f32("hqk,nk->hnq", logit_grad, chooser).astype(jnp.bfloat16)
    prob_cols = dot_f32("hqk,nk->hnq", probs_low, chooser).astype(jnp.bfloat16)
    key_each = dot_f32("hnq,qhd->nhd", logit_cols, queries)
    value_each = dot_f32("hnq,qhd->nhd", prob_cols, contexts)
    slots = jnp.stack([key_each, value_each])
    slots = slots.reshape(2, suffix_count, heads_here // fold, fold * HD).sum(axis=2)
    if fold < KVH:
        slots = lax.dynamic_update_slice_in_dim(
            jnp.zeros((2, suffix_count, KVH * HD), jnp.float32), slots, first, 2
        )
    slots = slots.reshape(2 * suffix_count, n_tensor, key_cols).transpose(1, 0, 2)
    (grads,) = exchange("tensor", 5, (slots, True))
    grads = jnp.sum(grads, axis=0).astype(jnp.bfloat16).reshape(2, suffix_count, key_cols)
    grads = jnp.concatenate([query_grad, grads[0], grads[1]], axis=1)
    (grads,) = exchange("prompt", 6, (grads, False))
    rows = n_prompt * suffix_count
    grads = grads.reshape(rows, head_cols + 2 * key_cols)
    steps_iota = lax.broadcasted_iota(jnp.int32, (n_prompt, suffix_count, seq_len), 2)
    chooser_all = steps_iota == suffix_all[:, :, None]
    embed_rows = dot_f32("pns,psd->pnd", chooser_all.astype(jnp.bfloat16), embeds)
    norm_rows = jnp.sum(
        jnp.where(chooser_all, inverse_norm[:, None, :, 0], 0.0), axis=-1, keepdims=True
    )
    scaled = (embed_rows * norm_rows).reshape(rows, rows_here)
    norm_rows = norm_rows.reshape(rows, 1)
    branch = dot_f32("nc,dc->nd", grads[:, :head_cols], query_weight)
    branch = branch + dot_f32("nc,dc->nd", grads[:, head_cols : head_cols + key_cols], key_weight)
    branch = branch + dot_f32("nc,dc->nd", grads[:, head_cols + key_cols :], value_weight)
    branch = branch * gain_rows
    inner = jnp.sum(branch * scaled, axis=-1)
    branch = branch.reshape(rows, n_tensor, slice_width).transpose(1, 0, 2)
    share, inner = exchange("tensor", 7, (branch, True), (inner[None, :], False))
    weighted = jnp.sum(share, axis=0)
    (inner,) = exchange("prompt", 8, (jnp.sum(inner, axis=0), False))
    inner = jnp.sum(inner, axis=0).reshape(rows, 1) / width
    scaled = lax.dynamic_slice_in_dim(scaled, here_tensor * slice_width, slice_width, 1)
    suffix_grad = (norm_rows * (weighted - scaled * inner)).astype(jnp.bfloat16)
    (suffix_grad,) = exchange("prompt", 9, (suffix_grad, False))
    scores = gather_score("tensor", 10, suffix_grad, vocab_table)
    scores = scores.reshape(n_prompt, suffix_count, vocab_table.shape[0])
    return jnp.where(banned[None, None, :] == 1, 0.0, scores)


PAD = 32
TINY = 1e-30
FULL = 32767.0
SEMS = 224


def pick_column(row, rows):
    wide = row.shape[1]
    down = lax.broadcasted_iota(jnp.int32, (rows, wide), 0)
    along = lax.broadcasted_iota(jnp.int32, (rows, wide), 1)
    return jnp.sum(jnp.where(down == along, row, 0.0), axis=1, keepdims=True)


def lay_row(column, wide):
    rows = column.shape[0]
    down = lax.broadcasted_iota(jnp.int32, (rows, wide), 0)
    along = lax.broadcasted_iota(jnp.int32, (rows, wide), 1)
    return jnp.sum(jnp.where(down == along, column, 0.0), axis=0, keepdims=True)


def lane_sums(values):
    total = values[:, :128]
    for j in range(128, values.shape[1], 128):
        total = total + values[:, j : j + 128]
    return jnp.sum(total, axis=1, keepdims=True)


def code_block(read, write, heads, rows):
    lanes = lax.broadcasted_iota(jnp.int32, (rows, HD), 1)
    powers = jnp.zeros((rows, HD), jnp.float32)
    for h in range(heads):
        block = read(h)
        peak = jnp.max(jnp.abs(block), axis=1, keepdims=True)
        power = jnp.floor(jnp.log2(jnp.maximum(peak, TINY))) + 1.0
        fixed = jnp.floor(block * (jnp.exp2(-power) * FULL) + 0.5)
        fixed = jnp.clip(fixed, -FULL, FULL)
        write(h, fixed.astype(jnp.int32).astype(jnp.int16))
        powers = jnp.where(lanes == h, power, powers)
    write(heads, powers.astype(jnp.int32).astype(jnp.int16))


def scale_of(tile):
    return jnp.exp2(tile.astype(jnp.int32).astype(jnp.float32)) * (1.0 / FULL)


def fused_kernel(
    embeds,
    out_grad,
    gain,
    query_weight,
    key_weight,
    value_weight,
    out_weight,
    suffix,
    vocab,
    banned,
    out,
    wq,
    wkv,
    wo,
    table,
    mine,
    stage,
    x,
    sums,
    norms,
    spots,
    nb,
    pkv,
    rkv,
    relay_kv,
    pp,
    coded,
    arrived,
    relay,
    total,
    kvg,
    whole,
    slots,
    slots_in,
    grads,
    scaled,
    weighted,
    pair_in,
    shares,
    inner_in,
    inner_z,
    suffix_grads,
    partial,
    gain_row,
    gain_all,
    barred,
    send_sem,
    recv_sem,
    load_sem,
    own_sem,
):
    z = lax.axis_index("prompt")
    t = lax.axis_index("tensor")
    chip, core = t // 2, lax.rem(t, 2)
    pair = 2 * chip + (1 - core)
    chip_y, chip_x = chip // 2, lax.rem(chip, 2)
    near = [
        chip,
        2 * chip_y + (1 - chip_x),
        2 * (1 - chip_y) + chip_x,
        2 * (1 - chip_y) + (1 - chip_x),
    ]
    seq, cols = embeds.shape[1], embeds.shape[2]
    width = gain.shape[0]
    rows_here, head_cols = query_weight.shape
    heads = head_cols // HD
    count = suffix.shape[1]
    rows = 4 * count
    quarter = seq // 4
    slice_width = rows_here // 8
    scale = 1.0 / math.sqrt(HD)
    dot = functools.partial(lax.dot_general, preferred_element_type=jnp.float32)
    plain = (((1,), (0,)), ((), ()))
    crossed = (((1,), (1,)), ((), ()))

    chunks = vocab.shape[0] // CHUNK

    def load_table(c):
        span = pl.ds(pl.multiple_of(c * CHUNK, CHUNK), CHUNK)
        return pltpu.make_async_copy(vocab.at[span], table.at[span], load_sem.at[8 + c])

    loads = {
        "g": pltpu.make_async_copy(gain, gain_all, load_sem.at[5]),
        "b": pltpu.make_async_copy(banned, barred, load_sem.at[6]),
        "s": pltpu.make_async_copy(suffix, spots.at[z], load_sem.at[7]),
        "e": pltpu.make_async_copy(embeds.at[0], mine, load_sem.at[0]),
        "k": pltpu.make_async_copy(key_weight, wkv.at[:, :HD], load_sem.at[1]),
        "v": pltpu.make_async_copy(value_weight, wkv.at[:, HD:], load_sem.at[2]),
        "q": pltpu.make_async_copy(query_weight, wq, load_sem.at[3]),
        "o": pltpu.make_async_copy(out_weight, wo, load_sem.at[4]),
    }
    for name in "egbs":
        loads[name].start()

    barrier = pltpu.get_barrier_semaphore()
    for step in range(1, 8):
        pl.semaphore_signal(
            barrier, inc=1, device_id={"tensor": lax.rem(t + step, 8)}, device_id_type=MESH
        )
    for step in range(1, 4):
        pl.semaphore_signal(
            barrier, inc=1, device_id={"prompt": lax.rem(z + step, 4)}, device_id_type=MESH
        )
    pl.semaphore_wait(barrier, 10)

    used = [0]
    sent = []

    def take(number=1):
        used[0] += number
        assert used[0] <= SEMS
        return used[0] - number

    def move(source, target, s, r, device):
        return pltpu.make_async_remote_copy(
            src_ref=source,
            dst_ref=target,
            send_sem=send_sem.at[s],
            recv_sem=recv_sem.at[r],
            device_id=device,
            device_id_type=MESH,
        )

    def push(source, target, s, r, device):
        copy = move(source, target, s, r, device)
        copy.start()
        sent.append(copy)

    def plane(s, other=False):
        return {"tensor": 2 * near[s] + ((1 - core) if other else core)}

    def along(step):
        return {"prompt": lax.rem(z + step, 4)}

    def rows_of(chip_index):
        return pl.ds(pl.multiple_of(quarter * chip_index, quarter), quarter)

    sources = (embeds.at[0], out_grad.at[0])
    own_cols = pl.ds(pl.multiple_of(core * cols, 128), cols)
    pair_cols = pl.ds(pl.multiple_of((1 - core) * cols, 128), cols)

    hop = [take(4) for _ in range(2)]

    def first_hop(a):
        for s in (3, 1, 2):
            push(
                sources[a].at[rows_of(near[s])], stage.at[a, s - 1], hop[a] + s, hop[a] + s, plane(s)
            )

    first_hop(0)
    at_spots = take(4)
    for step in range(1, 4):
        push(suffix, spots.at[z], at_spots + step, at_spots + step, along(step))

    loads["e"].wait()
    square = jnp.zeros((seq, 128), jnp.float32)
    for j in range(0, cols, 128):
        block = mine[:, j : j + 128].astype(jnp.float32)
        square = square + block * block
    square = jnp.sum(square, axis=1, keepdims=True)
    sums[t] = jnp.broadcast_to(lay_row(square, 128), (8, 128))
    at_sums = take(8)
    for step in range(1, 8):
        push(
            sums.at[t], sums.at[t], at_sums + step, at_sums + step, {"tensor": lax.rem(t + step, 8)}
        )

    for name in "kvqo":
        loads[name].start()

    across = [take(4) for _ in range(2)]
    across_in = [take(4) for _ in range(2)]

    def second_hop(a):
        for s in range(4):
            if s == 0:
                block = sources[a].at[rows_of(chip)]
            else:
                move(stage.at[a, s - 1], stage.at[a, s - 1], 0, hop[a] + s, plane(s)).wait_recv()
                block = stage.at[a, s - 1]
            target = x.at[a, z, rows_of(chip), own_cols]

            @pl.when(near[s] == z)
            def _():
                copy = pltpu.make_async_copy(block, target, own_sem.at[a])
                copy.start()
                copy.wait()

            @pl.when(near[s] != z)
            def _():
                move(block, target, across[a] + s, across_in[a] + z, {"prompt": near[s]}).start()

    second_hop(0)
    first_hop(1)
    for step in range(1, 8):
        move(sums.at[t], sums.at[t], 0, at_sums + step, plane(1)).wait_recv()
    square = sums[0]
    for j in range(1, 8):
        square = square + sums[j]
    norms[z] = lax.rsqrt(square / width + EPSILON)
    at_norms = take(4)
    for step in range(1, 4):
        push(norms.at[z], norms.at[z], at_norms + step, at_norms + step, along(step))

    order = (0, 1, 3, 2)
    third = [[take(4) for _ in range(4)] for _ in range(2)]
    fourth = [[take(4) for _ in range(4)] for _ in range(2)]

    def third_hop(a):
        for step in order:
            p = lax.rem(z + step, 4)
            block = x.at[a, p, rows_of(chip), own_cols]
            if step:
                move(block, block, 0, across_in[a] + p, plane(1)).wait_recv()
            for s in (3, 1, 2):
                push(block, block, third[a][step] + s, third[a][step] + s, plane(s))
            push(block, block, third[a][step], third[a][step], {"tensor": pair})

    def fourth_hop(a):
        for step in order:
            p = lax.rem(z + step, 4)
            for s in (1, 2, 3):
                block = x.at[a, p, rows_of(near[s]), own_cols]
                move(block, block, 0, third[a][step] + s, plane(s)).wait_recv()
                push(block, block, fourth[a][step] + s, fourth[a][step] + s, {"tensor": pair})

    def last_hop(a):
        for step in order:
            p = lax.rem(z + step, 4)
            for s in range(4):
                block = x.at[a, p, rows_of(near[s]), pair_cols]
                number = fourth[a][step] + s if s else third[a][step]
                move(block, block, 0, number, {"tensor": pair}).wait_recv()

    third_hop(0)
    second_hop(1)
    fourth_hop(0)
    last_hop(0)
    third_hop(1)

    for step in range(1, 4):
        move(norms.at[z], norms.at[z], 0, at_norms + step, plane(1)).wait_recv()
        move(suffix, spots.at[z], 0, at_spots + step, plane(1)).wait_recv()

    loads["g"].wait()
    loads["s"].wait()
    gain_here = pl.ds(pl.multiple_of(z * rows_here, rows_here), rows_here)
    gain_row[...] = gain_all[gain_here].astype(jnp.float32).reshape(1, rows_here)

    @pl.loop(0, 4)
    def _(p):
        inverse = pick_column(norms[p][:1], seq)
        gains = gain_row[...]
        for j in range(0, rows_here, 512):
            block = x[0, p, :, j : j + 512].astype(jnp.float32)
            block = block * inverse * gains[:, j : j + 512]
            nb[p, :, j : j + 512] = block.astype(jnp.bfloat16)

    loads["k"].wait()
    loads["v"].wait()
    normed = nb[...].reshape(4 * seq, rows_here)
    pkv[...] = dot(normed, wkv[...], plain).reshape(4, seq, 2 * HD)

    is_end = (z == 0) | (z == 3)
    is_mid = (z == 1) | (z == 2)
    end_far, end_mid = 3 - z, 1 + z // 3
    mid_far, mid_near = 6 - 3 * z, 3 * z - 3

    def line_sends(block, into, relay_into, base):
        hand = move(block(end_far), relay_into, base, base + 4, {"prompt": end_mid})
        one = move(block(3 - end_mid), into.at[z], base + 1, base + z, {"prompt": 3 - end_mid})
        two = move(block(end_mid), into.at[z], base + 2, base + z, {"prompt": end_mid})
        over = move(block(3 - z), into.at[z], base, base + z, {"prompt": 3 - z})
        back = move(block(mid_near), into.at[z], base + 1, base + z, {"prompt": mid_near})
        return (hand, one, two), (over, back)

    def line_start(block, into, relay_into, base):
        ends, mids = line_sends(block, into, relay_into, base)

        @pl.when(is_end)
        def _():
            for copy in ends:
                copy.start()

        @pl.when(is_mid)
        def _():
            for copy in mids:
                copy.start()

    def line_relay(block, into, relay_into, base, add, out_block):
        @pl.when(is_mid)
        def _():
            move(relay_into, relay_into, 0, base + 4, {"prompt": mid_far}).wait_recv()
            add()
            move(out_block, into.at[z], base + 2, base + z, {"prompt": mid_far}).start()

    def line_arrive(into, base):
        @pl.when(is_end)
        def _():
            for source in (end_mid, 3 - end_mid):
                move(into.at[z], into.at[z], 0, base + source, plane(1)).wait_recv()

        @pl.when(is_mid)
        def _():
            for source in (0, 3, 3 - z):
                move(into.at[z], into.at[z], 0, base + source, plane(1)).wait_recv()

    def line_sent(block, into, relay_into, base, out_block):
        ends, mids = line_sends(block, into, relay_into, base)

        @pl.when(is_end)
        def _():
            for copy in ends:
                copy.wait_send()

        @pl.when(is_mid)
        def _():
            for copy in mids:
                copy.wait_send()
            move(out_block, into.at[z], base + 2, base + z, {"prompt": mid_far}).wait_send()

    @pl.when(is_end)
    def _():
        rkv[end_far] = jnp.zeros(rkv.shape[1:], rkv.dtype)
        for i in range(2):
            arrived[i, end_far] = jnp.zeros(arrived.shape[2:], arrived.dtype)

    line_kv = take(5)
    line = [take(5) for _ in range(2)]
    kv_args = (lambda d: pkv.at[d], rkv, relay_kv)
    line_start(*kv_args, line_kv)
    for c in range(chunks):
        load_table(c).start()

    def code(i):
        for step in (3, 2, 1):
            d = lax.rem(z + step, 4)

            def write(h, tile):
                coded[i, d, :, h * HD : (h + 1) * HD] = tile

            code_block(lambda h: pp[i, d, :, h * HD : (h + 1) * HD], write, heads, seq)

    def line_of(i):
        return (lambda d: coded.at[i, d], arrived.at[i], relay.at[i])

    def add_coded(i):
        def add():
            factors = scale_of(relay[i, :, heads * HD :])

            def read(h):
                got = relay[i, :, h * HD : (h + 1) * HD].astype(jnp.int32).astype(jnp.float32)
                return got * factors[:, h : h + 1] + pp[i, mid_far, :, h * HD : (h + 1) * HD]

            def write(h, tile):
                total[i, :, h * HD : (h + 1) * HD] = tile

            code_block(read, write, heads, seq)

        return add

    loads["q"].wait()

    @pl.loop(0, head_cols // 256)
    def _(j):
        span = pl.ds(pl.multiple_of(j * 256, 256), 256)
        part = dot(nb[...].reshape(4 * seq, rows_here), wq[:, span], plain)
        pp[0, :, :, span] = part.reshape(4, seq, 256)

    code(0)
    line_start(*line_of(0), line[0])

    def add_kv():
        relay_kv[...] = relay_kv[...] + pkv[mid_far]

    line_relay(*kv_args, line_kv, add_kv, relay_kv)

    fourth_hop(1)
    last_hop(1)
    loads["o"].wait()

    @pl.loop(0, head_cols // 256)
    def _(j):
        span = pl.ds(pl.multiple_of(j * 256, 256), 256)
        part = dot(x[1].reshape(4 * seq, rows_here), wo[span, :], crossed)
        pp[1, :, :, span] = part.reshape(4, seq, 256)

    code(1)
    line_start(*line_of(1), line[1])

    line_arrive(rkv, line_kv)
    own = pkv[z]
    for step in range(1, 4):
        own = own + rkv[lax.rem(z + step, 4)]
    kvg[t] = own.astype(jnp.bfloat16)
    at_kv = take(8)
    for step in range(1, 8):
        push(kvg.at[t], kvg.at[t], at_kv + step, at_kv + step, {"tensor": lax.rem(t + step, 8)})
    line_relay(*line_of(0), line[0], add_coded(0), total.at[0])
    line_relay(*line_of(1), line[1], add_coded(1), total.at[1])

    over = lax.broadcasted_iota(jnp.int32, (rows, count), 1)
    place = jnp.zeros((rows, 1), jnp.float32)
    row_at = lax.broadcasted_iota(jnp.int32, (rows, 1), 0)
    spot_of = row_at // 4
    prompt_of = row_at - 4 * spot_of
    for p in range(4):
        mark = (spot_of == over) & (prompt_of == p)
        found = jnp.where(mark, spots[p].astype(jnp.float32), 0.0)
        place = place + jnp.sum(found, axis=1, keepdims=True)
    place = place + seq * prompt_of.astype(jnp.float32)
    marks = lax.broadcasted_iota(jnp.int32, (rows, 4 * seq), 1).astype(jnp.float32)
    chosen = (marks == place).astype(jnp.bfloat16)
    norm_rows = jnp.zeros((rows, 1), jnp.float32)
    inside = lax.broadcasted_iota(jnp.int32, (rows, 128), 1).astype(jnp.float32)
    for p in range(4):
        hit = (inside + p * seq == place) & (inside < seq)
        norm_rows = norm_rows + jnp.sum(jnp.where(hit, norms[p][:1], 0.0), axis=1, keepdims=True)
    for j in range(0, rows_here, 512):
        block = x[0, :, :, j : j + 512].reshape(4 * seq, 512)
        scaled[:, j : j + 512] = dot(chosen, block, plain) * norm_rows

    def finish(i):
        line_arrive(arrived.at[i], line[i])
        factors = [scale_of(arrived[i, lax.rem(z + s, 4), :, heads * HD :]) for s in (1, 2, 3)]
        for h in range(heads):
            span = slice(h * HD, (h + 1) * HD)
            value = pp[i, z, :, span]
            for s in (1, 2, 3):
                got = arrived[i, lax.rem(z + s, 4), :, span].astype(jnp.int32)
                value = value + got.astype(jnp.float32) * factors[s - 1][:, h : h + 1]
            whole[i, :, span] = value.astype(jnp.bfloat16)

    finish(0)
    for step in range(1, 8):
        move(kvg.at[t], kvg.at[t], 0, at_kv + step, plane(1)).wait_recv()
    finish(1)

    own_spots = jnp.where(
        lax.broadcasted_iota(jnp.int32, (PAD, count), 0)
        == lax.broadcasted_iota(jnp.int32, (PAD, count), 1),
        spots[z].astype(jnp.float32),
        0.0,
    )
    own_spots = jnp.sum(own_spots, axis=1, keepdims=True)
    real = lax.broadcasted_iota(jnp.int32, (PAD, 1), 0) < count
    own_spots = jnp.where(real, own_spots, -1.0)
    steps_iota = lax.broadcasted_iota(jnp.int32, (PAD, seq), 1).astype(jnp.float32)
    chooser = (steps_iota == own_spots).astype(jnp.bfloat16)
    causal = lax.broadcasted_iota(jnp.int32, (seq, seq), 1) <= lax.broadcasted_iota(
        jnp.int32, (seq, seq), 0
    )
    at_slots, slots_from = take(8), take(8)
    at_grads = take(12)

    def head_grads(group):
        span = {h: slice(h * HD, (h + 1) * HD) for h in group}
        queries = {h: whole[0, :, span[h]] for h in group}
        contexts = {h: whole[1, :, span[h]] for h in group}
        keys = {h: kvg[h, :, :HD] for h in group}
        values = {h: kvg[h, :, HD:] for h in group}
        logits = {h: dot(queries[h], keys[h], crossed) * scale for h in group}
        prob_grad = {h: dot(contexts[h], values[h], crossed) for h in group}
        largest = {
            h: jnp.max(jnp.where(causal, logits[h], -1e30), axis=-1, keepdims=True) for h in group
        }
        raised = {h: jnp.where(causal, jnp.exp(logits[h] - largest[h]), 0.0) for h in group}
        whole_sum = {h: jnp.sum(raised[h], axis=-1, keepdims=True) for h in group}
        probs = {h: raised[h] / whole_sum[h] for h in group}
        probs_low = {h: probs[h].astype(jnp.bfloat16) for h in group}
        less = {h: jnp.sum(prob_grad[h] * probs[h], axis=-1, keepdims=True) for h in group}
        logit_grad = {
            h: (probs[h] * (prob_grad[h] - less[h]) * scale).astype(jnp.bfloat16) for h in group
        }
        logit_rows = {h: dot(chooser, logit_grad[h], plain).astype(jnp.bfloat16) for h in group}
        logit_cols = {h: dot(chooser, logit_grad[h], crossed).astype(jnp.bfloat16) for h in group}
        prob_cols = {h: dot(chooser, probs_low[h], crossed).astype(jnp.bfloat16) for h in group}
        for h in group:
            grads[z, :, span[h]] = dot(logit_rows[h], keys[h], plain).astype(jnp.bfloat16)
            slots[h, :24] = dot(logit_cols[h], queries[h], plain)[:24]
            slots[h, 24:] = dot(prob_cols[h], contexts[h], plain)[:24]

    def send_slots(h):
        return move(slots.at[h], slots_in.at[t], at_slots + h, slots_from + t, {"tensor": h})

    halves = 2
    head_parts = []
    for half in range(halves):
        group = range(half * heads // halves, (half + 1) * heads // halves)
        head_grads(group)
        for h in group:

            @pl.when(t != h)
            def _():
                send_slots(h).start()

        part = grads.at[z, :, group.start * HD : group.stop * HD]
        head_parts.append(part)
        for step in (2, 1, 3):
            number = at_grads + 4 * half + step
            push(part, part, number, number, along(step))
    slots_in[t] = slots[t]
    for step in range(1, 8):
        source = lax.rem(t + step, 8)
        move(slots_in.at[t], slots_in.at[t], 0, slots_from + source, plane(1)).wait_recv()
    summed = slots_in[0]
    for j in range(1, 8):
        summed = summed + slots_in[j]
    filler = jnp.zeros((PAD - 24, HD), jnp.float32)
    key_rows = jnp.concatenate([summed[:24], filler], axis=0)
    value_rows = jnp.concatenate([summed[24:], filler], axis=0)
    grads[z, :, head_cols : head_cols + HD] = key_rows.astype(jnp.bfloat16)
    grads[z, :, head_cols + HD :] = value_rows.astype(jnp.bfloat16)
    tail_part = grads.at[z, :, head_cols:]
    for step in (2, 1, 3):
        push(tail_part, tail_part, at_grads + 8 + step, at_grads + 8 + step, along(step))
    for half in range(halves):
        for step in range(1, 4):
            part = head_parts[half]
            move(part, part, 0, at_grads + 4 * half + step, plane(1)).wait_recv()

    packed_at = lax.broadcasted_iota(jnp.int32, (rows, 4 * PAD), 1)
    packer = (packed_at == PAD * prompt_of + spot_of).astype(jnp.bfloat16)
    packed = dot(packer, grads[:, :, :head_cols].reshape(4 * PAD, head_cols), plain)
    packed = packed.astype(jnp.bfloat16)
    farthest = (3, 1, 2, 0)

    def owned(half, s):
        owner = 2 * near[s] + ((1 - core) if half == 0 else core)
        return pl.ds(pl.multiple_of(owner * slice_width, slice_width), slice_width)

    for half in range(2):
        for s in farthest:
            weighted[half, s] = dot(packed, wq[owned(half, s), :], crossed)
    for step in range(1, 4):
        move(tail_part, tail_part, 0, at_grads + 8 + step, plane(1)).wait_recv()
    packed = dot(packer, grads[:, :, head_cols:].reshape(4 * PAD, 2 * HD), plain)
    packed = packed.astype(jnp.bfloat16)
    inner = jnp.zeros((rows, 128), jnp.float32)
    at_pair, at_shares = take(4), take(4)
    for half in range(2):
        for s in farthest:
            span = owned(half, s)
            part = weighted[half, s] + dot(packed, wkv[span, :], crossed)
            part = part * gain_row[:, span]
            product = part * scaled[:, span]
            for j in range(0, slice_width, 128):
                inner = inner + product[:, j : j + 128]
            weighted[half, s] = part
            if half == 0:
                push(weighted.at[0, s], pair_in.at[s], at_pair + s, at_pair + s, {"tensor": pair})
    for s in farthest:
        move(pair_in.at[s], pair_in.at[s], 0, at_pair + s, {"tensor": pair}).wait_recv()
        weighted[1, s] = weighted[1, s] + pair_in[s]
        if s:
            push(weighted.at[1, s], shares.at[s - 1], at_shares + s, at_shares + s, plane(s))
    inner = jnp.sum(inner, axis=1, keepdims=True)
    inner_in[t] = jnp.broadcast_to(lay_row(inner, 128), (8, 128))
    at_inner = take(8)
    for step in range(1, 8):
        push(
            inner_in.at[t],
            inner_in.at[t],
            at_inner + step,
            at_inner + step,
            {"tensor": lax.rem(t + step, 8)},
        )
    for step in range(1, 8):
        move(inner_in.at[t], inner_in.at[t], 0, at_inner + step, plane(1)).wait_recv()
    inner = inner_in[0]
    for j in range(1, 8):
        inner = inner + inner_in[j]
    inner_z[z] = inner
    at_inner_z = take(4)
    for step in range(1, 4):
        push(inner_z.at[z], inner_z.at[z], at_inner_z + step, at_inner_z + step, along(step))
    for s in (1, 2, 3):
        move(shares.at[s - 1], shares.at[s - 1], 0, at_shares + s, plane(1)).wait_recv()
    own = weighted[1, 0] + shares[0] + shares[1] + shares[2]
    for step in range(1, 4):
        move(inner_z.at[z], inner_z.at[z], 0, at_inner_z + step, plane(1)).wait_recv()
    inner = (inner_z[0] + inner_z[1] + inner_z[2] + inner_z[3])[:1]
    inner = pick_column(inner, rows) / width

    here = pl.ds(pl.multiple_of(t * slice_width, slice_width), slice_width)
    suffix_grads[z, :, here] = (norm_rows * (own - scaled[:, here] * inner)).astype(jnp.bfloat16)

    def grad_of(p, chip_index, core_index):
        first = (2 * chip_index + core_index) * slice_width
        return suffix_grads.at[p, :, pl.ds(pl.multiple_of(first, slice_width), slice_width)]

    at_z = take(4)
    spread = [take(4) for _ in range(4)]
    doubled = [take(4) for _ in range(4)]
    mine_now = grad_of(z, chip, core)
    for step in (2, 1, 3):
        push(mine_now, mine_now, at_z + step, at_z + step, along(step))

    def to_plane(step):
        block = grad_of(lax.rem(z - step + 4, 4), chip, core)
        if step:
            move(block, block, 0, at_z + step, plane(1)).wait_recv()
        for s in (3, 1, 2):
            push(block, block, spread[step] + s, spread[step] + s, plane(s))
        push(block, block, spread[step], spread[step], {"tensor": pair})

    def to_pair(step):
        p = lax.rem(z - step + 4, 4)
        for s in (1, 2, 3):
            block = grad_of(p, near[s], core)
            move(block, block, 0, spread[step] + s, plane(s)).wait_recv()
            push(block, block, doubled[step] + s, doubled[step] + s, {"tensor": pair})

    def from_pair(step):
        p = lax.rem(z - step + 4, 4)
        for s in range(4):
            block = grad_of(p, near[s], 1 - core)
            number = doubled[step] + s if s else spread[step]
            move(block, block, 0, number, {"tensor": pair}).wait_recv()

    def multiply(step, half):
        p = lax.rem(z - step + 4, 4)
        features = pl.ds(pl.multiple_of(p * rows_here, rows_here), rows_here)
        wide = vocab.shape[0] // 2
        span = pl.ds(half * wide, wide)
        part = dot(suffix_grads[p], table[span, features], crossed)
        if step != order[0]:
            part = part + partial[:, span]
        if step != order[-1]:
            partial[:, span] = part
            return
        part = jnp.where(barred[:, span] == 1, 0.0, -part)
        for n in range(count):
            out[n, :, span] = part[4 * n : 4 * n + 4]

    to_plane(0)
    to_plane(1)
    to_pair(0)
    for c in range(chunks):
        load_table(c).wait()
    loads["b"].wait()
    from_pair(0)
    multiply(0, 0)
    to_plane(3)
    to_plane(2)
    to_pair(1)
    multiply(0, 1)
    from_pair(1)
    multiply(1, 0)
    to_pair(3)
    multiply(1, 1)
    from_pair(3)
    multiply(3, 0)
    to_pair(2)
    multiply(3, 1)
    from_pair(2)
    multiply(2, 0)
    multiply(2, 1)

    for copy in sent:
        copy.wait_send()
    for h in range(heads):

        @pl.when(t != h)
        def _():
            send_slots(h).wait_send()

    for a in range(2):
        for s in range(4):

            @pl.when(near[s] != z)
            def _():
                block = x.at[a, z, rows_of(chip), own_cols]
                move(block, block, across[a] + s, 0, {"prompt": near[s]}).wait_send()

    line_sent(*kv_args, line_kv, relay_kv)
    for i in range(2):
        line_sent(*line_of(i), line[i], total.at[i])


def fused(
    embeds,
    norm_gain,
    query_weight,
    key_weight,
    value_weight,
    out_weight,
    out_grad,
    suffix_pos,
    vocab_table,
    banned,
):
    seq, cols = embeds.shape[1:]
    rows_here, head_cols = query_weight.shape
    count = suffix_pos.shape[1]
    vocab_here, width = vocab_table.shape
    heads = head_cols // HD
    rows = 4 * count
    slice_width = rows_here // 8
    low, full, short = jnp.bfloat16, jnp.float32, jnp.int16
    coded = head_cols + HD
    local = pl.BlockSpec(memory_space=pltpu.VMEM)
    apart = pl.BlockSpec(memory_space=pl.ANY)
    scratch = [
        ((rows_here, head_cols), low),
        ((rows_here, 2 * HD), low),
        ((head_cols, rows_here), low),
        (vocab_table.shape, low),
        ((seq, cols), low),
        ((2, 3, seq // 4, cols), low),
        ((2, 4, seq, rows_here), low),
        ((8, 8, 128), full),
        ((4, 8, 128), full),
        ((4, 1, count), jnp.int32),
        ((4, seq, rows_here), low),
        ((4, seq, 2 * HD), full),
        ((4, seq, 2 * HD), full),
        ((seq, 2 * HD), full),
        ((2, 4, seq, head_cols), full),
        ((2, 4, seq, coded), short),
        ((2, 4, seq, coded), short),
        ((2, seq, coded), short),
        ((2, seq, coded), short),
        ((8, seq, 2 * HD), low),
        ((2, seq, head_cols), low),
        ((8, 48, HD), full),
        ((8, 48, HD), full),
        ((4, PAD, head_cols + 2 * HD), low),
        ((rows, rows_here), full),
        ((2, 4, rows, slice_width), full),
        ((4, rows, slice_width), full),
        ((3, rows, slice_width), full),
        ((8, 8, 128), full),
        ((4, 8, 128), full),
        ((4, rows, rows_here), low),
        ((rows, vocab_here), full),
        ((1, rows_here), full),
        ((width,), low),
        ((1, vocab_here), jnp.int32),
    ]
    scores = pl.pallas_call(
        fused_kernel,
        out_shape=jax.ShapeDtypeStruct((count, 4, vocab_here), full),
        in_specs=[apart] * 10,
        out_specs=local,
        scratch_shapes=[pltpu.VMEM(shape, dtype) for shape, dtype in scratch]
        + [
            pltpu.SemaphoreType.DMA((SEMS,)),
            pltpu.SemaphoreType.DMA((SEMS,)),
            pltpu.SemaphoreType.DMA((8 + vocab_here // CHUNK,)),
            pltpu.SemaphoreType.DMA((2,)),
        ],
        compiler_params=pltpu.CompilerParams(
            collective_id=11, has_side_effects=True, vmem_limit_bytes=60 << 20
        ),
    )(
        embeds,
        out_grad,
        norm_gain,
        query_weight,
        key_weight,
        value_weight,
        out_weight,
        suffix_pos,
        vocab_table,
        banned.reshape(1, -1),
    )
    return scores.transpose(1, 0, 2)


def fits(mesh_sizes, arrays):
    embeds, query_weight, key_weight, suffix_pos, vocab_table = arrays
    return (
        mesh_sizes == (4, 8)
        and embeds.shape[1] == 64
        and query_weight.shape[1] == 8 * HD
        and key_weight.shape[1] == HD
        and query_weight.shape[0] == 2 * embeds.shape[2]
        and query_weight.shape[0] % 2048 == 0
        and suffix_pos.shape[1] == 20
        and vocab_table.shape[0] % CHUNK == 0
    )


def part_of(*args):
    sizes = (lax.axis_size("prompt"), lax.axis_size("tensor"))
    if fits(sizes, (args[0], args[2], args[3], args[7], args[8])):
        return fused(*args)
    return on_device(*args)


def solution(mesh):
    return jax.shard_map(
        part_of,
        mesh=mesh,
        in_specs=(
            P("prompt", None, "tensor"),
            P(),
            P("prompt", "tensor"),
            P("prompt", "tensor"),
            P("prompt", "tensor"),
            P("tensor", "prompt"),
            P("prompt", None, "tensor"),
            P("prompt", None),
            P(("prompt", "tensor"), None),
            P(("prompt", "tensor")),
        ),
        out_specs=P(None, None, ("prompt", "tensor")),
        check_vma=False,
    )
```

```python
import functools
import math

import jax
import jax.numpy as jnp
from jax import lax
from jax.experimental import pallas as pl
from jax.experimental.pallas import tpu as pltpu
from jax.sharding import PartitionSpec as P

KVH = 8
HD = 128


EPSILON = 1e-05


def exchange_kernel(axis, count, spread, *refs):
    arrays = len(spread)
    sources, targets = refs[:arrays], refs[arrays : 2 * arrays]
    send_sem, recv_sem, own_sem = refs[2 * arrays :]
    here = lax.axis_index(axis)

    def block(i, to):
        return sources[i].at[to] if spread[i] else sources[i]

    kept = []
    for i in range(arrays):
        copy = pltpu.make_async_copy(block(i, here), targets[i].at[here], own_sem.at[i])
        copy.start()
        kept.append(copy)
    barrier = pltpu.get_barrier_semaphore()
    for step in range(1, count):
        peer = lax.rem(here + step, count)
        pl.semaphore_signal(
            barrier, inc=1, device_id={axis: peer}, device_id_type=pl.DeviceIdType.MESH
        )
    pl.semaphore_wait(barrier, count - 1)
    copies = []
    for step in range(1, count):
        peer = lax.rem(here + step, count)
        for i in range(arrays):
            copy = pltpu.make_async_remote_copy(
                src_ref=block(i, peer),
                dst_ref=targets[i].at[here],
                send_sem=send_sem.at[i, step - 1],
                recv_sem=recv_sem.at[i, step - 1],
                device_id={axis: peer},
                device_id_type=pl.DeviceIdType.MESH,
            )
            copy.start()
            copies.append(copy)
    for copy in kept + copies:
        copy.wait()


def exchange(axis, number, *operands):
    count = lax.axis_size(axis)
    arrays = [array for array, _ in operands]
    spread = tuple(each for _, each in operands)
    shapes = [
        jax.ShapeDtypeStruct(((count,) + (a.shape[1:] if each else a.shape)), a.dtype)
        for a, each in operands
    ]
    space = pl.BlockSpec(memory_space=pltpu.VMEM)
    sems = pltpu.SemaphoreType.DMA((len(arrays), count - 1))
    return pl.pallas_call(
        functools.partial(exchange_kernel, axis, count, spread),
        out_shape=shapes,
        in_specs=[space] * len(arrays),
        out_specs=[space] * len(arrays),
        scratch_shapes=[sems, sems, pltpu.SemaphoreType.DMA((len(arrays),))],
        compiler_params=pltpu.CompilerParams(
            collective_id=number, has_side_effects=True, vmem_limit_bytes=40 << 20
        ),
    )(*arrays)


def dot_f32(spec, a, b):
    return jnp.einsum(spec, a, b, preferred_element_type=jnp.float32)


MESH = pl.DeviceIdType.MESH


def greet(axis, peers):
    barrier = pltpu.get_barrier_semaphore()
    for peer in peers:
        pl.semaphore_signal(barrier, inc=1, device_id={axis: peer}, device_id_type=MESH)
    pl.semaphore_wait(barrier, len(peers))


def gather_kernel(axis, count, arrays, *refs):
    sources, targets = refs[:arrays], refs[arrays : 2 * arrays]
    send_sem, recv_sem, own_sem = refs[2 * arrays :]
    here = lax.axis_index(axis)
    chips = count // 2
    chip, core = here // 2, lax.rem(here, 2)
    pair = 2 * chip + (1 - core)
    kept = []
    for i in range(arrays):
        copy = pltpu.make_async_copy(sources[i], targets[i].at[here], own_sem.at[i])
        copy.start()
        kept.append(copy)

    def push(i, source, slot, number, peer):
        return pltpu.make_async_remote_copy(
            src_ref=source,
            dst_ref=targets[i].at[slot],
            send_sem=send_sem.at[i, number],
            recv_sem=recv_sem.at[i, number],
            device_id={axis: peer},
            device_id_type=MESH,
        )

    others = [2 * lax.rem(chip + step, chips) + core for step in range(1, chips)]
    greet(axis, others + [pair])
    first = []
    for step in range(1, chips):
        for i in range(arrays):
            copy = push(i, sources[i], here, step, others[step - 1])
            copy.start()
            first.append(copy)
    rest = []
    for i in range(arrays):
        copy = push(i, sources[i], here, 0, pair)
        copy.start()
        rest.append(copy)
    for step in range(1, chips):
        slot = 2 * lax.rem(chip + chips - step, chips) + core
        for i in range(arrays):
            first[(step - 1) * arrays + i].wait_recv()
            copy = push(i, targets[i].at[slot], slot, chips - 1 + step, pair)
            copy.start()
            rest.append(copy)
    for copy in first:
        copy.wait_send()
    for copy in kept + rest:
        copy.wait()


def gather(axis, number, *arrays):
    count = lax.axis_size(axis)
    shapes = [jax.ShapeDtypeStruct((count,) + a.shape, a.dtype) for a in arrays]
    space = pl.BlockSpec(memory_space=pltpu.VMEM)
    sems = pltpu.SemaphoreType.DMA((len(arrays), count - 1))
    return pl.pallas_call(
        functools.partial(gather_kernel, axis, count, len(arrays)),
        out_shape=shapes,
        in_specs=[space] * len(arrays),
        out_specs=[space] * len(arrays),
        scratch_shapes=[sems, sems, pltpu.SemaphoreType.DMA((len(arrays),))],
        compiler_params=pltpu.CompilerParams(
            collective_id=number, has_side_effects=True, vmem_limit_bytes=40 << 20
        ),
    )(*arrays)


def line_kernel(axis, source, target, relay, send_sem, recv_sem, own_sem):
    here = lax.axis_index(axis)
    own = pltpu.make_async_copy(source.at[here], target.at[here], own_sem.at[0])
    own.start()
    greet(axis, [lax.rem(here + step, 4) for step in range(1, 4)])

    def push(block, slot, number, peer, into=None):
        return pltpu.make_async_remote_copy(
            src_ref=block,
            dst_ref=target.at[slot] if into is None else into,
            send_sem=send_sem.at[number],
            recv_sem=recv_sem.at[slot if into is None else 4],
            device_id={axis: peer},
            device_id_type=MESH,
        )

    for role in range(4):
        far = 3 if role < 2 else 0
        middle = 1 if role < 2 else 2
        across = 3 - middle

        @pl.when(here == role)
        def _():
            if role == middle:
                sent = [
                    push(source.at[across], role, 0, across),
                    push(source.at[3 - far], role, 1, 3 - far),
                ]
                for copy in sent:
                    copy.start()
                total = push(relay, role, 2, far)
                push(source.at[far], role, 3, far, relay).wait_recv()
                relay[...] = relay[...] + source[far]
                total.start()
                sent.append(total)
                arriving = [0, across, 3]
            else:
                handed = push(source.at[far], role, 0, middle, relay)
                handed.start()
                target[far] = jnp.zeros_like(target[far])
                handed.wait_send()
                sent = [
                    push(source.at[across], role, 1, across),
                    push(source.at[middle], role, 2, middle),
                ]
                for copy in sent:
                    copy.start()
                arriving = [1, 2]
            for slot in arriving:
                push(source.at[slot], slot, 3, slot).wait_recv()
            for copy in sent:
                copy.wait_send()

    own.wait()


def line_exchange(axis, number, blocks):
    if lax.axis_size(axis) != 4:
        return exchange(axis, number, (blocks, True))[0]
    space = pl.BlockSpec(memory_space=pltpu.VMEM)
    return pl.pallas_call(
        functools.partial(line_kernel, axis),
        out_shape=jax.ShapeDtypeStruct(blocks.shape, blocks.dtype),
        in_specs=[space],
        out_specs=space,
        scratch_shapes=[
            pltpu.VMEM(blocks.shape[1:], blocks.dtype),
            pltpu.SemaphoreType.DMA((4,)),
            pltpu.SemaphoreType.DMA((5,)),
            pltpu.SemaphoreType.DMA((1,)),
        ],
        compiler_params=pltpu.CompilerParams(
            collective_id=number, has_side_effects=True, vmem_limit_bytes=40 << 20
        ),
    )(blocks)


CHUNK = 512


def score_kernel(
    axis, count, part, vocab, scores, got, flat, table, send_sem, recv_sem, own_sem, load_sem
):
    def load(c):
        span = pl.ds(pl.multiple_of(c * CHUNK, CHUNK), CHUNK)
        return pltpu.make_async_copy(vocab.at[span], table.at[span], load_sem.at[c])

    chunks = vocab.shape[0] // CHUNK
    for c in range(chunks):
        load(c).start()
    gather_kernel(axis, count, 1, part, got, send_sem, recv_sem, own_sem)
    wide = part.shape[2]
    for p in range(part.shape[0]):
        for t in range(count):
            start = (p * count + t) * wide
            flat[:, start : start + wide] = got[t, p]

    @pl.loop(0, chunks)
    def _(c):
        load(c).wait()
        span = pl.ds(pl.multiple_of(c * CHUNK, CHUNK), CHUNK)
        scores[:, span] = -lax.dot_general(
            flat[...],
            table[span, :],
            (((1,), (1,)), ((), ())),
            preferred_element_type=jnp.float32,
        )


def gather_score(axis, number, part, vocab):
    count = lax.axis_size(axis)
    n_prompt, rows, wide = part.shape
    vocab_here, width = vocab.shape
    if wide % 128 or vocab_here % CHUNK or rows % 16:
        (part,) = gather(axis, number, part)
        return -dot_f32("rd,vd->rv", part.transpose(2, 1, 0, 3).reshape(rows, width), vocab)
    sems = pltpu.SemaphoreType.DMA((1, count - 1))
    return pl.pallas_call(
        functools.partial(score_kernel, axis, count),
        out_shape=jax.ShapeDtypeStruct((rows, vocab_here), jnp.float32),
        in_specs=[pl.BlockSpec(memory_space=pltpu.VMEM), pl.BlockSpec(memory_space=pl.ANY)],
        out_specs=pl.BlockSpec(memory_space=pltpu.VMEM),
        scratch_shapes=[
            pltpu.VMEM((count,) + part.shape, part.dtype),
            pltpu.VMEM((rows, width), part.dtype),
            pltpu.VMEM(vocab.shape, vocab.dtype),
            sems,
            sems,
            pltpu.SemaphoreType.DMA((1,)),
            pltpu.SemaphoreType.DMA((vocab_here // CHUNK,)),
        ],
        compiler_params=pltpu.CompilerParams(
            collective_id=number, has_side_effects=True, vmem_limit_bytes=52 << 20
        ),
    )(part, vocab)


def on_device(
    embeds,
    norm_gain,
    query_weight,
    key_weight,
    value_weight,
    out_weight,
    out_grad,
    suffix_pos,
    vocab_table,
    banned,
):
    n_prompt = lax.axis_size("prompt")
    n_tensor = lax.axis_size("tensor")
    here_prompt = lax.axis_index("prompt")
    here_tensor = lax.axis_index("tensor")
    seq_len = embeds.shape[1]
    suffix_count = suffix_pos.shape[1]
    width = embeds.shape[2] * n_tensor
    rows_here, head_cols = query_weight.shape
    key_cols = key_weight.shape[1]
    heads_here = head_cols // HD
    slice_width = rows_here // n_tensor
    logit_scale = 1.0 / math.sqrt(HD)

    split_rows = seq_len // n_tensor
    ratio = n_tensor // n_prompt
    feature_cols = embeds.shape[2]
    both = jnp.concatenate(
        [
            embeds.reshape(n_tensor, split_rows, feature_cols),
            out_grad.reshape(n_tensor, split_rows, feature_cols),
        ],
        axis=1,
    )
    (both,) = exchange("tensor", 0, (both, True))
    own = both[:, :split_rows].astype(jnp.float32)
    inverse_norm = lax.rsqrt(jnp.sum(own * own, axis=(0, 2))[:, None] / width + EPSILON)
    inverse_norm = jnp.broadcast_to(inverse_norm, (split_rows, 128))
    both = both.reshape(n_prompt, ratio, 2 * split_rows, feature_cols)
    both, inverse_norm, suffix_all = exchange(
        "prompt", 1, (both, True), (inverse_norm, False), (suffix_pos, False)
    )
    both, inverse_norm = gather("tensor", 2, both, inverse_norm)
    suffix_all = suffix_all.reshape(n_prompt, suffix_count)
    both = both.reshape(n_tensor, n_prompt, ratio, 2, split_rows, feature_cols)
    both = both.transpose(3, 1, 0, 4, 2, 5).reshape(2, n_prompt, seq_len, rows_here)
    embeds, out_grad = both[0], both[1]
    inverse_norm = inverse_norm[..., :1].transpose(1, 0, 2, 3).reshape(n_prompt, seq_len, 1)
    embeds_float = embeds.astype(jnp.float32)
    gain_rows = lax.dynamic_slice_in_dim(norm_gain, here_prompt * rows_here, rows_here, 0)
    gain_rows = gain_rows.astype(jnp.float32)
    normed = (embeds_float * inverse_norm * gain_rows).astype(jnp.bfloat16)

    parts = jnp.concatenate(
        [
            dot_f32("psd,dc->psc", normed, query_weight),
            dot_f32("psd,dc->psc", normed, key_weight),
            dot_f32("psd,dc->psc", normed, value_weight),
            dot_f32("psd,cd->psc", out_grad, out_weight),
        ],
        axis=2,
    )
    parts = line_exchange("prompt", 3, parts)
    whole = jnp.sum(parts, axis=0).astype(jnp.bfloat16)
    contexts = whole[:, head_cols + 2 * key_cols :]
    contexts = contexts.reshape(seq_len, heads_here, HD)
    queries = whole[:, :head_cols].reshape(seq_len, heads_here, HD)
    (key_values,) = gather("tensor", 4, whole[:, head_cols : head_cols + 2 * key_cols])
    key_values = key_values.reshape(n_tensor, seq_len, 2, key_cols).transpose(2, 1, 0, 3)
    key_values = key_values.reshape(2, seq_len, KVH * HD)
    fold = min(heads_here, KVH)
    first = ((here_tensor * heads_here) % KVH) * HD
    if fold < KVH:
        key_values = lax.dynamic_slice_in_dim(key_values, first, fold * HD, 2)
    key_values = key_values.reshape(2, seq_len, fold, HD)
    if heads_here > fold:
        key_values = jnp.tile(key_values, (1, 1, heads_here // fold, 1))
    keys, values = key_values[0], key_values[1]

    logits = dot_f32("qhd,khd->hqk", queries, keys) * logit_scale
    row_index = lax.broadcasted_iota(jnp.int32, (seq_len, seq_len), 0)
    col_index = lax.broadcasted_iota(jnp.int32, (seq_len, seq_len), 1)
    causal = col_index <= row_index
    largest = jnp.max(jnp.where(causal, logits, -1e30), axis=-1, keepdims=True)
    raised = jnp.where(causal, jnp.exp(logits - largest), 0.0)
    probs = raised / jnp.sum(raised, axis=-1, keepdims=True)
    probs_low = probs.astype(jnp.bfloat16)
    prob_grad = dot_f32("qhd,khd->hqk", contexts, values)
    logit_grad = (
        probs * (prob_grad - jnp.sum(prob_grad * probs, axis=-1, keepdims=True)) * logit_scale
    ).astype(jnp.bfloat16)
    steps_iota = lax.broadcasted_iota(jnp.int32, (suffix_count, seq_len), 1)
    chooser = (steps_iota == suffix_pos[0][:, None]).astype(jnp.bfloat16)
    logit_rows = dot_f32("ns,hsk->hnk", chooser, logit_grad).astype(jnp.bfloat16)
    query_grad = dot_f32("hnk,khd->nhd", logit_rows, keys).astype(jnp.bfloat16)
    query_grad = query_grad.reshape(suffix_count, head_cols)
    logit_cols = dot_f32("hqk,nk->hnq", logit_grad, chooser).astype(jnp.bfloat16)
    prob_cols = dot_f32("hqk,nk->hnq", probs_low, chooser).astype(jnp.bfloat16)
    key_each = dot_f32("hnq,qhd->nhd", logit_cols, queries)
    value_each = dot_f32("hnq,qhd->nhd", prob_cols, contexts)
    slots = jnp.stack([key_each, value_each])
    slots = slots.reshape(2, suffix_count, heads_here // fold, fold * HD).sum(axis=2)
    if fold < KVH:
        slots = lax.dynamic_update_slice_in_dim(
            jnp.zeros((2, suffix_count, KVH * HD), jnp.float32), slots, first, 2
        )
    slots = slots.reshape(2 * suffix_count, n_tensor, key_cols).transpose(1, 0, 2)
    (grads,) = exchange("tensor", 5, (slots, True))
    grads = jnp.sum(grads, axis=0).astype(jnp.bfloat16).reshape(2, suffix_count, key_cols)
    grads = jnp.concatenate([query_grad, grads[0], grads[1]], axis=1)
    (grads,) = exchange("prompt", 6, (grads, False))
    rows = n_prompt * suffix_count
    grads = grads.reshape(rows, head_cols + 2 * key_cols)
    steps_iota = lax.broadcasted_iota(jnp.int32, (n_prompt, suffix_count, seq_len), 2)
    chooser_all = steps_iota == suffix_all[:, :, None]
    embed_rows = dot_f32("pns,psd->pnd", chooser_all.astype(jnp.bfloat16), embeds)
    norm_rows = jnp.sum(
        jnp.where(chooser_all, inverse_norm[:, None, :, 0], 0.0), axis=-1, keepdims=True
    )
    scaled = (embed_rows * norm_rows).reshape(rows, rows_here)
    norm_rows = norm_rows.reshape(rows, 1)
    branch = dot_f32("nc,dc->nd", grads[:, :head_cols], query_weight)
    branch = branch + dot_f32("nc,dc->nd", grads[:, head_cols : head_cols + key_cols], key_weight)
    branch = branch + dot_f32("nc,dc->nd", grads[:, head_cols + key_cols :], value_weight)
    branch = branch * gain_rows
    inner = jnp.sum(branch * scaled, axis=-1)
    branch = branch.reshape(rows, n_tensor, slice_width).transpose(1, 0, 2)
    share, inner = exchange("tensor", 7, (branch, True), (inner[None, :], False))
    weighted = jnp.sum(share, axis=0)
    (inner,) = exchange("prompt", 8, (jnp.sum(inner, axis=0), False))
    inner = jnp.sum(inner, axis=0).reshape(rows, 1) / width
    scaled = lax.dynamic_slice_in_dim(scaled, here_tensor * slice_width, slice_width, 1)
    suffix_grad = (norm_rows * (weighted - scaled * inner)).astype(jnp.bfloat16)
    (suffix_grad,) = exchange("prompt", 9, (suffix_grad, False))
    scores = gather_score("tensor", 10, suffix_grad, vocab_table)
    scores = scores.reshape(n_prompt, suffix_count, vocab_table.shape[0])
    return jnp.where(banned[None, None, :] == 1, 0.0, scores)


PAD = 32
TINY = 1e-30
FULL = 32767.0
SEMS = 232


def pick_column(row, rows):
    wide = row.shape[1]
    down = lax.broadcasted_iota(jnp.int32, (rows, wide), 0)
    along = lax.broadcasted_iota(jnp.int32, (rows, wide), 1)
    return jnp.sum(jnp.where(down == along, row, 0.0), axis=1, keepdims=True)


def lay_row(column, wide):
    rows = column.shape[0]
    down = lax.broadcasted_iota(jnp.int32, (rows, wide), 0)
    along = lax.broadcasted_iota(jnp.int32, (rows, wide), 1)
    return jnp.sum(jnp.where(down == along, column, 0.0), axis=0, keepdims=True)


def lane_sums(values):
    total = values[:, :128]
    for j in range(128, values.shape[1], 128):
        total = total + values[:, j : j + 128]
    return jnp.sum(total, axis=1, keepdims=True)


def code_block(read, write, heads, rows):
    lanes = lax.broadcasted_iota(jnp.int32, (rows, HD), 1)
    powers = jnp.zeros((rows, HD), jnp.float32)
    for h in range(heads):
        block = read(h)
        peak = jnp.max(jnp.abs(block), axis=1, keepdims=True)
        power = jnp.floor(jnp.log2(jnp.maximum(peak, TINY))) + 1.0
        fixed = jnp.floor(block * (jnp.exp2(-power) * FULL) + 0.5)
        fixed = jnp.clip(fixed, -FULL, FULL)
        write(h, fixed.astype(jnp.int32).astype(jnp.int16))
        powers = jnp.where(lanes == h, power, powers)
    square = jnp.concatenate([powers, jnp.zeros((HD - rows, HD), jnp.float32)], axis=0).T
    write(heads, square[:16].astype(jnp.int32).astype(jnp.int16))


def scale_of(tile, rows):
    factors = jnp.exp2(tile.astype(jnp.int32).astype(jnp.float32)) * (1.0 / FULL)
    square = jnp.concatenate([factors, jnp.zeros((HD - 16, HD), jnp.float32)], axis=0).T
    return square[:rows]


def fused_kernel(
    embeds,
    out_grad,
    gain,
    query_weight,
    key_weight,
    value_weight,
    out_weight,
    suffix,
    vocab,
    banned,
    out,
    wq,
    wkv,
    wo,
    table,
    mine,
    stage,
    x,
    sums,
    norms,
    spots,
    nb,
    pkv,
    rkv,
    relay_kv,
    pp,
    coded,
    arrived,
    relay,
    total,
    powers,
    powers_in,
    powers_relay,
    powers_total,
    kvg,
    whole,
    slots,
    slots_in,
    grads,
    scaled,
    weighted,
    pair_in,
    shares,
    inner_in,
    inner_z,
    suffix_grads,
    partial,
    gain_row,
    gain_all,
    barred,
    send_sem,
    recv_sem,
    load_sem,
    own_sem,
):
    z = lax.axis_index("prompt")
    t = lax.axis_index("tensor")
    chip, core = t // 2, lax.rem(t, 2)
    pair = 2 * chip + (1 - core)
    chip_y, chip_x = chip // 2, lax.rem(chip, 2)
    near = [
        chip,
        2 * chip_y + (1 - chip_x),
        2 * (1 - chip_y) + chip_x,
        2 * (1 - chip_y) + (1 - chip_x),
    ]
    seq, cols = embeds.shape[1], embeds.shape[2]
    width = gain.shape[0]
    rows_here, head_cols = query_weight.shape
    heads = head_cols // HD
    count = suffix.shape[1]
    rows = 4 * count
    quarter = seq // 4
    slice_width = rows_here // 8
    scale = 1.0 / math.sqrt(HD)
    dot = functools.partial(lax.dot_general, preferred_element_type=jnp.float32)
    plain = (((1,), (0,)), ((), ()))
    crossed = (((1,), (1,)), ((), ()))

    chunks = vocab.shape[0] // CHUNK

    def load_table(c):
        span = pl.ds(pl.multiple_of(c * CHUNK, CHUNK), CHUNK)
        return pltpu.make_async_copy(vocab.at[span], table.at[span], load_sem.at[8 + c])

    loads = {
        "g": pltpu.make_async_copy(gain, gain_all, load_sem.at[5]),
        "b": pltpu.make_async_copy(banned, barred, load_sem.at[6]),
        "s": pltpu.make_async_copy(suffix, spots.at[z], load_sem.at[7]),
        "e": pltpu.make_async_copy(embeds.at[0], mine.at[0], load_sem.at[0]),
        "d": pltpu.make_async_copy(out_grad.at[0], mine.at[1], own_sem.at[2]),
        "k": pltpu.make_async_copy(key_weight, wkv.at[:, :HD], load_sem.at[1]),
        "v": pltpu.make_async_copy(value_weight, wkv.at[:, HD:], load_sem.at[2]),
        "q": pltpu.make_async_copy(query_weight, wq, load_sem.at[3]),
        "o": pltpu.make_async_copy(out_weight, wo, load_sem.at[4]),
    }
    for name in "edgbs":
        loads[name].start()

    barrier = pltpu.get_barrier_semaphore()
    for step in range(1, 8):
        pl.semaphore_signal(
            barrier, inc=1, device_id={"tensor": lax.rem(t + step, 8)}, device_id_type=MESH
        )
    for step in range(1, 4):
        pl.semaphore_signal(
            barrier, inc=1, device_id={"prompt": lax.rem(z + step, 4)}, device_id_type=MESH
        )
    pl.semaphore_wait(barrier, 10)

    used = [0]
    sent = []

    def take(number=1):
        used[0] += number
        assert used[0] <= SEMS
        return used[0] - number

    def move(source, target, s, r, device):
        return pltpu.make_async_remote_copy(
            src_ref=source,
            dst_ref=target,
            send_sem=send_sem.at[s],
            recv_sem=recv_sem.at[r],
            device_id=device,
            device_id_type=MESH,
        )

    def push(source, target, s, r, device):
        copy = move(source, target, s, r, device)
        copy.start()
        sent.append(copy)

    def plane(s, other=False):
        return {"tensor": 2 * near[s] + ((1 - core) if other else core)}

    def along(step):
        return {"prompt": lax.rem(z + step, 4)}

    def rows_of(chip_index):
        return pl.ds(pl.multiple_of(quarter * chip_index, quarter), quarter)

    sources = (mine.at[0], mine.at[1])
    own_cols = pl.ds(pl.multiple_of(core * cols, 128), cols)
    pair_cols = pl.ds(pl.multiple_of((1 - core) * cols, 128), cols)

    hop = [take(4) for _ in range(2)]

    def first_hop(a):
        for s in (3, 1, 2):
            push(
                sources[a].at[rows_of(near[s])], stage.at[a, s - 1], hop[a] + s, hop[a] + s, plane(s)
            )

    loads["e"].wait()
    first_hop(0)
    at_spots = take(4)
    for step in range(1, 4):
        push(suffix, spots.at[z], at_spots + step, at_spots + step, along(step))

    square = jnp.zeros((seq, 128), jnp.float32)
    for j in range(0, cols, 128):
        block = mine[0, :, j : j + 128].astype(jnp.float32)
        square = square + block * block
    square = jnp.sum(square, axis=1, keepdims=True)
    sums[t] = jnp.broadcast_to(lay_row(square, 128), (8, 128))
    at_sums = take(8)
    for step in range(1, 8):
        push(
            sums.at[t], sums.at[t], at_sums + step, at_sums + step, {"tensor": lax.rem(t + step, 8)}
        )

    for name in "kvqo":
        loads[name].start()

    across = [take(4) for _ in range(2)]
    across_in = [take(4) for _ in range(2)]

    def second_hop(a):
        for s in range(4):
            if s == 0:
                block = sources[a].at[rows_of(chip)]
            else:
                move(stage.at[a, s - 1], stage.at[a, s - 1], 0, hop[a] + s, plane(s)).wait_recv()
                block = stage.at[a, s - 1]
            target = x.at[a, z, rows_of(chip), own_cols]

            @pl.when(near[s] == z)
            def _():
                copy = pltpu.make_async_copy(block, target, own_sem.at[a])
                copy.start()
                copy.wait()

            @pl.when(near[s] != z)
            def _():
                move(block, target, across[a] + s, across_in[a] + z, {"prompt": near[s]}).start()

    second_hop(0)
    loads["d"].wait()
    first_hop(1)
    for step in range(1, 8):
        move(sums.at[t], sums.at[t], 0, at_sums + step, plane(1)).wait_recv()
    square = sums[0]
    for j in range(1, 8):
        square = square + sums[j]
    norms[z] = lax.rsqrt(square / width + EPSILON)
    at_norms = take(4)
    for step in range(1, 4):
        push(norms.at[z], norms.at[z], at_norms + step, at_norms + step, along(step))

    order = (0, 1, 3, 2)
    third = [[take(4) for _ in range(4)] for _ in range(2)]
    fourth = [[take(4) for _ in range(4)] for _ in range(2)]

    def third_hop(a):
        for step in order:
            p = lax.rem(z + step, 4)
            block = x.at[a, p, rows_of(chip), own_cols]
            if step:
                move(block, block, 0, across_in[a] + p, plane(1)).wait_recv()
            for s in (3, 1, 2):
                push(block, block, third[a][step] + s, third[a][step] + s, plane(s))
            push(block, block, third[a][step], third[a][step], {"tensor": pair})

    def fourth_hop(a):
        for step in order:
            p = lax.rem(z + step, 4)
            for s in (1, 2, 3):
                block = x.at[a, p, rows_of(near[s]), own_cols]
                move(block, block, 0, third[a][step] + s, plane(s)).wait_recv()
                push(block, block, fourth[a][step] + s, fourth[a][step] + s, {"tensor": pair})

    def last_hop(a):
        for step in order:
            p = lax.rem(z + step, 4)
            for s in range(4):
                block = x.at[a, p, rows_of(near[s]), pair_cols]
                number = fourth[a][step] + s if s else third[a][step]
                move(block, block, 0, number, {"tensor": pair}).wait_recv()

    third_hop(0)
    second_hop(1)
    fourth_hop(0)
    last_hop(0)
    third_hop(1)

    for step in range(1, 4):
        move(norms.at[z], norms.at[z], 0, at_norms + step, plane(1)).wait_recv()
        move(suffix, spots.at[z], 0, at_spots + step, plane(1)).wait_recv()

    loads["g"].wait()
    loads["s"].wait()
    gain_here = pl.ds(pl.multiple_of(z * rows_here, rows_here), rows_here)
    gain_row[...] = gain_all[gain_here].astype(jnp.float32).reshape(1, rows_here)

    @pl.loop(0, 4)
    def _(p):
        inverse = pick_column(norms[p][:1], seq)
        gains = gain_row[...]
        for j in range(0, rows_here, 512):
            block = x[0, p, :, j : j + 512].astype(jnp.float32)
            block = block * inverse * gains[:, j : j + 512]
            nb[p, :, j : j + 512] = block.astype(jnp.bfloat16)

    loads["k"].wait()
    loads["v"].wait()
    normed = nb[...].reshape(4 * seq, rows_here)
    pkv[...] = dot(normed, wkv[...], plain).reshape(4, seq, 2 * HD)

    is_end = (z == 0) | (z == 3)
    is_mid = (z == 1) | (z == 2)
    end_far, end_mid = 3 - z, 1 + z // 3
    mid_far, mid_near = 6 - 3 * z, 3 * z - 3

    def line_sends(block, into, relay_into, base):
        hand = move(block(end_far), relay_into, base, base + 4, {"prompt": end_mid})
        one = move(block(3 - end_mid), into.at[z], base + 1, base + z, {"prompt": 3 - end_mid})
        two = move(block(end_mid), into.at[z], base + 2, base + z, {"prompt": end_mid})
        over = move(block(3 - z), into.at[z], base, base + z, {"prompt": 3 - z})
        back = move(block(mid_near), into.at[z], base + 1, base + z, {"prompt": mid_near})
        return (hand, one, two), (over, back)

    def line_start(block, into, relay_into, base):
        ends, mids = line_sends(block, into, relay_into, base)

        @pl.when(is_end)
        def _():
            for copy in ends:
                copy.start()

        @pl.when(is_mid)
        def _():
            for copy in mids:
                copy.start()

    def line_relay(block, into, relay_into, base, add, out_block):
        @pl.when(is_mid)
        def _():
            move(relay_into, relay_into, 0, base + 4, {"prompt": mid_far}).wait_recv()
            add()
            move(out_block, into.at[z], base + 2, base + z, {"prompt": mid_far}).start()

    def line_arrive(into, base):
        @pl.when(is_end)
        def _():
            for source in (end_mid, 3 - end_mid):
                move(into.at[z], into.at[z], 0, base + source, plane(1)).wait_recv()

        @pl.when(is_mid)
        def _():
            for source in (0, 3, 3 - z):
                move(into.at[z], into.at[z], 0, base + source, plane(1)).wait_recv()

    def line_sent(block, into, relay_into, base, out_block):
        ends, mids = line_sends(block, into, relay_into, base)

        @pl.when(is_end)
        def _():
            for copy in ends:
                copy.wait_send()

        @pl.when(is_mid)
        def _():
            for copy in mids:
                copy.wait_send()
            move(out_block, into.at[z], base + 2, base + z, {"prompt": mid_far}).wait_send()

    @pl.when(is_end)
    def _():
        rkv[end_far] = jnp.zeros(rkv.shape[1:], rkv.dtype)
        for i in range(2):
            arrived[i, end_far] = jnp.zeros(arrived.shape[2:], arrived.dtype)
            powers_in[i, end_far] = jnp.zeros(powers_in.shape[2:], powers_in.dtype)

    line_kv = take(5)
    line = [take(5) for _ in range(2)]
    line_powers = [take(5) for _ in range(2)]
    kv_args = (lambda d: pkv.at[d], rkv, relay_kv)
    line_start(*kv_args, line_kv)
    for c in range(chunks):
        load_table(c).start()

    def code(i):
        for step in (3, 2, 1):
            d = lax.rem(z + step, 4)

            def write(h, tile):
                if h == heads:
                    powers[i, d] = tile
                else:
                    coded[i, d, :, h * HD : (h + 1) * HD] = tile

            code_block(lambda h: pp[i, d, :, h * HD : (h + 1) * HD], write, heads, seq)

    def line_of(i):
        return (lambda d: coded.at[i, d], arrived.at[i], relay.at[i])

    def powers_of(i):
        return (lambda d: powers.at[i, d], powers_in.at[i], powers_relay.at[i])

    def add_coded(i):
        def add():
            factors = scale_of(powers_relay[i], seq)

            def read(h):
                got = relay[i, :, h * HD : (h + 1) * HD].astype(jnp.int32).astype(jnp.float32)
                return got * factors[:, h : h + 1] + pp[i, mid_far, :, h * HD : (h + 1) * HD]

            def write(h, tile):
                if h == heads:
                    powers_total[i] = tile
                else:
                    total[i, :, h * HD : (h + 1) * HD] = tile

            code_block(read, write, heads, seq)

        return add

    def relay_coded(i):
        @pl.when(is_mid)
        def _():
            for buffer, base in ((relay.at[i], line[i]), (powers_relay.at[i], line_powers[i])):
                move(buffer, buffer, 0, base + 4, {"prompt": mid_far}).wait_recv()
            add_coded(i)()
            for block, into, base in (
                (powers_total.at[i], powers_in.at[i], line_powers[i]),
                (total.at[i], arrived.at[i], line[i]),
            ):
                move(block, into.at[z], base + 2, base + z, {"prompt": mid_far}).start()

    loads["q"].wait()

    @pl.loop(0, head_cols // 256)
    def _(j):
        span = pl.ds(pl.multiple_of(j * 256, 256), 256)
        part = dot(nb[...].reshape(4 * seq, rows_here), wq[:, span], plain)
        pp[0, :, :, span] = part.reshape(4, seq, 256)

    code(0)
    line_start(*powers_of(0), line_powers[0])
    line_start(*line_of(0), line[0])

    def add_kv():
        relay_kv[...] = relay_kv[...] + pkv[mid_far]

    line_relay(*kv_args, line_kv, add_kv, relay_kv)

    fourth_hop(1)
    last_hop(1)
    loads["o"].wait()

    @pl.loop(0, head_cols // 256)
    def _(j):
        span = pl.ds(pl.multiple_of(j * 256, 256), 256)
        part = dot(x[1].reshape(4 * seq, rows_here), wo[span, :], crossed)
        pp[1, :, :, span] = part.reshape(4, seq, 256)

    code(1)
    line_start(*powers_of(1), line_powers[1])
    line_start(*line_of(1), line[1])

    line_arrive(rkv, line_kv)
    own = pkv[z]
    for step in range(1, 4):
        own = own + rkv[lax.rem(z + step, 4)]
    kvg[t] = own.astype(jnp.bfloat16)
    at_kv = take(8)
    for step in range(1, 8):
        push(kvg.at[t], kvg.at[t], at_kv + step, at_kv + step, {"tensor": lax.rem(t + step, 8)})
    relay_coded(0)
    relay_coded(1)

    over = lax.broadcasted_iota(jnp.int32, (rows, count), 1)
    place = jnp.zeros((rows, 1), jnp.float32)
    row_at = lax.broadcasted_iota(jnp.int32, (rows, 1), 0)
    spot_of = row_at // 4
    prompt_of = row_at - 4 * spot_of
    for p in range(4):
        mark = (spot_of == over) & (prompt_of == p)
        found = jnp.where(mark, spots[p].astype(jnp.float32), 0.0)
        place = place + jnp.sum(found, axis=1, keepdims=True)
    place = place + seq * prompt_of.astype(jnp.float32)
    marks = lax.broadcasted_iota(jnp.int32, (rows, 4 * seq), 1).astype(jnp.float32)
    chosen = (marks == place).astype(jnp.bfloat16)
    norm_rows = jnp.zeros((rows, 1), jnp.float32)
    inside = lax.broadcasted_iota(jnp.int32, (rows, 128), 1).astype(jnp.float32)
    for p in range(4):
        hit = (inside + p * seq == place) & (inside < seq)
        norm_rows = norm_rows + jnp.sum(jnp.where(hit, norms[p][:1], 0.0), axis=1, keepdims=True)
    for j in range(0, rows_here, 512):
        block = x[0, :, :, j : j + 512].reshape(4 * seq, 512)
        scaled[:, j : j + 512] = dot(chosen, block, plain) * norm_rows

    def finish(i):
        line_arrive(powers_in.at[i], line_powers[i])
        line_arrive(arrived.at[i], line[i])
        factors = [scale_of(powers_in[i, lax.rem(z + s, 4)], seq) for s in (1, 2, 3)]
        for h in range(heads):
            span = slice(h * HD, (h + 1) * HD)
            value = pp[i, z, :, span]
            for s in (1, 2, 3):
                got = arrived[i, lax.rem(z + s, 4), :, span].astype(jnp.int32)
                value = value + got.astype(jnp.float32) * factors[s - 1][:, h : h + 1]
            whole[i, :, span] = value.astype(jnp.bfloat16)

    finish(0)
    for step in range(1, 8):
        move(kvg.at[t], kvg.at[t], 0, at_kv + step, plane(1)).wait_recv()
    finish(1)

    own_spots = jnp.where(
        lax.broadcasted_iota(jnp.int32, (PAD, count), 0)
        == lax.broadcasted_iota(jnp.int32, (PAD, count), 1),
        spots[z].astype(jnp.float32),
        0.0,
    )
    own_spots = jnp.sum(own_spots, axis=1, keepdims=True)
    real = lax.broadcasted_iota(jnp.int32, (PAD, 1), 0) < count
    own_spots = jnp.where(real, own_spots, -1.0)
    steps_iota = lax.broadcasted_iota(jnp.int32, (PAD, seq), 1).astype(jnp.float32)
    chooser = (steps_iota == own_spots).astype(jnp.bfloat16)
    causal = lax.broadcasted_iota(jnp.int32, (seq, seq), 1) <= lax.broadcasted_iota(
        jnp.int32, (seq, seq), 0
    )
    at_slots, slots_from = take(8), take(8)
    at_grads = take(12)

    def head_grads(group):
        span = {h: slice(h * HD, (h + 1) * HD) for h in group}
        queries = {h: whole[0, :, span[h]] for h in group}
        contexts = {h: whole[1, :, span[h]] for h in group}
        keys = {h: kvg[h, :, :HD] for h in group}
        values = {h: kvg[h, :, HD:] for h in group}
        logits = {h: dot(queries[h], keys[h], crossed) * scale for h in group}
        prob_grad = {h: dot(contexts[h], values[h], crossed) for h in group}
        largest = {
            h: jnp.max(jnp.where(causal, logits[h], -1e30), axis=-1, keepdims=True) for h in group
        }
        raised = {h: jnp.where(causal, jnp.exp(logits[h] - largest[h]), 0.0) for h in group}
        whole_sum = {h: jnp.sum(raised[h], axis=-1, keepdims=True) for h in group}
        probs = {h: raised[h] / whole_sum[h] for h in group}
        probs_low = {h: probs[h].astype(jnp.bfloat16) for h in group}
        less = {h: jnp.sum(prob_grad[h] * probs[h], axis=-1, keepdims=True) for h in group}
        logit_grad = {
            h: (probs[h] * (prob_grad[h] - less[h]) * scale).astype(jnp.bfloat16) for h in group
        }
        logit_rows = {h: dot(chooser, logit_grad[h], plain).astype(jnp.bfloat16) for h in group}
        logit_cols = {h: dot(chooser, logit_grad[h], crossed).astype(jnp.bfloat16) for h in group}
        prob_cols = {h: dot(chooser, probs_low[h], crossed).astype(jnp.bfloat16) for h in group}
        for h in group:
            grads[z, :, span[h]] = dot(logit_rows[h], keys[h], plain).astype(jnp.bfloat16)
            slots[h, :24] = dot(logit_cols[h], queries[h], plain)[:24]
            slots[h, 24:] = dot(prob_cols[h], contexts[h], plain)[:24]

    def send_slots(h):
        return move(slots.at[h], slots_in.at[t], at_slots + h, slots_from + t, {"tensor": h})

    halves = 2
    head_parts = []
    for half in range(halves):
        group = range(half * heads // halves, (half + 1) * heads // halves)
        head_grads(group)
        for h in group:

            @pl.when(t != h)
            def _():
                send_slots(h).start()

        part = grads.at[z, :, group.start * HD : group.stop * HD]
        head_parts.append(part)
        for step in (2, 1, 3):
            number = at_grads + 4 * half + step
            push(part, part, number, number, along(step))
    slots_in[t] = slots[t]
    for step in range(1, 8):
        source = lax.rem(t + step, 8)
        move(slots_in.at[t], slots_in.at[t], 0, slots_from + source, plane(1)).wait_recv()
    summed = slots_in[0]
    for j in range(1, 8):
        summed = summed + slots_in[j]
    filler = jnp.zeros((PAD - 24, HD), jnp.float32)
    key_rows = jnp.concatenate([summed[:24], filler], axis=0)
    value_rows = jnp.concatenate([summed[24:], filler], axis=0)
    grads[z, :, head_cols : head_cols + HD] = key_rows.astype(jnp.bfloat16)
    grads[z, :, head_cols + HD :] = value_rows.astype(jnp.bfloat16)
    tail_part = grads.at[z, :, head_cols:]
    for step in (2, 1, 3):
        push(tail_part, tail_part, at_grads + 8 + step, at_grads + 8 + step, along(step))
    for half in range(halves):
        for step in range(1, 4):
            part = head_parts[half]
            move(part, part, 0, at_grads + 4 * half + step, plane(1)).wait_recv()

    packed_at = lax.broadcasted_iota(jnp.int32, (rows, 4 * PAD), 1)
    packer = (packed_at == PAD * prompt_of + spot_of).astype(jnp.bfloat16)
    packed = dot(packer, grads[:, :, :head_cols].reshape(4 * PAD, head_cols), plain)
    packed = packed.astype(jnp.bfloat16)
    farthest = (3, 1, 2, 0)

    def owned(half, s):
        owner = 2 * near[s] + ((1 - core) if half == 0 else core)
        return pl.ds(pl.multiple_of(owner * slice_width, slice_width), slice_width)

    for half in range(2):
        for s in farthest:
            weighted[half, s] = dot(packed, wq[owned(half, s), :], crossed)
    for step in range(1, 4):
        move(tail_part, tail_part, 0, at_grads + 8 + step, plane(1)).wait_recv()
    packed = dot(packer, grads[:, :, head_cols:].reshape(4 * PAD, 2 * HD), plain)
    packed = packed.astype(jnp.bfloat16)
    inner = jnp.zeros((rows, 128), jnp.float32)
    at_pair, at_shares = take(4), take(4)
    for half in range(2):
        for s in farthest:
            span = owned(half, s)
            part = weighted[half, s] + dot(packed, wkv[span, :], crossed)
            part = part * gain_row[:, span]
            product = part * scaled[:, span]
            for j in range(0, slice_width, 128):
                inner = inner + product[:, j : j + 128]
            weighted[half, s] = part
            if half == 0:
                push(weighted.at[0, s], pair_in.at[s], at_pair + s, at_pair + s, {"tensor": pair})
    for s in farthest:
        move(pair_in.at[s], pair_in.at[s], 0, at_pair + s, {"tensor": pair}).wait_recv()
        weighted[1, s] = weighted[1, s] + pair_in[s]
        if s:
            push(weighted.at[1, s], shares.at[s - 1], at_shares + s, at_shares + s, plane(s))
    inner = jnp.sum(inner, axis=1, keepdims=True)
    inner_in[t] = jnp.broadcast_to(lay_row(inner, 128), (8, 128))
    at_inner = take(8)
    for step in range(1, 8):
        push(
            inner_in.at[t],
            inner_in.at[t],
            at_inner + step,
            at_inner + step,
            {"tensor": lax.rem(t + step, 8)},
        )
    for step in range(1, 8):
        move(inner_in.at[t], inner_in.at[t], 0, at_inner + step, plane(1)).wait_recv()
    inner = inner_in[0]
    for j in range(1, 8):
        inner = inner + inner_in[j]
    inner_z[z] = inner
    at_inner_z = take(4)
    for step in range(1, 4):
        push(inner_z.at[z], inner_z.at[z], at_inner_z + step, at_inner_z + step, along(step))
    for s in (1, 2, 3):
        move(shares.at[s - 1], shares.at[s - 1], 0, at_shares + s, plane(1)).wait_recv()
    own = weighted[1, 0] + shares[0] + shares[1] + shares[2]
    for step in range(1, 4):
        move(inner_z.at[z], inner_z.at[z], 0, at_inner_z + step, plane(1)).wait_recv()
    inner = (inner_z[0] + inner_z[1] + inner_z[2] + inner_z[3])[:1]
    inner = pick_column(inner, rows) / width

    here = pl.ds(pl.multiple_of(t * slice_width, slice_width), slice_width)
    suffix_grads[z, :, here] = (norm_rows * (own - scaled[:, here] * inner)).astype(jnp.bfloat16)

    def grad_of(p, chip_index, core_index):
        first = (2 * chip_index + core_index) * slice_width
        return suffix_grads.at[p, :, pl.ds(pl.multiple_of(first, slice_width), slice_width)]

    at_z = take(4)
    spread = [take(4) for _ in range(4)]
    doubled = [take(4) for _ in range(4)]
    mine_now = grad_of(z, chip, core)
    for step in (2, 1, 3):
        push(mine_now, mine_now, at_z + step, at_z + step, along(step))

    def to_plane(step):
        block = grad_of(lax.rem(z - step + 4, 4), chip, core)
        if step:
            move(block, block, 0, at_z + step, plane(1)).wait_recv()
        for s in (3, 1, 2):
            push(block, block, spread[step] + s, spread[step] + s, plane(s))
        push(block, block, spread[step], spread[step], {"tensor": pair})

    def to_pair(step):
        p = lax.rem(z - step + 4, 4)
        for s in (1, 2, 3):
            block = grad_of(p, near[s], core)
            move(block, block, 0, spread[step] + s, plane(s)).wait_recv()
            push(block, block, doubled[step] + s, doubled[step] + s, {"tensor": pair})

    def from_pair(step):
        p = lax.rem(z - step + 4, 4)
        for s in range(4):
            block = grad_of(p, near[s], 1 - core)
            number = doubled[step] + s if s else spread[step]
            move(block, block, 0, number, {"tensor": pair}).wait_recv()

    def multiply(step, half):
        p = lax.rem(z - step + 4, 4)
        features = pl.ds(pl.multiple_of(p * rows_here, rows_here), rows_here)
        wide = vocab.shape[0] // 2
        span = pl.ds(half * wide, wide)
        part = dot(suffix_grads[p], table[span, features], crossed)
        if step != order[0]:
            part = part + partial[:, span]
        if step != order[-1]:
            partial[:, span] = part
            return
        part = jnp.where(barred[:, span] == 1, 0.0, -part)
        for n in range(count):
            out[n, :, span] = part[4 * n : 4 * n + 4]

    to_plane(0)
    to_plane(1)
    to_pair(0)
    for c in range(chunks):
        load_table(c).wait()
    loads["b"].wait()
    from_pair(0)
    multiply(0, 0)
    to_plane(3)
    to_plane(2)
    to_pair(1)
    multiply(0, 1)
    from_pair(1)
    multiply(1, 0)
    to_pair(3)
    multiply(1, 1)
    from_pair(3)
    multiply(3, 0)
    to_pair(2)
    multiply(3, 1)
    from_pair(2)
    multiply(2, 0)
    multiply(2, 1)

    for copy in sent:
        copy.wait_send()
    for h in range(heads):

        @pl.when(t != h)
        def _():
            send_slots(h).wait_send()

    for a in range(2):
        for s in range(4):

            @pl.when(near[s] != z)
            def _():
                block = x.at[a, z, rows_of(chip), own_cols]
                move(block, block, across[a] + s, 0, {"prompt": near[s]}).wait_send()

    line_sent(*kv_args, line_kv, relay_kv)
    for i in range(2):
        line_sent(*powers_of(i), line_powers[i], powers_total.at[i])
        line_sent(*line_of(i), line[i], total.at[i])


def fused(
    embeds,
    norm_gain,
    query_weight,
    key_weight,
    value_weight,
    out_weight,
    out_grad,
    suffix_pos,
    vocab_table,
    banned,
):
    seq, cols = embeds.shape[1:]
    rows_here, head_cols = query_weight.shape
    count = suffix_pos.shape[1]
    vocab_here, width = vocab_table.shape
    heads = head_cols // HD
    rows = 4 * count
    slice_width = rows_here // 8
    low, full, short = jnp.bfloat16, jnp.float32, jnp.int16
    coded = head_cols
    local = pl.BlockSpec(memory_space=pltpu.VMEM)
    apart = pl.BlockSpec(memory_space=pl.ANY)
    scratch = [
        ((rows_here, head_cols), low),
        ((rows_here, 2 * HD), low),
        ((head_cols, rows_here), low),
        (vocab_table.shape, low),
        ((2, seq, cols), low),
        ((2, 3, seq // 4, cols), low),
        ((2, 4, seq, rows_here), low),
        ((8, 8, 128), full),
        ((4, 8, 128), full),
        ((4, 1, count), jnp.int32),
        ((4, seq, rows_here), low),
        ((4, seq, 2 * HD), full),
        ((4, seq, 2 * HD), full),
        ((seq, 2 * HD), full),
        ((2, 4, seq, head_cols), full),
        ((2, 4, seq, coded), short),
        ((2, 4, seq, coded), short),
        ((2, seq, coded), short),
        ((2, seq, coded), short),
        ((2, 4, 16, HD), short),
        ((2, 4, 16, HD), short),
        ((2, 16, HD), short),
        ((2, 16, HD), short),
        ((8, seq, 2 * HD), low),
        ((2, seq, head_cols), low),
        ((8, 48, HD), full),
        ((8, 48, HD), full),
        ((4, PAD, head_cols + 2 * HD), low),
        ((rows, rows_here), full),
        ((2, 4, rows, slice_width), full),
        ((4, rows, slice_width), full),
        ((3, rows, slice_width), full),
        ((8, 8, 128), full),
        ((4, 8, 128), full),
        ((4, rows, rows_here), low),
        ((rows, vocab_here), full),
        ((1, rows_here), full),
        ((width,), low),
        ((1, vocab_here), jnp.int32),
    ]
    scores = pl.pallas_call(
        fused_kernel,
        out_shape=jax.ShapeDtypeStruct((count, 4, vocab_here), full),
        in_specs=[apart] * 10,
        out_specs=local,
        scratch_shapes=[pltpu.VMEM(shape, dtype) for shape, dtype in scratch]
        + [
            pltpu.SemaphoreType.DMA((SEMS,)),
            pltpu.SemaphoreType.DMA((SEMS,)),
            pltpu.SemaphoreType.DMA((8 + vocab_here // CHUNK,)),
            pltpu.SemaphoreType.DMA((3,)),
        ],
        compiler_params=pltpu.CompilerParams(
            collective_id=11, has_side_effects=True, vmem_limit_bytes=60 << 20
        ),
    )(
        embeds,
        out_grad,
        norm_gain,
        query_weight,
        key_weight,
        value_weight,
        out_weight,
        suffix_pos,
        vocab_table,
        banned.reshape(1, -1),
    )
    return scores.transpose(1, 0, 2)


def fits(mesh_sizes, arrays):
    embeds, query_weight, key_weight, suffix_pos, vocab_table = arrays
    return (
        mesh_sizes == (4, 8)
        and embeds.shape[1] == 64
        and query_weight.shape[1] == 8 * HD
        and key_weight.shape[1] == HD
        and query_weight.shape[0] == 2 * embeds.shape[2]
        and query_weight.shape[0] % 2048 == 0
        and suffix_pos.shape[1] == 20
        and vocab_table.shape[0] % CHUNK == 0
    )


def part_of(*args):
    sizes = (lax.axis_size("prompt"), lax.axis_size("tensor"))
    if fits(sizes, (args[0], args[2], args[3], args[7], args[8])):
        return fused(*args)
    return on_device(*args)


def solution(mesh):
    return jax.shard_map(
        part_of,
        mesh=mesh,
        in_specs=(
            P("prompt", None, "tensor"),
            P(),
            P("prompt", "tensor"),
            P("prompt", "tensor"),
            P("prompt", "tensor"),
            P("tensor", "prompt"),
            P("prompt", None, "tensor"),
            P("prompt", None),
            P(("prompt", "tensor"), None),
            P(("prompt", "tensor")),
        ),
        out_specs=P(None, None, ("prompt", "tensor")),
        check_vma=False,
    )
```

```python
import functools
import math

import jax
import jax.numpy as jnp
from jax import lax
from jax.experimental import pallas as pl
from jax.experimental.pallas import tpu as pltpu
from jax.sharding import PartitionSpec as P

KVH = 8
HD = 128


EPSILON = 1e-05


def exchange_kernel(axis, count, spread, *refs):
    arrays = len(spread)
    sources, targets = refs[:arrays], refs[arrays : 2 * arrays]
    send_sem, recv_sem, own_sem = refs[2 * arrays :]
    here = lax.axis_index(axis)

    def block(i, to):
        return sources[i].at[to] if spread[i] else sources[i]

    kept = []
    for i in range(arrays):
        copy = pltpu.make_async_copy(block(i, here), targets[i].at[here], own_sem.at[i])
        copy.start()
        kept.append(copy)
    barrier = pltpu.get_barrier_semaphore()
    for step in range(1, count):
        peer = lax.rem(here + step, count)
        pl.semaphore_signal(
            barrier, inc=1, device_id={axis: peer}, device_id_type=pl.DeviceIdType.MESH
        )
    pl.semaphore_wait(barrier, count - 1)
    copies = []
    for step in range(1, count):
        peer = lax.rem(here + step, count)
        for i in range(arrays):
            copy = pltpu.make_async_remote_copy(
                src_ref=block(i, peer),
                dst_ref=targets[i].at[here],
                send_sem=send_sem.at[i, step - 1],
                recv_sem=recv_sem.at[i, step - 1],
                device_id={axis: peer},
                device_id_type=pl.DeviceIdType.MESH,
            )
            copy.start()
            copies.append(copy)
    for copy in kept + copies:
        copy.wait()


def exchange(axis, number, *operands):
    count = lax.axis_size(axis)
    arrays = [array for array, _ in operands]
    spread = tuple(each for _, each in operands)
    shapes = [
        jax.ShapeDtypeStruct(((count,) + (a.shape[1:] if each else a.shape)), a.dtype)
        for a, each in operands
    ]
    space = pl.BlockSpec(memory_space=pltpu.VMEM)
    sems = pltpu.SemaphoreType.DMA((len(arrays), count - 1))
    return pl.pallas_call(
        functools.partial(exchange_kernel, axis, count, spread),
        out_shape=shapes,
        in_specs=[space] * len(arrays),
        out_specs=[space] * len(arrays),
        scratch_shapes=[sems, sems, pltpu.SemaphoreType.DMA((len(arrays),))],
        compiler_params=pltpu.CompilerParams(
            collective_id=number, has_side_effects=True, vmem_limit_bytes=40 << 20
        ),
    )(*arrays)


def dot_f32(spec, a, b):
    return jnp.einsum(spec, a, b, preferred_element_type=jnp.float32)


MESH = pl.DeviceIdType.MESH


def greet(axis, peers):
    barrier = pltpu.get_barrier_semaphore()
    for peer in peers:
        pl.semaphore_signal(barrier, inc=1, device_id={axis: peer}, device_id_type=MESH)
    pl.semaphore_wait(barrier, len(peers))


def gather_kernel(axis, count, arrays, *refs):
    sources, targets = refs[:arrays], refs[arrays : 2 * arrays]
    send_sem, recv_sem, own_sem = refs[2 * arrays :]
    here = lax.axis_index(axis)
    chips = count // 2
    chip, core = here // 2, lax.rem(here, 2)
    pair = 2 * chip + (1 - core)
    kept = []
    for i in range(arrays):
        copy = pltpu.make_async_copy(sources[i], targets[i].at[here], own_sem.at[i])
        copy.start()
        kept.append(copy)

    def push(i, source, slot, number, peer):
        return pltpu.make_async_remote_copy(
            src_ref=source,
            dst_ref=targets[i].at[slot],
            send_sem=send_sem.at[i, number],
            recv_sem=recv_sem.at[i, number],
            device_id={axis: peer},
            device_id_type=MESH,
        )

    others = [2 * lax.rem(chip + step, chips) + core for step in range(1, chips)]
    greet(axis, others + [pair])
    first = []
    for step in range(1, chips):
        for i in range(arrays):
            copy = push(i, sources[i], here, step, others[step - 1])
            copy.start()
            first.append(copy)
    rest = []
    for i in range(arrays):
        copy = push(i, sources[i], here, 0, pair)
        copy.start()
        rest.append(copy)
    for step in range(1, chips):
        slot = 2 * lax.rem(chip + chips - step, chips) + core
        for i in range(arrays):
            first[(step - 1) * arrays + i].wait_recv()
            copy = push(i, targets[i].at[slot], slot, chips - 1 + step, pair)
            copy.start()
            rest.append(copy)
    for copy in first:
        copy.wait_send()
    for copy in kept + rest:
        copy.wait()


def gather(axis, number, *arrays):
    count = lax.axis_size(axis)
    shapes = [jax.ShapeDtypeStruct((count,) + a.shape, a.dtype) for a in arrays]
    space = pl.BlockSpec(memory_space=pltpu.VMEM)
    sems = pltpu.SemaphoreType.DMA((len(arrays), count - 1))
    return pl.pallas_call(
        functools.partial(gather_kernel, axis, count, len(arrays)),
        out_shape=shapes,
        in_specs=[space] * len(arrays),
        out_specs=[space] * len(arrays),
        scratch_shapes=[sems, sems, pltpu.SemaphoreType.DMA((len(arrays),))],
        compiler_params=pltpu.CompilerParams(
            collective_id=number, has_side_effects=True, vmem_limit_bytes=40 << 20
        ),
    )(*arrays)


def line_kernel(axis, source, target, relay, send_sem, recv_sem, own_sem):
    here = lax.axis_index(axis)
    own = pltpu.make_async_copy(source.at[here], target.at[here], own_sem.at[0])
    own.start()
    greet(axis, [lax.rem(here + step, 4) for step in range(1, 4)])

    def push(block, slot, number, peer, into=None):
        return pltpu.make_async_remote_copy(
            src_ref=block,
            dst_ref=target.at[slot] if into is None else into,
            send_sem=send_sem.at[number],
            recv_sem=recv_sem.at[slot if into is None else 4],
            device_id={axis: peer},
            device_id_type=MESH,
        )

    for role in range(4):
        far = 3 if role < 2 else 0
        middle = 1 if role < 2 else 2
        across = 3 - middle

        @pl.when(here == role)
        def _():
            if role == middle:
                sent = [
                    push(source.at[across], role, 0, across),
                    push(source.at[3 - far], role, 1, 3 - far),
                ]
                for copy in sent:
                    copy.start()
                total = push(relay, role, 2, far)
                push(source.at[far], role, 3, far, relay).wait_recv()
                relay[...] = relay[...] + source[far]
                total.start()
                sent.append(total)
                arriving = [0, across, 3]
            else:
                handed = push(source.at[far], role, 0, middle, relay)
                handed.start()
                target[far] = jnp.zeros_like(target[far])
                handed.wait_send()
                sent = [
                    push(source.at[across], role, 1, across),
                    push(source.at[middle], role, 2, middle),
                ]
                for copy in sent:
                    copy.start()
                arriving = [1, 2]
            for slot in arriving:
                push(source.at[slot], slot, 3, slot).wait_recv()
            for copy in sent:
                copy.wait_send()

    own.wait()


def line_exchange(axis, number, blocks):
    if lax.axis_size(axis) != 4:
        return exchange(axis, number, (blocks, True))[0]
    space = pl.BlockSpec(memory_space=pltpu.VMEM)
    return pl.pallas_call(
        functools.partial(line_kernel, axis),
        out_shape=jax.ShapeDtypeStruct(blocks.shape, blocks.dtype),
        in_specs=[space],
        out_specs=space,
        scratch_shapes=[
            pltpu.VMEM(blocks.shape[1:], blocks.dtype),
            pltpu.SemaphoreType.DMA((4,)),
            pltpu.SemaphoreType.DMA((5,)),
            pltpu.SemaphoreType.DMA((1,)),
        ],
        compiler_params=pltpu.CompilerParams(
            collective_id=number, has_side_effects=True, vmem_limit_bytes=40 << 20
        ),
    )(blocks)


CHUNK = 512


def score_kernel(
    axis, count, part, vocab, scores, got, flat, table, send_sem, recv_sem, own_sem, load_sem
):
    def load(c):
        span = pl.ds(pl.multiple_of(c * CHUNK, CHUNK), CHUNK)
        return pltpu.make_async_copy(vocab.at[span], table.at[span], load_sem.at[c])

    chunks = vocab.shape[0] // CHUNK
    for c in range(chunks):
        load(c).start()
    gather_kernel(axis, count, 1, part, got, send_sem, recv_sem, own_sem)
    wide = part.shape[2]
    for p in range(part.shape[0]):
        for t in range(count):
            start = (p * count + t) * wide
            flat[:, start : start + wide] = got[t, p]

    @pl.loop(0, chunks)
    def _(c):
        load(c).wait()
        span = pl.ds(pl.multiple_of(c * CHUNK, CHUNK), CHUNK)
        scores[:, span] = -lax.dot_general(
            flat[...],
            table[span, :],
            (((1,), (1,)), ((), ())),
            preferred_element_type=jnp.float32,
        )


def gather_score(axis, number, part, vocab):
    count = lax.axis_size(axis)
    n_prompt, rows, wide = part.shape
    vocab_here, width = vocab.shape
    if wide % 128 or vocab_here % CHUNK or rows % 16:
        (part,) = gather(axis, number, part)
        return -dot_f32("rd,vd->rv", part.transpose(2, 1, 0, 3).reshape(rows, width), vocab)
    sems = pltpu.SemaphoreType.DMA((1, count - 1))
    return pl.pallas_call(
        functools.partial(score_kernel, axis, count),
        out_shape=jax.ShapeDtypeStruct((rows, vocab_here), jnp.float32),
        in_specs=[pl.BlockSpec(memory_space=pltpu.VMEM), pl.BlockSpec(memory_space=pl.ANY)],
        out_specs=pl.BlockSpec(memory_space=pltpu.VMEM),
        scratch_shapes=[
            pltpu.VMEM((count,) + part.shape, part.dtype),
            pltpu.VMEM((rows, width), part.dtype),
            pltpu.VMEM(vocab.shape, vocab.dtype),
            sems,
            sems,
            pltpu.SemaphoreType.DMA((1,)),
            pltpu.SemaphoreType.DMA((vocab_here // CHUNK,)),
        ],
        compiler_params=pltpu.CompilerParams(
            collective_id=number, has_side_effects=True, vmem_limit_bytes=52 << 20
        ),
    )(part, vocab)


def on_device(
    embeds,
    norm_gain,
    query_weight,
    key_weight,
    value_weight,
    out_weight,
    out_grad,
    suffix_pos,
    vocab_table,
    banned,
):
    n_prompt = lax.axis_size("prompt")
    n_tensor = lax.axis_size("tensor")
    here_prompt = lax.axis_index("prompt")
    here_tensor = lax.axis_index("tensor")
    seq_len = embeds.shape[1]
    suffix_count = suffix_pos.shape[1]
    width = embeds.shape[2] * n_tensor
    rows_here, head_cols = query_weight.shape
    key_cols = key_weight.shape[1]
    heads_here = head_cols // HD
    slice_width = rows_here // n_tensor
    logit_scale = 1.0 / math.sqrt(HD)

    split_rows = seq_len // n_tensor
    ratio = n_tensor // n_prompt
    feature_cols = embeds.shape[2]
    both = jnp.concatenate(
        [
            embeds.reshape(n_tensor, split_rows, feature_cols),
            out_grad.reshape(n_tensor, split_rows, feature_cols),
        ],
        axis=1,
    )
    (both,) = exchange("tensor", 0, (both, True))
    own = both[:, :split_rows].astype(jnp.float32)
    inverse_norm = lax.rsqrt(jnp.sum(own * own, axis=(0, 2))[:, None] / width + EPSILON)
    inverse_norm = jnp.broadcast_to(inverse_norm, (split_rows, 128))
    both = both.reshape(n_prompt, ratio, 2 * split_rows, feature_cols)
    both, inverse_norm, suffix_all = exchange(
        "prompt", 1, (both, True), (inverse_norm, False), (suffix_pos, False)
    )
    both, inverse_norm = gather("tensor", 2, both, inverse_norm)
    suffix_all = suffix_all.reshape(n_prompt, suffix_count)
    both = both.reshape(n_tensor, n_prompt, ratio, 2, split_rows, feature_cols)
    both = both.transpose(3, 1, 0, 4, 2, 5).reshape(2, n_prompt, seq_len, rows_here)
    embeds, out_grad = both[0], both[1]
    inverse_norm = inverse_norm[..., :1].transpose(1, 0, 2, 3).reshape(n_prompt, seq_len, 1)
    embeds_float = embeds.astype(jnp.float32)
    gain_rows = lax.dynamic_slice_in_dim(norm_gain, here_prompt * rows_here, rows_here, 0)
    gain_rows = gain_rows.astype(jnp.float32)
    normed = (embeds_float * inverse_norm * gain_rows).astype(jnp.bfloat16)

    parts = jnp.concatenate(
        [
            dot_f32("psd,dc->psc", normed, query_weight),
            dot_f32("psd,dc->psc", normed, key_weight),
            dot_f32("psd,dc->psc", normed, value_weight),
            dot_f32("psd,cd->psc", out_grad, out_weight),
        ],
        axis=2,
    )
    parts = line_exchange("prompt", 3, parts)
    whole = jnp.sum(parts, axis=0).astype(jnp.bfloat16)
    contexts = whole[:, head_cols + 2 * key_cols :]
    contexts = contexts.reshape(seq_len, heads_here, HD)
    queries = whole[:, :head_cols].reshape(seq_len, heads_here, HD)
    (key_values,) = gather("tensor", 4, whole[:, head_cols : head_cols + 2 * key_cols])
    key_values = key_values.reshape(n_tensor, seq_len, 2, key_cols).transpose(2, 1, 0, 3)
    key_values = key_values.reshape(2, seq_len, KVH * HD)
    fold = min(heads_here, KVH)
    first = ((here_tensor * heads_here) % KVH) * HD
    if fold < KVH:
        key_values = lax.dynamic_slice_in_dim(key_values, first, fold * HD, 2)
    key_values = key_values.reshape(2, seq_len, fold, HD)
    if heads_here > fold:
        key_values = jnp.tile(key_values, (1, 1, heads_here // fold, 1))
    keys, values = key_values[0], key_values[1]

    logits = dot_f32("qhd,khd->hqk", queries, keys) * logit_scale
    row_index = lax.broadcasted_iota(jnp.int32, (seq_len, seq_len), 0)
    col_index = lax.broadcasted_iota(jnp.int32, (seq_len, seq_len), 1)
    causal = col_index <= row_index
    largest = jnp.max(jnp.where(causal, logits, -1e30), axis=-1, keepdims=True)
    raised = jnp.where(causal, jnp.exp(logits - largest), 0.0)
    probs = raised / jnp.sum(raised, axis=-1, keepdims=True)
    probs_low = probs.astype(jnp.bfloat16)
    prob_grad = dot_f32("qhd,khd->hqk", contexts, values)
    logit_grad = (
        probs * (prob_grad - jnp.sum(prob_grad * probs, axis=-1, keepdims=True)) * logit_scale
    ).astype(jnp.bfloat16)
    steps_iota = lax.broadcasted_iota(jnp.int32, (suffix_count, seq_len), 1)
    chooser = (steps_iota == suffix_pos[0][:, None]).astype(jnp.bfloat16)
    logit_rows = dot_f32("ns,hsk->hnk", chooser, logit_grad).astype(jnp.bfloat16)
    query_grad = dot_f32("hnk,khd->nhd", logit_rows, keys).astype(jnp.bfloat16)
    query_grad = query_grad.reshape(suffix_count, head_cols)
    logit_cols = dot_f32("hqk,nk->hnq", logit_grad, chooser).astype(jnp.bfloat16)
    prob_cols = dot_f32("hqk,nk->hnq", probs_low, chooser).astype(jnp.bfloat16)
    key_each = dot_f32("hnq,qhd->nhd", logit_cols, queries)
    value_each = dot_f32("hnq,qhd->nhd", prob_cols, contexts)
    slots = jnp.stack([key_each, value_each])
    slots = slots.reshape(2, suffix_count, heads_here // fold, fold * HD).sum(axis=2)
    if fold < KVH:
        slots = lax.dynamic_update_slice_in_dim(
            jnp.zeros((2, suffix_count, KVH * HD), jnp.float32), slots, first, 2
        )
    slots = slots.reshape(2 * suffix_count, n_tensor, key_cols).transpose(1, 0, 2)
    (grads,) = exchange("tensor", 5, (slots, True))
    grads = jnp.sum(grads, axis=0).astype(jnp.bfloat16).reshape(2, suffix_count, key_cols)
    grads = jnp.concatenate([query_grad, grads[0], grads[1]], axis=1)
    (grads,) = exchange("prompt", 6, (grads, False))
    rows = n_prompt * suffix_count
    grads = grads.reshape(rows, head_cols + 2 * key_cols)
    steps_iota = lax.broadcasted_iota(jnp.int32, (n_prompt, suffix_count, seq_len), 2)
    chooser_all = steps_iota == suffix_all[:, :, None]
    embed_rows = dot_f32("pns,psd->pnd", chooser_all.astype(jnp.bfloat16), embeds)
    norm_rows = jnp.sum(
        jnp.where(chooser_all, inverse_norm[:, None, :, 0], 0.0), axis=-1, keepdims=True
    )
    scaled = (embed_rows * norm_rows).reshape(rows, rows_here)
    norm_rows = norm_rows.reshape(rows, 1)
    branch = dot_f32("nc,dc->nd", grads[:, :head_cols], query_weight)
    branch = branch + dot_f32("nc,dc->nd", grads[:, head_cols : head_cols + key_cols], key_weight)
    branch = branch + dot_f32("nc,dc->nd", grads[:, head_cols + key_cols :], value_weight)
    branch = branch * gain_rows
    inner = jnp.sum(branch * scaled, axis=-1)
    branch = branch.reshape(rows, n_tensor, slice_width).transpose(1, 0, 2)
    share, inner = exchange("tensor", 7, (branch, True), (inner[None, :], False))
    weighted = jnp.sum(share, axis=0)
    (inner,) = exchange("prompt", 8, (jnp.sum(inner, axis=0), False))
    inner = jnp.sum(inner, axis=0).reshape(rows, 1) / width
    scaled = lax.dynamic_slice_in_dim(scaled, here_tensor * slice_width, slice_width, 1)
    suffix_grad = (norm_rows * (weighted - scaled * inner)).astype(jnp.bfloat16)
    (suffix_grad,) = exchange("prompt", 9, (suffix_grad, False))
    scores = gather_score("tensor", 10, suffix_grad, vocab_table)
    scores = scores.reshape(n_prompt, suffix_count, vocab_table.shape[0])
    return jnp.where(banned[None, None, :] == 1, 0.0, scores)


PAD = 32
TINY = 1e-30
FULL = 32767.0
SEMS = 232


def pick_column(row, rows):
    wide = row.shape[1]
    down = lax.broadcasted_iota(jnp.int32, (rows, wide), 0)
    along = lax.broadcasted_iota(jnp.int32, (rows, wide), 1)
    return jnp.sum(jnp.where(down == along, row, 0.0), axis=1, keepdims=True)


def lay_row(column, wide):
    rows = column.shape[0]
    down = lax.broadcasted_iota(jnp.int32, (rows, wide), 0)
    along = lax.broadcasted_iota(jnp.int32, (rows, wide), 1)
    return jnp.sum(jnp.where(down == along, column, 0.0), axis=0, keepdims=True)


def lane_sums(values):
    total = values[:, :128]
    for j in range(128, values.shape[1], 128):
        total = total + values[:, j : j + 128]
    return jnp.sum(total, axis=1, keepdims=True)


def code_block(read, write, heads, rows):
    lanes = lax.broadcasted_iota(jnp.int32, (rows, HD), 1)
    powers = jnp.zeros((rows, HD), jnp.float32)
    for h in range(heads):
        block = read(h)
        peak = jnp.max(jnp.abs(block), axis=1, keepdims=True)
        power = jnp.floor(jnp.log2(jnp.maximum(peak, TINY))) + 1.0
        fixed = jnp.floor(block * (jnp.exp2(-power) * FULL) + 0.5)
        fixed = jnp.clip(fixed, -FULL, FULL)
        write(h, fixed.astype(jnp.int32).astype(jnp.int16))
        powers = jnp.where(lanes == h, power, powers)
    square = jnp.concatenate([powers, jnp.zeros((HD - rows, HD), jnp.float32)], axis=0).T
    write(heads, square[:16].astype(jnp.int32).astype(jnp.int16))


def scale_of(tile, rows):
    factors = jnp.exp2(tile.astype(jnp.int32).astype(jnp.float32)) * (1.0 / FULL)
    square = jnp.concatenate([factors, jnp.zeros((HD - 16, HD), jnp.float32)], axis=0).T
    return square[:rows]


def fused_kernel(
    embeds,
    out_grad,
    gain,
    query_weight,
    key_weight,
    value_weight,
    out_weight,
    suffix,
    vocab,
    banned,
    out,
    wq,
    wkv,
    wo,
    table,
    mine,
    stage,
    x,
    sums,
    norms,
    spots,
    nb,
    pkv,
    rkv,
    relay_kv,
    pp,
    coded,
    arrived,
    relay,
    total,
    powers,
    powers_in,
    powers_relay,
    powers_total,
    kvg,
    whole,
    slots,
    slots_in,
    grads,
    scaled,
    weighted,
    pair_in,
    shares,
    inner_in,
    inner_z,
    suffix_grads,
    partial,
    gain_row,
    gain_all,
    barred,
    result,
    send_sem,
    recv_sem,
    load_sem,
    own_sem,
):
    z = lax.axis_index("prompt")
    t = lax.axis_index("tensor")
    chip, core = t // 2, lax.rem(t, 2)
    pair = 2 * chip + (1 - core)
    chip_y, chip_x = chip // 2, lax.rem(chip, 2)
    near = [
        chip,
        2 * chip_y + (1 - chip_x),
        2 * (1 - chip_y) + chip_x,
        2 * (1 - chip_y) + (1 - chip_x),
    ]
    seq, cols = embeds.shape[1], embeds.shape[2]
    width = gain.shape[0]
    rows_here, head_cols = query_weight.shape
    heads = head_cols // HD
    count = suffix.shape[1]
    rows = 4 * count
    quarter = seq // 4
    slice_width = rows_here // 8
    scale = 1.0 / math.sqrt(HD)
    dot = functools.partial(lax.dot_general, preferred_element_type=jnp.float32)
    plain = (((1,), (0,)), ((), ()))
    crossed = (((1,), (1,)), ((), ()))

    chunks = vocab.shape[0] // CHUNK

    def load_table(c):
        span = pl.ds(pl.multiple_of(c * CHUNK, CHUNK), CHUNK)
        return pltpu.make_async_copy(vocab.at[span], table.at[span], load_sem.at[8 + c])

    loads = {
        "g": pltpu.make_async_copy(gain, gain_all, load_sem.at[5]),
        "b": pltpu.make_async_copy(banned, barred, load_sem.at[6]),
        "s": pltpu.make_async_copy(suffix, spots.at[z], load_sem.at[7]),
        "e": pltpu.make_async_copy(embeds.at[0], mine.at[0], load_sem.at[0]),
        "d": pltpu.make_async_copy(out_grad.at[0], mine.at[1], own_sem.at[2]),
        "k": pltpu.make_async_copy(key_weight, wkv.at[:, :HD], load_sem.at[1]),
        "v": pltpu.make_async_copy(value_weight, wkv.at[:, HD:], load_sem.at[2]),
        "q": pltpu.make_async_copy(query_weight, wq, load_sem.at[3]),
        "o": pltpu.make_async_copy(out_weight, wo, load_sem.at[4]),
    }
    for name in "edgbs":
        loads[name].start()

    barrier = pltpu.get_barrier_semaphore()
    for step in range(1, 8):
        pl.semaphore_signal(
            barrier, inc=1, device_id={"tensor": lax.rem(t + step, 8)}, device_id_type=MESH
        )
    for step in range(1, 4):
        pl.semaphore_signal(
            barrier, inc=1, device_id={"prompt": lax.rem(z + step, 4)}, device_id_type=MESH
        )
    pl.semaphore_wait(barrier, 10)

    used = [0]
    sent = []

    def take(number=1):
        used[0] += number
        assert used[0] <= SEMS
        return used[0] - number

    def move(source, target, s, r, device):
        return pltpu.make_async_remote_copy(
            src_ref=source,
            dst_ref=target,
            send_sem=send_sem.at[s],
            recv_sem=recv_sem.at[r],
            device_id=device,
            device_id_type=MESH,
        )

    def push(source, target, s, r, device):
        copy = move(source, target, s, r, device)
        copy.start()
        sent.append(copy)

    def plane(s, other=False):
        return {"tensor": 2 * near[s] + ((1 - core) if other else core)}

    def along(step):
        return {"prompt": lax.rem(z + step, 4)}

    def rows_of(chip_index):
        return pl.ds(pl.multiple_of(quarter * chip_index, quarter), quarter)

    sources = (mine.at[0], mine.at[1])
    own_cols = pl.ds(pl.multiple_of(core * cols, 128), cols)
    pair_cols = pl.ds(pl.multiple_of((1 - core) * cols, 128), cols)

    hop = [take(4) for _ in range(2)]

    def first_hop(a):
        for s in (3, 1, 2):
            push(
                sources[a].at[rows_of(near[s])], stage.at[a, s - 1], hop[a] + s, hop[a] + s, plane(s)
            )

    loads["e"].wait()
    first_hop(0)
    at_spots = take(4)
    for step in range(1, 4):
        push(suffix, spots.at[z], at_spots + step, at_spots + step, along(step))

    square = jnp.zeros((seq, 128), jnp.float32)
    for j in range(0, cols, 128):
        block = mine[0, :, j : j + 128].astype(jnp.float32)
        square = square + block * block
    square = jnp.sum(square, axis=1, keepdims=True)
    sums[t] = jnp.broadcast_to(lay_row(square, 128), (8, 128))
    at_sums = take(8)
    for step in range(1, 8):
        push(
            sums.at[t], sums.at[t], at_sums + step, at_sums + step, {"tensor": lax.rem(t + step, 8)}
        )

    for name in "kvqo":
        loads[name].start()

    across = [take(4) for _ in range(2)]
    across_in = [take(4) for _ in range(2)]

    def second_hop(a):
        for s in range(4):
            if s == 0:
                block = sources[a].at[rows_of(chip)]
            else:
                move(stage.at[a, s - 1], stage.at[a, s - 1], 0, hop[a] + s, plane(s)).wait_recv()
                block = stage.at[a, s - 1]
            target = x.at[a, z, rows_of(chip), own_cols]

            @pl.when(near[s] == z)
            def _():
                copy = pltpu.make_async_copy(block, target, own_sem.at[a])
                copy.start()
                copy.wait()

            @pl.when(near[s] != z)
            def _():
                move(block, target, across[a] + s, across_in[a] + z, {"prompt": near[s]}).start()

    second_hop(0)
    loads["d"].wait()
    first_hop(1)
    for step in range(1, 8):
        move(sums.at[t], sums.at[t], 0, at_sums + step, plane(1)).wait_recv()
    square = sums[0]
    for j in range(1, 8):
        square = square + sums[j]
    norms[z] = lax.rsqrt(square / width + EPSILON)
    at_norms = take(4)
    for step in range(1, 4):
        push(norms.at[z], norms.at[z], at_norms + step, at_norms + step, along(step))

    order = (0, 1, 3, 2)
    third = [[take(4) for _ in range(4)] for _ in range(2)]
    fourth = [[take(4) for _ in range(4)] for _ in range(2)]

    def third_hop(a):
        for step in order:
            p = lax.rem(z + step, 4)
            block = x.at[a, p, rows_of(chip), own_cols]
            if step:
                move(block, block, 0, across_in[a] + p, plane(1)).wait_recv()
            for s in (3, 1, 2):
                push(block, block, third[a][step] + s, third[a][step] + s, plane(s))
            push(block, block, third[a][step], third[a][step], {"tensor": pair})

    def fourth_hop(a):
        for step in order:
            p = lax.rem(z + step, 4)
            for s in (1, 2, 3):
                block = x.at[a, p, rows_of(near[s]), own_cols]
                move(block, block, 0, third[a][step] + s, plane(s)).wait_recv()
                push(block, block, fourth[a][step] + s, fourth[a][step] + s, {"tensor": pair})

    def last_hop(a):
        for step in order:
            p = lax.rem(z + step, 4)
            for s in range(4):
                block = x.at[a, p, rows_of(near[s]), pair_cols]
                number = fourth[a][step] + s if s else third[a][step]
                move(block, block, 0, number, {"tensor": pair}).wait_recv()

    third_hop(0)
    second_hop(1)
    fourth_hop(0)
    last_hop(0)
    third_hop(1)

    for step in range(1, 4):
        move(norms.at[z], norms.at[z], 0, at_norms + step, plane(1)).wait_recv()
        move(suffix, spots.at[z], 0, at_spots + step, plane(1)).wait_recv()

    loads["g"].wait()
    loads["s"].wait()
    gain_here = pl.ds(pl.multiple_of(z * rows_here, rows_here), rows_here)
    gain_row[...] = gain_all[gain_here].astype(jnp.float32).reshape(1, rows_here)

    @pl.loop(0, 4)
    def _(p):
        inverse = pick_column(norms[p][:1], seq)
        gains = gain_row[...]
        for j in range(0, rows_here, 512):
            block = x[0, p, :, j : j + 512].astype(jnp.float32)
            block = block * inverse * gains[:, j : j + 512]
            nb[p, :, j : j + 512] = block.astype(jnp.bfloat16)

    loads["k"].wait()
    loads["v"].wait()
    normed = nb[...].reshape(4 * seq, rows_here)
    pkv[...] = dot(normed, wkv[...], plain).reshape(4, seq, 2 * HD)

    is_end = (z == 0) | (z == 3)
    is_mid = (z == 1) | (z == 2)
    end_far, end_mid = 3 - z, 1 + z // 3
    mid_far, mid_near = 6 - 3 * z, 3 * z - 3

    def line_sends(block, into, relay_into, base):
        hand = move(block(end_far), relay_into, base, base + 4, {"prompt": end_mid})
        one = move(block(3 - end_mid), into.at[z], base + 1, base + z, {"prompt": 3 - end_mid})
        two = move(block(end_mid), into.at[z], base + 2, base + z, {"prompt": end_mid})
        over = move(block(3 - z), into.at[z], base, base + z, {"prompt": 3 - z})
        back = move(block(mid_near), into.at[z], base + 1, base + z, {"prompt": mid_near})
        return (hand, one, two), (over, back)

    def line_start(block, into, relay_into, base):
        ends, mids = line_sends(block, into, relay_into, base)

        @pl.when(is_end)
        def _():
            for copy in ends:
                copy.start()

        @pl.when(is_mid)
        def _():
            for copy in mids:
                copy.start()

    def line_relay(block, into, relay_into, base, add, out_block):
        @pl.when(is_mid)
        def _():
            move(relay_into, relay_into, 0, base + 4, {"prompt": mid_far}).wait_recv()
            add()
            move(out_block, into.at[z], base + 2, base + z, {"prompt": mid_far}).start()

    def line_arrive(into, base):
        @pl.when(is_end)
        def _():
            for source in (end_mid, 3 - end_mid):
                move(into.at[z], into.at[z], 0, base + source, plane(1)).wait_recv()

        @pl.when(is_mid)
        def _():
            for source in (0, 3, 3 - z):
                move(into.at[z], into.at[z], 0, base + source, plane(1)).wait_recv()

    def line_sent(block, into, relay_into, base, out_block):
        ends, mids = line_sends(block, into, relay_into, base)

        @pl.when(is_end)
        def _():
            for copy in ends:
                copy.wait_send()

        @pl.when(is_mid)
        def _():
            for copy in mids:
                copy.wait_send()
            move(out_block, into.at[z], base + 2, base + z, {"prompt": mid_far}).wait_send()

    @pl.when(is_end)
    def _():
        rkv[end_far] = jnp.zeros(rkv.shape[1:], rkv.dtype)
        for i in range(2):
            arrived[i, end_far] = jnp.zeros(arrived.shape[2:], arrived.dtype)
            powers_in[i, end_far] = jnp.zeros(powers_in.shape[2:], powers_in.dtype)

    line_kv = take(5)
    line = [take(5) for _ in range(2)]
    line_powers = [take(5) for _ in range(2)]
    kv_args = (lambda d: pkv.at[d], rkv, relay_kv)
    line_start(*kv_args, line_kv)
    for c in range(chunks):
        load_table(c).start()

    def code(i):
        for step in (3, 2, 1):
            d = lax.rem(z + step, 4)

            def write(h, tile):
                if h == heads:
                    powers[i, d] = tile
                else:
                    coded[i, d, :, h * HD : (h + 1) * HD] = tile

            code_block(lambda h: pp[i, d, :, h * HD : (h + 1) * HD], write, heads, seq)

    def line_of(i):
        return (lambda d: coded.at[i, d], arrived.at[i], relay.at[i])

    def powers_of(i):
        return (lambda d: powers.at[i, d], powers_in.at[i], powers_relay.at[i])

    def add_coded(i):
        def add():
            factors = scale_of(powers_relay[i], seq)

            def read(h):
                got = relay[i, :, h * HD : (h + 1) * HD].astype(jnp.int32).astype(jnp.float32)
                return got * factors[:, h : h + 1] + pp[i, mid_far, :, h * HD : (h + 1) * HD]

            def write(h, tile):
                if h == heads:
                    powers_total[i] = tile
                else:
                    total[i, :, h * HD : (h + 1) * HD] = tile

            code_block(read, write, heads, seq)

        return add

    def relay_coded(i):
        @pl.when(is_mid)
        def _():
            for buffer, base in ((relay.at[i], line[i]), (powers_relay.at[i], line_powers[i])):
                move(buffer, buffer, 0, base + 4, {"prompt": mid_far}).wait_recv()
            add_coded(i)()
            for block, into, base in (
                (powers_total.at[i], powers_in.at[i], line_powers[i]),
                (total.at[i], arrived.at[i], line[i]),
            ):
                move(block, into.at[z], base + 2, base + z, {"prompt": mid_far}).start()

    loads["q"].wait()

    @pl.loop(0, head_cols // 256)
    def _(j):
        span = pl.ds(pl.multiple_of(j * 256, 256), 256)
        part = dot(nb[...].reshape(4 * seq, rows_here), wq[:, span], plain)
        pp[0, :, :, span] = part.reshape(4, seq, 256)

    code(0)
    line_start(*powers_of(0), line_powers[0])
    line_start(*line_of(0), line[0])

    def add_kv():
        relay_kv[...] = relay_kv[...] + pkv[mid_far]

    line_relay(*kv_args, line_kv, add_kv, relay_kv)

    fourth_hop(1)
    last_hop(1)
    loads["o"].wait()

    @pl.loop(0, head_cols // 256)
    def _(j):
        span = pl.ds(pl.multiple_of(j * 256, 256), 256)
        part = dot(x[1].reshape(4 * seq, rows_here), wo[span, :], crossed)
        pp[1, :, :, span] = part.reshape(4, seq, 256)

    code(1)
    line_start(*powers_of(1), line_powers[1])
    line_start(*line_of(1), line[1])

    line_arrive(rkv, line_kv)
    own = pkv[z]
    for step in range(1, 4):
        own = own + rkv[lax.rem(z + step, 4)]
    kvg[t] = own.astype(jnp.bfloat16)
    at_kv = take(8)
    for step in range(1, 8):
        push(kvg.at[t], kvg.at[t], at_kv + step, at_kv + step, {"tensor": lax.rem(t + step, 8)})
    relay_coded(0)
    relay_coded(1)

    over = lax.broadcasted_iota(jnp.int32, (rows, count), 1)
    place = jnp.zeros((rows, 1), jnp.float32)
    row_at = lax.broadcasted_iota(jnp.int32, (rows, 1), 0)
    spot_of = row_at // 4
    prompt_of = row_at - 4 * spot_of
    for p in range(4):
        mark = (spot_of == over) & (prompt_of == p)
        found = jnp.where(mark, spots[p].astype(jnp.float32), 0.0)
        place = place + jnp.sum(found, axis=1, keepdims=True)
    place = place + seq * prompt_of.astype(jnp.float32)
    marks = lax.broadcasted_iota(jnp.int32, (rows, 4 * seq), 1).astype(jnp.float32)
    chosen = (marks == place).astype(jnp.bfloat16)
    norm_rows = jnp.zeros((rows, 1), jnp.float32)
    inside = lax.broadcasted_iota(jnp.int32, (rows, 128), 1).astype(jnp.float32)
    for p in range(4):
        hit = (inside + p * seq == place) & (inside < seq)
        norm_rows = norm_rows + jnp.sum(jnp.where(hit, norms[p][:1], 0.0), axis=1, keepdims=True)
    for j in range(0, rows_here, 512):
        block = x[0, :, :, j : j + 512].reshape(4 * seq, 512)
        scaled[:, j : j + 512] = dot(chosen, block, plain) * norm_rows

    def finish(i):
        line_arrive(powers_in.at[i], line_powers[i])
        line_arrive(arrived.at[i], line[i])
        factors = [scale_of(powers_in[i, lax.rem(z + s, 4)], seq) for s in (1, 2, 3)]
        for h in range(heads):
            span = slice(h * HD, (h + 1) * HD)
            value = pp[i, z, :, span]
            for s in (1, 2, 3):
                got = arrived[i, lax.rem(z + s, 4), :, span].astype(jnp.int32)
                value = value + got.astype(jnp.float32) * factors[s - 1][:, h : h + 1]
            whole[i, :, span] = value.astype(jnp.bfloat16)

    finish(0)
    for step in range(1, 8):
        move(kvg.at[t], kvg.at[t], 0, at_kv + step, plane(1)).wait_recv()
    finish(1)

    own_spots = jnp.where(
        lax.broadcasted_iota(jnp.int32, (PAD, count), 0)
        == lax.broadcasted_iota(jnp.int32, (PAD, count), 1),
        spots[z].astype(jnp.float32),
        0.0,
    )
    own_spots = jnp.sum(own_spots, axis=1, keepdims=True)
    real = lax.broadcasted_iota(jnp.int32, (PAD, 1), 0) < count
    own_spots = jnp.where(real, own_spots, -1.0)
    steps_iota = lax.broadcasted_iota(jnp.int32, (PAD, seq), 1).astype(jnp.float32)
    chooser = (steps_iota == own_spots).astype(jnp.bfloat16)
    causal = lax.broadcasted_iota(jnp.int32, (seq, seq), 1) <= lax.broadcasted_iota(
        jnp.int32, (seq, seq), 0
    )
    at_slots, slots_from = take(8), take(8)
    at_grads = take(12)

    def head_grads(group):
        span = {h: slice(h * HD, (h + 1) * HD) for h in group}
        queries = {h: whole[0, :, span[h]] for h in group}
        contexts = {h: whole[1, :, span[h]] for h in group}
        keys = {h: kvg[h, :, :HD] for h in group}
        values = {h: kvg[h, :, HD:] for h in group}
        logits = {h: dot(queries[h], keys[h], crossed) * scale for h in group}
        prob_grad = {h: dot(contexts[h], values[h], crossed) for h in group}
        largest = {
            h: jnp.max(jnp.where(causal, logits[h], -1e30), axis=-1, keepdims=True) for h in group
        }
        raised = {h: jnp.where(causal, jnp.exp(logits[h] - largest[h]), 0.0) for h in group}
        whole_sum = {h: jnp.sum(raised[h], axis=-1, keepdims=True) for h in group}
        probs = {h: raised[h] / whole_sum[h] for h in group}
        probs_low = {h: probs[h].astype(jnp.bfloat16) for h in group}
        less = {h: jnp.sum(prob_grad[h] * probs[h], axis=-1, keepdims=True) for h in group}
        logit_grad = {
            h: (probs[h] * (prob_grad[h] - less[h]) * scale).astype(jnp.bfloat16) for h in group
        }
        logit_rows = {h: dot(chooser, logit_grad[h], plain).astype(jnp.bfloat16) for h in group}
        logit_cols = {h: dot(chooser, logit_grad[h], crossed).astype(jnp.bfloat16) for h in group}
        prob_cols = {h: dot(chooser, probs_low[h], crossed).astype(jnp.bfloat16) for h in group}
        for h in group:
            grads[z, :, span[h]] = dot(logit_rows[h], keys[h], plain).astype(jnp.bfloat16)
            slots[h, :24] = dot(logit_cols[h], queries[h], plain)[:24]
            slots[h, 24:] = dot(prob_cols[h], contexts[h], plain)[:24]

    def send_slots(h):
        return move(slots.at[h], slots_in.at[t], at_slots + h, slots_from + t, {"tensor": h})

    halves = 2
    head_parts = []
    for half in range(halves):
        group = range(half * heads // halves, (half + 1) * heads // halves)
        head_grads(group)
        for h in group:

            @pl.when(t != h)
            def _():
                send_slots(h).start()

        part = grads.at[z, :, group.start * HD : group.stop * HD]
        head_parts.append(part)
        for step in (2, 1, 3):
            number = at_grads + 4 * half + step
            push(part, part, number, number, along(step))
    slots_in[t] = slots[t]
    for step in range(1, 8):
        source = lax.rem(t + step, 8)
        move(slots_in.at[t], slots_in.at[t], 0, slots_from + source, plane(1)).wait_recv()
    summed = slots_in[0]
    for j in range(1, 8):
        summed = summed + slots_in[j]
    filler = jnp.zeros((PAD - 24, HD), jnp.float32)
    key_rows = jnp.concatenate([summed[:24], filler], axis=0)
    value_rows = jnp.concatenate([summed[24:], filler], axis=0)
    grads[z, :, head_cols : head_cols + HD] = key_rows.astype(jnp.bfloat16)
    grads[z, :, head_cols + HD :] = value_rows.astype(jnp.bfloat16)
    tail_part = grads.at[z, :, head_cols:]
    for step in (2, 1, 3):
        push(tail_part, tail_part, at_grads + 8 + step, at_grads + 8 + step, along(step))
    for half in range(halves):
        for step in range(1, 4):
            part = head_parts[half]
            move(part, part, 0, at_grads + 4 * half + step, plane(1)).wait_recv()

    packed_at = lax.broadcasted_iota(jnp.int32, (rows, 4 * PAD), 1)
    packer = (packed_at == PAD * prompt_of + spot_of).astype(jnp.bfloat16)
    packed = dot(packer, grads[:, :, :head_cols].reshape(4 * PAD, head_cols), plain)
    packed = packed.astype(jnp.bfloat16)
    farthest = (3, 1, 2, 0)

    def owned(half, s):
        owner = 2 * near[s] + ((1 - core) if half == 0 else core)
        return pl.ds(pl.multiple_of(owner * slice_width, slice_width), slice_width)

    for half in range(2):
        for s in farthest:
            weighted[half, s] = dot(packed, wq[owned(half, s), :], crossed)
    for step in range(1, 4):
        move(tail_part, tail_part, 0, at_grads + 8 + step, plane(1)).wait_recv()
    packed = dot(packer, grads[:, :, head_cols:].reshape(4 * PAD, 2 * HD), plain)
    packed = packed.astype(jnp.bfloat16)
    inner = jnp.zeros((rows, 128), jnp.float32)
    at_pair, at_shares = take(4), take(4)
    for half in range(2):
        for s in farthest:
            span = owned(half, s)
            part = weighted[half, s] + dot(packed, wkv[span, :], crossed)
            part = part * gain_row[:, span]
            product = part * scaled[:, span]
            for j in range(0, slice_width, 128):
                inner = inner + product[:, j : j + 128]
            weighted[half, s] = part
            if half == 0:
                push(weighted.at[0, s], pair_in.at[s], at_pair + s, at_pair + s, {"tensor": pair})
    for s in farthest:
        move(pair_in.at[s], pair_in.at[s], 0, at_pair + s, {"tensor": pair}).wait_recv()
        weighted[1, s] = weighted[1, s] + pair_in[s]
        if s:
            push(weighted.at[1, s], shares.at[s - 1], at_shares + s, at_shares + s, plane(s))
    inner = jnp.sum(inner, axis=1, keepdims=True)
    inner_in[t] = jnp.broadcast_to(lay_row(inner, 128), (8, 128))
    at_inner = take(8)
    for step in range(1, 8):
        push(
            inner_in.at[t],
            inner_in.at[t],
            at_inner + step,
            at_inner + step,
            {"tensor": lax.rem(t + step, 8)},
        )
    for step in range(1, 8):
        move(inner_in.at[t], inner_in.at[t], 0, at_inner + step, plane(1)).wait_recv()
    inner = inner_in[0]
    for j in range(1, 8):
        inner = inner + inner_in[j]
    inner_z[z] = inner
    at_inner_z = take(4)
    for step in range(1, 4):
        push(inner_z.at[z], inner_z.at[z], at_inner_z + step, at_inner_z + step, along(step))
    for s in (1, 2, 3):
        move(shares.at[s - 1], shares.at[s - 1], 0, at_shares + s, plane(1)).wait_recv()
    own = weighted[1, 0] + shares[0] + shares[1] + shares[2]
    for step in range(1, 4):
        move(inner_z.at[z], inner_z.at[z], 0, at_inner_z + step, plane(1)).wait_recv()
    inner = (inner_z[0] + inner_z[1] + inner_z[2] + inner_z[3])[:1]
    inner = pick_column(inner, rows) / width

    here = pl.ds(pl.multiple_of(t * slice_width, slice_width), slice_width)
    suffix_grads[z, :, here] = (norm_rows * (own - scaled[:, here] * inner)).astype(jnp.bfloat16)

    def grad_of(p, chip_index, core_index):
        first = (2 * chip_index + core_index) * slice_width
        return suffix_grads.at[p, :, pl.ds(pl.multiple_of(first, slice_width), slice_width)]

    at_z = take(4)
    spread = [take(4) for _ in range(4)]
    doubled = [take(4) for _ in range(4)]
    mine_now = grad_of(z, chip, core)
    for step in (2, 1, 3):
        push(mine_now, mine_now, at_z + step, at_z + step, along(step))

    def to_plane(step):
        block = grad_of(lax.rem(z - step + 4, 4), chip, core)
        if step:
            move(block, block, 0, at_z + step, plane(1)).wait_recv()
        for s in (3, 1, 2):
            push(block, block, spread[step] + s, spread[step] + s, plane(s))
        push(block, block, spread[step], spread[step], {"tensor": pair})

    def to_pair(step):
        p = lax.rem(z - step + 4, 4)
        for s in (1, 2, 3):
            block = grad_of(p, near[s], core)
            move(block, block, 0, spread[step] + s, plane(s)).wait_recv()
            push(block, block, doubled[step] + s, doubled[step] + s, {"tensor": pair})

    def from_pair(step):
        p = lax.rem(z - step + 4, 4)
        for s in range(4):
            block = grad_of(p, near[s], 1 - core)
            number = doubled[step] + s if s else spread[step]
            move(block, block, 0, number, {"tensor": pair}).wait_recv()

    def leave(half):
        wide = vocab.shape[0] // 2
        span = pl.ds(half * wide, wide)
        return pltpu.make_async_copy(
            result.at[:, :, span], out.at[:, :, span], own_sem.at[3 + half]
        )

    def multiply(step, half):
        p = lax.rem(z - step + 4, 4)
        features = pl.ds(pl.multiple_of(p * rows_here, rows_here), rows_here)
        wide = vocab.shape[0] // 2
        span = pl.ds(half * wide, wide)
        part = dot(suffix_grads[p], table[span, features], crossed)
        if step != order[0]:
            part = part + partial[:, span]
        if step != order[-1]:
            partial[:, span] = part
            return
        part = jnp.where(barred[:, span] == 1, 0.0, -part)
        for n in range(count):
            result[n, :, span] = part[4 * n : 4 * n + 4]
        leave(half).start()

    to_plane(0)
    to_plane(1)
    to_pair(0)
    for c in range(chunks):
        load_table(c).wait()
    loads["b"].wait()
    from_pair(0)
    multiply(0, 0)
    to_plane(3)
    to_plane(2)
    to_pair(1)
    multiply(0, 1)
    from_pair(1)
    multiply(1, 0)
    to_pair(3)
    multiply(1, 1)
    from_pair(3)
    multiply(3, 0)
    to_pair(2)
    multiply(3, 1)
    from_pair(2)
    multiply(2, 0)
    multiply(2, 1)
    leave(0).wait()
    leave(1).wait()

    for copy in sent:
        copy.wait_send()
    for h in range(heads):

        @pl.when(t != h)
        def _():
            send_slots(h).wait_send()

    for a in range(2):
        for s in range(4):

            @pl.when(near[s] != z)
            def _():
                block = x.at[a, z, rows_of(chip), own_cols]
                move(block, block, across[a] + s, 0, {"prompt": near[s]}).wait_send()

    line_sent(*kv_args, line_kv, relay_kv)
    for i in range(2):
        line_sent(*powers_of(i), line_powers[i], powers_total.at[i])
        line_sent(*line_of(i), line[i], total.at[i])


def fused(
    embeds,
    norm_gain,
    query_weight,
    key_weight,
    value_weight,
    out_weight,
    out_grad,
    suffix_pos,
    vocab_table,
    banned,
):
    seq, cols = embeds.shape[1:]
    rows_here, head_cols = query_weight.shape
    count = suffix_pos.shape[1]
    vocab_here, width = vocab_table.shape
    heads = head_cols // HD
    rows = 4 * count
    slice_width = rows_here // 8
    low, full, short = jnp.bfloat16, jnp.float32, jnp.int16
    coded = head_cols
    local = pl.BlockSpec(memory_space=pltpu.VMEM)
    apart = pl.BlockSpec(memory_space=pl.ANY)
    scratch = [
        ((rows_here, head_cols), low),
        ((rows_here, 2 * HD), low),
        ((head_cols, rows_here), low),
        (vocab_table.shape, low),
        ((2, seq, cols), low),
        ((2, 3, seq // 4, cols), low),
        ((2, 4, seq, rows_here), low),
        ((8, 8, 128), full),
        ((4, 8, 128), full),
        ((4, 1, count), jnp.int32),
        ((4, seq, rows_here), low),
        ((4, seq, 2 * HD), full),
        ((4, seq, 2 * HD), full),
        ((seq, 2 * HD), full),
        ((2, 4, seq, head_cols), full),
        ((2, 4, seq, coded), short),
        ((2, 4, seq, coded), short),
        ((2, seq, coded), short),
        ((2, seq, coded), short),
        ((2, 4, 16, HD), short),
        ((2, 4, 16, HD), short),
        ((2, 16, HD), short),
        ((2, 16, HD), short),
        ((8, seq, 2 * HD), low),
        ((2, seq, head_cols), low),
        ((8, 48, HD), full),
        ((8, 48, HD), full),
        ((4, PAD, head_cols + 2 * HD), low),
        ((rows, rows_here), full),
        ((2, 4, rows, slice_width), full),
        ((4, rows, slice_width), full),
        ((3, rows, slice_width), full),
        ((8, 8, 128), full),
        ((4, 8, 128), full),
        ((4, rows, rows_here), low),
        ((rows, vocab_here), full),
        ((1, rows_here), full),
        ((width,), low),
        ((1, vocab_here), jnp.int32),
        ((count, 4, vocab_here), full),
    ]
    scores = pl.pallas_call(
        fused_kernel,
        out_shape=jax.ShapeDtypeStruct((count, 4, vocab_here), full),
        in_specs=[apart] * 10,
        out_specs=apart,
        scratch_shapes=[pltpu.VMEM(shape, dtype) for shape, dtype in scratch]
        + [
            pltpu.SemaphoreType.DMA((SEMS,)),
            pltpu.SemaphoreType.DMA((SEMS,)),
            pltpu.SemaphoreType.DMA((8 + vocab_here // CHUNK,)),
            pltpu.SemaphoreType.DMA((5,)),
        ],
        compiler_params=pltpu.CompilerParams(
            collective_id=11, has_side_effects=True, vmem_limit_bytes=60 << 20
        ),
    )(
        embeds,
        out_grad,
        norm_gain,
        query_weight,
        key_weight,
        value_weight,
        out_weight,
        suffix_pos,
        vocab_table,
        banned.reshape(1, -1),
    )
    return scores.transpose(1, 0, 2)


def fits(mesh_sizes, arrays):
    embeds, query_weight, key_weight, suffix_pos, vocab_table = arrays
    return (
        mesh_sizes == (4, 8)
        and embeds.shape[1] == 64
        and query_weight.shape[1] == 8 * HD
        and key_weight.shape[1] == HD
        and query_weight.shape[0] == 2 * embeds.shape[2]
        and query_weight.shape[0] % 2048 == 0
        and suffix_pos.shape[1] == 20
        and vocab_table.shape[0] % CHUNK == 0
    )


def part_of(*args):
    sizes = (lax.axis_size("prompt"), lax.axis_size("tensor"))
    if fits(sizes, (args[0], args[2], args[3], args[7], args[8])):
        return fused(*args)
    return on_device(*args)


def solution(mesh):
    return jax.shard_map(
        part_of,
        mesh=mesh,
        in_specs=(
            P("prompt", None, "tensor"),
            P(),
            P("prompt", "tensor"),
            P("prompt", "tensor"),
            P("prompt", "tensor"),
            P("tensor", "prompt"),
            P("prompt", None, "tensor"),
            P("prompt", None),
            P(("prompt", "tensor"), None),
            P(("prompt", "tensor")),
        ),
        out_specs=P(None, None, ("prompt", "tensor")),
        check_vma=False,
    )
```
